32 devices in a mesh: groups: 2 (over y), strip: 4 (over z), angle: 2 (over x), depth: 2 (over core).
Axes of the slice: x: 2, y: 2, z: 4, core: 2. Of those that a mesh axis runs over, the one named last changes fastest.
Arguments:
- crystal: bfloat16 [16, 2, 512, 384], P(('groups', 'depth'), None, 'strip'), parts along dimension 0, may hold values from -4 to 4
- probe: bfloat16 [2, 256, 256], replicated, may hold values from -5 to 5
- amplitude: bfloat16 [4, 2048, 256], P('angle', ('groups', 'strip', 'depth')), parts along dimension 1, may hold values from 0.5 to 8
- shear: int32 [16, 8], P(('groups', 'angle'), 'depth'), parts along dimension 0, may hold values from 0 to 15
- scan_x: int32 [4, 4, 2], P(('groups', 'angle')), parts along dimension 0, may hold values from 0 to 112
- scan_y: int32 [4, 4, 2], P(('groups', 'angle')), parts along dimension 0, may hold values from 0 to 128
- slot_angle: int32 [4, 4, 2], P(('groups', 'angle')), parts along dimension 0, may hold values from 0 to 3
- owner_slot: int32 [4, 4, 2], P(('groups', 'angle')), parts along dimension 0, may hold values from 0 to 1, each once within a row
- counts: int32 [4, 4], P(('groups', 'angle')), parts along dimension 0, may hold values from 1 to 2
Outputs:
- gradient: float32 [16, 2, 512, 384], P(('groups', 'depth'), None, ('strip', 'angle')), parts along dimension 0
The draws below stay inside these ranges and needn't reach their ends.
There are 2 independent parts, one for each index of `groups`. The reference program is written for one: setup_inputs(seed, part) draws one part's arguments, and reference() takes and returns one part's arrays. A program takes and returns all parts, laid end to end along the dimension named above; an argument that names none is the same for every part. Nothing has to cross between parts.
Inputs may be any that keep to these rules, and one draw needn't show every extreme that they name: `owner_slot`: for each angle group and home strip, the 2 entries are a permutation of 0 to 1.
All inputs are finite; a program needn't handle non-finite values.
Results may differ from the reference program's by a relative error of at most 0.02.
Values may be sent and summed in bfloat16 or wider, within the bound.
A program may use at most 64 MiB of HBM per device.

```python
import math
import jax
import jax.numpy as jnp
from jax import lax

FRAME = 256
WX = 128
SHEAR = 16
NY = 384
NZ_DEV = 4
ANG_DEV = 4
BAND = 144
M = 2
NX = 512
NZ = 8
ANGLES = 8
ANGLE_GROUPS = 2
SLOTS = 4
N_STRIP = 4
N_ANGLE = 2
N_DEPTH = 2


def set_ends(entries, rng, low, largest):
    longest = entries.shape.index(max(entries.shape))
    spots = []
    for shift in (0, 1):
        where = [jax.random.randint(jax.random.fold_in(rng, axis), (), 0, length) for axis, length in enumerate(entries.shape)]
        where[longest] = (where[longest] + shift) % entries.shape[longest]
        spots.append(tuple(where))
    return entries.at[spots[0]].set(low).at[spots[1]].set(largest)


def block_levels(key, dims, shards, smallest, high):
    factor_of = 1.0
    for dim, parts in shards:
        steps = jax.random.uniform(jax.random.fold_in(jax.random.fold_in(key, 6), dim), (parts,), jnp.float32, smallest / len(shards), high / len(shards))
        factor_of = factor_of * jnp.repeat(jnp.exp(steps), dims[dim] // parts).reshape((-1,) + (1,) * (len(dims) - 1 - dim))
    return factor_of


def centred(rng, extent, spread, bound, split=(), held_as=jnp.bfloat16):
    array = spread * jax.random.normal(rng, extent, jnp.float32)
    if split:
        array = array * block_levels(rng, extent, split, -0.22, 0.18)
    return jnp.clip(array, -bound, bound).astype(held_as)


def setup_inputs(seed: int = 0, part: int = 0) -> dict:
    key_of = jax.random.split(jax.random.key(seed), 10)
    part_keys = jax.random.split(jax.random.fold_in(key_of[9], part), 10)
    return {
        "crystal": centred(part_keys[0], (NZ, 2, NX, NY), 0.5, 4.0, ((0, 2), (2, 4))),
        "probe": centred(key_of[1], (2, FRAME, FRAME), 1.0, 5.0),
        "amplitude": jnp.clip(jnp.exp(math.log(8.0) - 2.7725887 * jax.random.uniform(part_keys[2], (SLOTS, N_STRIP * FRAME, FRAME), jnp.float32) ** block_levels(part_keys[2], (SLOTS, N_STRIP * FRAME, FRAME), ((0, 2), (1, 8)), -0.2, 0.2)), 0.5, 8.0).astype(jnp.bfloat16),
        "shear": set_ends(jax.random.randint(part_keys[3], (ANGLES, NZ), 0, SHEAR), jax.random.fold_in(part_keys[3], 1), 0, SHEAR - 1).astype(jnp.int32),
        "scan_x": set_ends(jax.random.randint(part_keys[4], (ANGLE_GROUPS, N_STRIP, M), 0, min(WX, 3 * WX - FRAME - SHEAR + 1)), jax.random.fold_in(part_keys[4], 1), 0, (min(WX, 3 * WX - FRAME - SHEAR + 1)) - 1).astype(jnp.int32),
        "scan_y": set_ends(jax.random.randint(part_keys[5], (ANGLE_GROUPS, N_STRIP, M), 0, NY - FRAME + 1), jax.random.fold_in(part_keys[5], 1), 0, NY - FRAME).astype(jnp.int32),
        "slot_angle": set_ends(jax.random.randint(part_keys[6], (ANGLE_GROUPS, N_STRIP, M), 0, ANG_DEV), jax.random.fold_in(part_keys[6], 1), 0, ANG_DEV - 1).astype(jnp.int32),
        "owner_slot": jax.vmap(lambda own: jax.random.permutation(own, M))(jax.random.split(part_keys[7], ANGLE_GROUPS * N_STRIP)).reshape((ANGLE_GROUPS, N_STRIP, M)).astype(jnp.int32),
        "counts": set_ends(jax.random.randint(part_keys[8], (ANGLE_GROUPS, N_STRIP), M // 2, M + 1), jax.random.fold_in(part_keys[8], 1), M // 2, M).astype(jnp.int32),
    }


def spot(*values):
    return tuple((jnp.asarray(value, jnp.int32) for value in values))

def dft_parts():
    index_row = jnp.arange(FRAME, dtype=jnp.int32)
    wound = index_row[:, None] * index_row[None, :] % FRAME
    phase = wound.astype(jnp.float32) * (2.0 * math.pi / FRAME)
    scaling = 1.0 / math.sqrt(FRAME)
    return ((jnp.cos(phase) * scaling).astype(jnp.bfloat16), (-jnp.sin(phase) * scaling).astype(jnp.bfloat16))

def stamp(value):
    return lax.optimization_barrier(value.astype(jnp.bfloat16)).astype(jnp.float32)

def complex_times(left, right, sign):
    out_re = left[0] * right[0] - sign * left[1] * right[1]
    out_im = left[0] * right[1] + sign * left[1] * right[0]
    return jnp.stack([out_re, out_im], axis=0)

def right_product(block, table_re, table_im, sign):
    part_re = block[0]
    part_im = block[1]
    first = jnp.dot(part_re, table_re, preferred_element_type=jnp.float32)
    second = jnp.dot(part_im, table_im, preferred_element_type=jnp.float32)
    third = jnp.dot(part_re, table_im, preferred_element_type=jnp.float32)
    fourth = jnp.dot(part_im, table_re, preferred_element_type=jnp.float32)
    return jnp.stack([first - sign * second, sign * third + fourth], axis=0)

def row_product(rows_re, rows_im, block, sign):
    part_re = block[0]
    part_im = block[1]
    first = jnp.dot(rows_re, part_re, preferred_element_type=jnp.float32)
    second = jnp.dot(rows_im, part_im, preferred_element_type=jnp.float32)
    third = jnp.dot(rows_im, part_re, preferred_element_type=jnp.float32)
    fourth = jnp.dot(rows_re, part_im, preferred_element_type=jnp.float32)
    return jnp.stack([first - sign * second, sign * third + fourth], axis=0)

def reference(crystal, probe, amplitude, shear, scan_x, scan_y, slot_angle, owner_slot, counts):
    table_re, table_im = dft_parts()
    pad_re = jnp.pad(table_re, ((BAND, BAND), (0, 0)))
    pad_im = jnp.pad(table_im, ((BAND, BAND), (0, 0)))
    probe_pad = jnp.pad(probe, ((0, 0), (BAND, BAND), (0, 0)))
    crystal_pad = jnp.pad(crystal, ((0, 0), (0, 0), (SHEAR, SHEAR), (0, 0)))
    depth_rows = FRAME // N_DEPTH
    quarter = N_STRIP // 4
    band_index = jnp.arange(BAND, dtype=jnp.int32)

    def group_step(summed, group):
        shear_rows = lax.dynamic_slice_in_dim(shear, jnp.asarray(group * ANG_DEV, jnp.int32), ANG_DEV, 0)
        offsets = scan_x[group]
        columns = scan_y[group]
        angles = slot_angle[group]
        owners = owner_slot[group]
        limits = counts[group]

        def pattern_step(gradient_pad, item):
            home = item // M
            slot_id = item % M
            living = (slot_id < limits[home]).astype(jnp.float32)
            offset = offsets[home, slot_id]
            column = columns[home, slot_id]
            quota = owners[home, slot_id]
            owner = (home + 4 * (quota % quarter) + 1) % N_STRIP
            shifts = shear_rows[angles[home, slot_id]]
            starts = [jnp.asarray(band_k * WX - offset - SHEAR + BAND, jnp.int32) for band_k in range(3)]
            rows_re = [lax.dynamic_slice_in_dim(pad_re, first_row, BAND, 0) for first_row in starts]
            rows_im = [lax.dynamic_slice_in_dim(pad_im, first_row, BAND, 0) for first_row in starts]
            probes = [lax.dynamic_slice_in_dim(probe_pad, first_row, BAND, 1).astype(jnp.float32) for first_row in starts]
            spectrum = jnp.zeros((2, FRAME, FRAME), jnp.float32)
            for slab in range(N_DEPTH):
                slab_sum = jnp.zeros((2, FRAME, FRAME), jnp.float32)
                for band_k in range(3):
                    accum = jnp.zeros((2, BAND, FRAME), jnp.float32)
                    for layer_index in range(slab * NZ_DEV, (slab + 1) * NZ_DEV):
                        lift = shifts[layer_index]
                        window = lax.dynamic_slice(crystal_pad[layer_index], spot(0, (home + band_k) * WX + lift, column), (2, BAND, FRAME)).astype(jnp.float32)
                        local_row = band_index + lift - SHEAR
                        inside = ((local_row >= 0) & (local_row < WX)).astype(jnp.float32)
                        accum = accum + window * inside[None, :, None]
                    band = accum.astype(jnp.bfloat16)
                    exit_band = complex_times(probes[band_k], band.astype(jnp.float32), 1.0).astype(jnp.bfloat16)
                    section = right_product(exit_band, table_re, table_im, 1.0).astype(jnp.bfloat16)
                    slab_sum = slab_sum + row_product(rows_re[band_k].T, rows_im[band_k].T, section, 1.0)
                spectrum = spectrum + stamp(slab_sum)
            measured = lax.dynamic_slice(amplitude, spot(group * M + quota, owner * FRAME, 0), (1, FRAME, FRAME))[0].astype(jnp.float32)
            magnitude = jnp.sqrt(spectrum[0] * spectrum[0] + spectrum[1] * spectrum[1])
            factor = (1.0 - measured / jnp.maximum(magnitude, 1.0)) * living
            residual = (spectrum * factor[None]).astype(jnp.bfloat16)
            inverse_rows = right_product(residual, table_re, table_im, -1.0).astype(jnp.bfloat16)
            for band_k in range(3):
                back_total = jnp.zeros((2, BAND, FRAME), jnp.float32)
                for block_index in range(N_DEPTH):
                    row_low = block_index * depth_rows
                    wave = row_product(rows_re[band_k][:, row_low:row_low + depth_rows], rows_im[band_k][:, row_low:row_low + depth_rows], inverse_rows[:, row_low:row_low + depth_rows], -1.0)
                    back_total = back_total + stamp(complex_times(probes[band_k], wave, -1.0))
                back_band = stamp(back_total)
                for layer_index in range(NZ):
                    lift = shifts[layer_index]
                    local_row = band_index + lift - SHEAR
                    inside = ((local_row >= 0) & (local_row < WX)).astype(jnp.float32)
                    position = spot(layer_index, 0, (home + band_k) * WX + lift, column)
                    current = lax.dynamic_slice(gradient_pad, position, (1, 2, BAND, FRAME))
                    gradient_pad = lax.dynamic_update_slice(gradient_pad, current + (back_band * inside[None, :, None])[None], position)
            return (gradient_pad, None)
        items = jnp.arange((N_STRIP - 2) * M, dtype=jnp.int32)
        start_pad = jnp.zeros((NZ, 2, NX + 2 * SHEAR, NY), jnp.float32)
        gradient_pad, unused = lax.scan(pattern_step, start_pad, items)
        cropped = gradient_pad[:, :, SHEAR:SHEAR + NX]
        return (summed + stamp(cropped), None)
    summed, unused = lax.scan(group_step, jnp.zeros((NZ, 2, NX, NY), jnp.float32), jnp.arange(N_ANGLE, dtype=jnp.int32))
    return summed * (1.0 / ANGLES)
```

```python
import functools

import jax
import jax.numpy as jnp
import numpy as np
from jax import lax
from jax.experimental import pallas as pl
from jax.experimental.pallas import tpu as pltpu
from jax.sharding import PartitionSpec as P

FRAME = 256
WX = 128
SHEAR = 16
REACHES = 3
ROWS = (WX, FRAME, FRAME - WX)
BASES = (0, 0, WX)
VMEM_LIMIT = 44 * 2**20
MESH = pl.DeviceIdType.MESH


def dft_tables():
    index_row = np.arange(FRAME)
    phase = (index_row[:, None] * index_row[None, :] % FRAME) * (2.0 * np.pi / FRAME)
    real = np.cos(phase) / np.sqrt(FRAME)
    imag = -np.sin(phase) / np.sqrt(FRAME)
    table = np.block([[real, imag], [-imag, real]]).astype(np.float32)
    return jnp.asarray(table, jnp.bfloat16), jnp.asarray(table.T, jnp.bfloat16)


def dot(left, right):
    return jnp.dot(left, right, preferred_element_type=jnp.float32)


def differences(rows, columns):
    shape = (rows, columns)
    return lax.broadcasted_iota(jnp.int32, shape, 1) - lax.broadcasted_iota(jnp.int32, shape, 0)


def one_hot(mask):
    return jnp.where(mask, 1.0, 0.0).astype(jnp.bfloat16)


class Meta:
    def __init__(self, lifts, owner_slot, slots, lead):
        self.lifts, self.owner_slot = lifts, owner_slot
        self.slots, self.lead = slots, lead

    def shear(self, angle, z):
        return self.lifts[self.lead + (angle, z)]

    def pick(self, ref, home, quota):
        value = jnp.int32(0)
        for m in range(self.slots):
            at = self.lead + (0, m, home)
            value = value + jnp.where(self.owner_slot[at] == quota, ref[at], 0)
        return value

    def slot(self, home, quota):
        value = jnp.int32(0)
        for m in range(self.slots):
            at = self.lead + (0, m, home)
            value = value + jnp.where(self.owner_slot[at] == quota, m, 0)
        return value


def kernel(
    sizes,
    scaling,
    crystal,
    probe_in,
    amplitude,
    table_in,
    table_t_in,
    shear_in,
    scan_x_in,
    scan_y_in,
    slot_angle_in,
    owner_slot_in,
    counts_in,
    out,
    shear_out,
    scan_y_out,
    slot_angle_out,
    owner_slot_out,
    shear,
    scan_x,
    scan_y,
    slot_angle,
    owner_slot,
    counts,
    shears,
    scans_y,
    slot_angles,
    owner_slots,
    film,
    probe,
    table,
    table_t,
    sent0,
    sent1,
    sent2,
    got0,
    got1,
    got2,
    mix0,
    mix1,
    mix2,
    part0,
    part1,
    part2,
    own,
    measured,
    cuts,
    windows,
    spreads,
    picks,
    placed,
    spec,
    back,
    load_sem,
    film_send,
    film_recv,
    mix_send,
    mix_recv,
    own_send,
    own_recv,
    amp_send,
    amp_recv,
    meta_load,
    meta_send,
    meta_recv,
    meta_pull,
    cut_send,
    pass_send,
    win_recv,
):
    strips, angle_devs, depths, layers, slots, columns = sizes
    quarter = strips // 4
    half = slots // depths
    share = WX // angle_devs
    reach = share + SHEAR
    sent = (sent0, sent1, sent2)
    got = (got0, got1, got2)
    mix = (mix0, mix1, mix2)
    parts = (part0, part1, part2)
    s = lax.axis_index("strip")
    a = lax.axis_index("angle")
    d = lax.axis_index("depth")
    meta = Meta(shear, owner_slot, slots, ())

    def rcopy(source, target, send_sem, recv_sem, **where):
        return pltpu.make_async_remote_copy(
            source, target, send_sem, recv_sem, device_id=where, device_id_type=MESH
        )

    def wrap(strip):
        return lax.rem(strip + 4 * strips, strips)

    metas = [
        pltpu.make_async_copy(source, target, meta_load.at[i])
        for i, (source, target) in enumerate(
            (
                (shear_in, shear),
                (scan_x_in, scan_x),
                (scan_y_in, scan_y),
                (slot_angle_in, slot_angle),
                (owner_slot_in, owner_slot),
                (counts_in, counts),
            )
        )
    ]
    loads = [
        pltpu.make_async_copy(
            crystal.at[layer, part],
            film.at[layer * WX : (layer + 1) * WX, part * columns : (part + 1) * columns],
            load_sem.at[layer * 2 + part],
        )
        for layer in range(layers)
        for part in range(2)
    ]
    late = [
        pltpu.make_async_copy(source, target, load_sem.at[2 * layers + i])
        for i, (source, target) in enumerate(
            ((probe_in, probe), (table_in, table), (table_t_in, table_t))
        )
    ]
    for copy in metas + loads:
        copy.start()

    barrier = pltpu.get_barrier_semaphore()
    shifts = set()
    for k in range(REACHES):
        for t in range(quarter):
            shifts |= {(1 - k + 4 * t) % strips, (k - 1 - 4 * t) % strips}
    expected = jnp.int32(0)
    for shift in sorted(shifts | {0}):
        peer = wrap(s + shift)
        if quarter == 1 and shift:
            close = jnp.abs(peer - s) == 1
        else:
            close = peer >= 0
        near = angle_devs + depths - 1 - (1 if shift == 0 else 0)
        expected = expected + jnp.where(close, near, 0)

        @pl.when(close)
        def _():
            for step in range(angle_devs):
                if shift or step:
                    place = {"strip": peer, "angle": lax.rem(a + step, angle_devs)}
                    pl.semaphore_signal(barrier, 1, device_id=place, device_id_type=MESH)
            for step in range(1, depths):
                place = {"strip": peer, "depth": lax.rem(d + step, depths)}
                pl.semaphore_signal(barrier, 1, device_id=place, device_id_type=MESH)

    out[...] = jnp.zeros(out.shape, jnp.float32)
    placed[...] = jnp.zeros(placed.shape, jnp.bfloat16)

    for copy in metas + loads:
        copy.wait()
    for copy in late:
        copy.start()

    def block(k, device):
        rows = ROWS[k] // depths
        return pl.ds(pl.multiple_of(device * rows, rows), rows)

    def mix_copy(k, q, step):
        target = lax.rem(d + step, depths)
        return rcopy(
            sent[k].at[q, block(k, target)],
            mix[k].at[q, step],
            mix_send.at[k, q, step],
            mix_recv.at[k, q, step],
            depth=target,
        )

    def film_copy(k, q):
        return rcopy(
            parts[k].at[q],
            got[k].at[q % half, block(k, d)],
            film_send.at[k, q],
            film_recv.at[k, d, q % half],
            strip=wrap(s - k + 4 * (q % quarter) + 1),
            depth=q // half,
        )

    def own_copy(q):
        return rcopy(
            sent[1].at[q],
            own.at[d, q % half],
            own_send.at[q],
            own_recv.at[d, q % half],
            depth=q // half,
        )

    def exchange(k, q):
        for step in range(1, depths):
            mix_copy(k, q, step).start()

    def merge(k, q):
        value = sent[k][q, block(k, d)].astype(jnp.float32)
        for step in range(1, depths):
            mix_copy(k, q, step).wait_recv()
            value = value + mix[k][q, step].astype(jnp.float32)
        parts[k][q] = value.astype(jnp.bfloat16)
        film_copy(k, q).start()

    def own_strip(k, q):
        return (1 - k + 4 * (q % quarter)) % strips == 0

    def project(k, q):
        home = s - k
        offset = meta.pick(scan_x, home, q) - WX * k + BASES[k]
        angle = meta.pick(slot_angle, home, q)
        corner = meta.pick(scan_y, home, q)
        gap = differences(ROWS[k], WX)
        chosen = jnp.concatenate(
            [one_hot(gap == offset + meta.shear(angle, z)) for z in range(layers)], axis=1
        )
        tall = dot(chosen, film[...]).astype(jnp.bfloat16)
        window = one_hot(differences(columns, FRAME) == -corner)
        return jnp.concatenate(
            [dot(tall[:, :columns], window), dot(tall[:, columns:], window)], axis=1
        ).astype(jnp.bfloat16)

    def reached(k):
        return (s - k >= 0) & (s - k <= strips - 3)

    for q in range(slots):
        for k in (0, 2):

            @pl.when(reached(k))
            def _():
                sent[k][q] = project(k, q)
                if q or k:
                    exchange(k, q)

            if q == 0 and k == 0:
                pl.semaphore_wait(barrier, expected)

                @pl.when(reached(0))
                def _():
                    exchange(0, 0)


    def amp_copy(other):
        return rcopy(
            amplitude.at[other * half : (other + 1) * half],
            measured.at[d],
            amp_send.at[other],
            amp_recv.at[d],
            depth=other,
        )

    def amp_own(other):
        return pltpu.make_async_copy(
            amplitude.at[other * half : (other + 1) * half], measured.at[d], amp_recv.at[d]
        )

    tables = (
        (shear_in, shear_out, shears),
        (scan_y_in, scan_y_out, scans_y),
        (slot_angle_in, slot_angle_out, slot_angles),
        (owner_slot_in, owner_slot_out, owner_slots),
    )

    def meta_copies(step):
        return [
            rcopy(
                source,
                target.at[step],
                meta_send.at[step, i],
                meta_recv.at[step, i],
                angle=lax.rem(a + step, angle_devs),
            )
            for i, (source, target, _) in enumerate(tables)
        ]

    def meta_pulls(step):
        return [
            pltpu.make_async_copy(target.at[step], local.at[step], meta_pull.at[step, i])
            for i, (_, target, local) in enumerate(tables)
        ]

    for step in range(1, angle_devs):
        for copy in meta_copies(step):
            copy.start()

    for other in range(depths):

        @pl.when(d != other)
        def _():
            amp_copy(other).start()

        @pl.when(d == other)
        def _():
            amp_own(other).start()

    for q in range(slots):
        for k in (0, 2):

            @pl.when(reached(k))
            def _():
                merge(k, q)


    @pl.when(reached(1))
    def _():
        for q in range(slots):
            sent[1][q] = project(1, q)
            if own_strip(1, q):

                @pl.when(d == q // half)
                def _():
                    own[d, q % half] = sent[1][q]

                @pl.when(d != q // half)
                def _():
                    own_copy(q).start()
            else:
                exchange(1, q)
        for q in range(slots):
            if not own_strip(1, q):
                merge(1, q)

    groups = [(meta, scan_y, slot_angle)]
    for step in range(1, angle_devs):
        lead = (step,)
        groups.append((Meta(shears, owner_slots, slots, lead), scans_y, slot_angles))
    depth_rows = placed.shape[0]

    def prepare(step, k):
        home = s - k
        source, corners, angles = groups[step]
        lifts = []
        for q in range(slots):
            corner = source.pick(corners, home, q)
            spreads[step, k, q] = one_hot(differences(FRAME, columns) == corner)
            angle = source.pick(angles, home, q)
            lifts.append([source.shear(angle, z) for z in range(layers)])
        gap = differences(share, depth_rows)
        for z in range(layers):
            mask = gap == SHEAR - 1 - lifts[0][z]
            for q in range(1, slots):
                mask = mask | (gap == q * reach + SHEAR - 1 - lifts[q][z])
            picks[step, k, z * share : (z + 1) * share] = one_hot(mask)

    for k in range(REACHES):

        @pl.when(reached(k))
        def _():
            prepare(0, k)

    for copy in late:
        copy.wait()
    for other in range(depths):

        @pl.when(d != other)
        def _():
            rcopy(
                amplitude.at[other * half : (other + 1) * half],
                measured.at[other],
                amp_send.at[other],
                amp_recv.at[other],
                depth=other,
            ).wait_recv()

        @pl.when(d == other)
        def _():
            amp_own(other).wait()


    def cut_copy(k, lane, quota, home, step):
        target = lax.rem(a + step, angle_devs)
        return rcopy(
            cuts.at[lane, k, target],
            windows.at[step, k, quota],
            cut_send.at[k, lane, step],
            win_recv.at[step, k, quota],
            strip=wrap(home + k),
            angle=target,
        )

    def owned(act):
        for lane in range(half):
            quota = d * half + lane
            home = wrap(s - 1 - 4 * lax.rem(quota, quarter))

            @pl.when(home <= strips - 3)
            def _():
                act(lane, quota, home, wrap(home + 1) == s)

    def dispatch(k, lane, quota, home, local, act):
        for step in list(range(1, angle_devs)) + [0]:
            if k == 1 and step == 0:

                @pl.when(jnp.logical_not(local))
                def _():
                    act(cut_copy(k, lane, quota, home, step))
            else:
                act(cut_copy(k, lane, quota, home, step))

    def work(lane, quota, home, local):
        def arrive(k):
            for source in range(depths):
                rows = ROWS[k] // depths
                rcopy(
                    parts[k].at[lane],
                    got[k].at[lane, source * rows : (source + 1) * rows],
                    film_send.at[k, lane],
                    film_recv.at[k, source, lane],
                    strip=wrap(home + k),
                    depth=source,
                ).wait_recv()

        @pl.when(local)
        def _():
            value = own[d, lane].astype(jnp.float32)
            for step in range(1, depths):
                source = lax.rem(d + step, depths)
                rcopy(
                    sent[1].at[lane],
                    own.at[source, lane],
                    own_send.at[lane],
                    own_recv.at[source, lane],
                    depth=source,
                ).wait_recv()
                value = value + own[source, lane].astype(jnp.float32)
            got[1][lane] = value.astype(jnp.bfloat16)

        @pl.when(jnp.logical_not(local))
        def _():
            arrive(1)

        def forward(low, high, extra):
            rows = slice(low, high)
            whole = got1[lane, rows].astype(jnp.float32) + extra.astype(jnp.float32)
            re, im = whole[:, :FRAME], whole[:, FRAME:]
            probe_re = probe[0, rows].astype(jnp.float32)
            probe_im = probe[1, rows].astype(jnp.float32)
            exit_wave = jnp.concatenate(
                [probe_re * re - probe_im * im, probe_re * im + probe_im * re], axis=1
            ).astype(jnp.bfloat16)
            section = dot(exit_wave, table[...]).astype(jnp.bfloat16)
            left = jnp.concatenate(
                [table_t[:, rows], table_t[:, FRAME + low : FRAME + high]], axis=1
            )
            return dot(left, jnp.concatenate([section[:, :FRAME], section[:, FRAME:]], axis=0))

        arrive(0)
        spec[...] = forward(0, WX, got0[lane])
        arrive(2)
        spectrum = spec[...] + forward(WX, FRAME, got2[lane])
        spec_re, spec_im = spectrum[:FRAME], spectrum[FRAME:]
        magnitude = jnp.sqrt(spec_re * spec_re + spec_im * spec_im)
        levels = jnp.concatenate(
            [measured[source, lane] for source in range(depths)], axis=0
        ).astype(jnp.float32)
        live = meta.slot(home, quota) < counts[0, home]
        live = jnp.where(live, 1.0, 0.0).astype(jnp.float32)
        factor = (1.0 - levels / jnp.maximum(magnitude, 1.0)) * live
        residual = jnp.concatenate([spec_re * factor, spec_im * factor], axis=1).astype(
            jnp.bfloat16
        )
        inverse = dot(residual, table_t[...]).astype(jnp.bfloat16)
        stacked = jnp.concatenate([inverse[:, :FRAME], inverse[:, FRAME:]], axis=0)
        offset = meta.pick(scan_x, home, quota)

        def backward(low, high):
            rows = slice(low, high)
            left = jnp.concatenate([table[rows], table[FRAME + low : FRAME + high]], axis=0)
            wave = dot(left, stacked)
            re, im = wave[: high - low], wave[high - low :]
            probe_re = probe[0, rows].astype(jnp.float32)
            probe_im = probe[1, rows].astype(jnp.float32)
            return jnp.concatenate(
                [probe_re * re + probe_im * im, probe_re * im - probe_im * re], axis=1
            ).astype(jnp.bfloat16)

        def cut(k, low, value):
            gap = differences(reach, value.shape[0])
            for part in range(angle_devs):
                first = WX * k - offset + part * share - (SHEAR - 1) - low
                cuts[lane, k, part] = dot(one_hot(gap == first), value).astype(jnp.bfloat16)

        top = backward(0, WX)
        back[0:WX] = top
        cut(0, 0, top)
        dispatch(0, lane, quota, home, local, lambda copy: copy.start())
        bottom = backward(WX, FRAME)
        back[WX:FRAME] = bottom
        cut(2, WX, bottom)
        dispatch(2, lane, quota, home, local, lambda copy: copy.start())
        cut(1, 0, back[...])
        dispatch(1, lane, quota, home, local, lambda copy: copy.start())

        @pl.when(local)
        def _():
            windows[0, 1, quota] = cuts[lane, 1, a]


    owned(work)

    for step in range(1, angle_devs):
        for copy in meta_copies(step):
            copy.wait_recv()
        for copy in meta_pulls(step):
            copy.start()
    for step in range(1, angle_devs):
        for copy in meta_pulls(step):
            copy.wait()
    for step in range(1, angle_devs):
        for k in range(REACHES):

            @pl.when(reached(k))
            def _():
                prepare(step, k)


    def pass_copy(step, k, q, other):
        return rcopy(
            windows.at[step, k, q],
            windows.at[step, k, q],
            pass_send.at[step, k, q % half, other],
            win_recv.at[step, k, q],
            depth=other,
        )

    def relay(step, k):
        for q in range(slots):

            @pl.when(d == q // half)
            def _():
                if not (step == 0 and own_strip(k, q)):
                    cut_copy(k, q % half, q, s - k, step).wait_recv()
                for other in range(depths):
                    if other != q // half:
                        pass_copy(step, k, q, other).start()

    def place(step, k, q, at):
        value = windows[step, k, q]
        spread = spreads[step, k, q]
        for part in range(2):
            placed[pl.ds(pl.multiple_of(at, 16), reach), part * columns : (part + 1) * columns] = dot(
                value[:, part * FRAME : (part + 1) * FRAME], spread
            ).astype(jnp.bfloat16)

    def deposit(step, k):
        for lane in range(half):
            q = d * half + lane
            place(step, k, q, q * reach)
        for q in range(slots):

            @pl.when(d != q // half)
            def _():
                pass_copy(step, k, q, q // half).wait_recv()
                place(step, k, q, q * reach)

        value = dot(picks[step, k], placed[...]) * scaling
        for z in range(layers):
            for part in range(2):
                out[z, part] += value[
                    z * share : (z + 1) * share, part * columns : (part + 1) * columns
                ]

    order = [(0, 1)] + [(step, 1) for step in range(1, angle_devs)]
    order += [(step, k) for step in list(range(1, angle_devs)) + [0] for k in (0, 2)]
    for i in range(len(order) + 1):
        if i < len(order):
            step, k = order[i]

            @pl.when(reached(k))
            def _():
                relay(step, k)

        if i:
            step, k = order[i - 1]

            @pl.when(reached(k))
            def _():
                deposit(step, k)

    for other in range(depths):

        @pl.when(d != other)
        def _():
            amp_copy(other).wait_send()

    for step in range(1, angle_devs):
        for copy in meta_copies(step):
            copy.wait_send()
    for k in range(REACHES):

        @pl.when(reached(k))
        def _():
            for q in range(slots):
                if own_strip(k, q):

                    @pl.when(d != q // half)
                    def _():
                        own_copy(q).wait_send()
                else:
                    film_copy(k, q).wait_send()
                    for step in range(1, depths):
                        mix_copy(k, q, step).wait_send()

    def drain(lane, quota, home, local):
        for k in range(REACHES):
            dispatch(k, lane, quota, home, local, lambda copy: copy.wait_send())

    owned(drain)

    for step, k in order:

        @pl.when(reached(k))
        def _():
            for q in range(slots):

                @pl.when(d == q // half)
                def _():
                    for other in range(depths):
                        if other != q // half:
                            pass_copy(step, k, q, other).wait_send()


def body(sizes_of, crystal, probe, amplitude, shear, scan_x, scan_y, slot_angle, owner_slot, counts):
    strips, angle_devs, depths = sizes_of
    layers, _, _, columns = crystal.shape
    slots = owner_slot.shape[2]
    half = slots // depths
    share = WX // angle_devs
    reach = share + SHEAR
    depth_rows = -(-(slots * reach) // 128) * 128
    table, table_t = dft_tables()
    bf16 = jnp.bfloat16
    scan_x, scan_y, slot_angle, owner_slot = [
        jnp.swapaxes(value, 1, 2) for value in (scan_x, scan_y, slot_angle, owner_slot)
    ]
    sizes = (strips, angle_devs, depths, layers, slots, columns)
    tables = (shear, scan_y, slot_angle, owner_slot)
    hbm = pl.BlockSpec(memory_space=pltpu.HBM)
    vmem = pl.BlockSpec(memory_space=pltpu.VMEM)
    dma = pltpu.SemaphoreType.DMA
    small = (shear, scan_x, scan_y, slot_angle, owner_slot, counts)
    scratch = [pltpu.SMEM(x.shape, jnp.int32) for x in small]
    scratch += [pltpu.SMEM((angle_devs,) + x.shape, jnp.int32) for x in tables]
    scratch += [
        pltpu.VMEM((layers * WX, 2 * columns), bf16),
        pltpu.VMEM(probe.shape, bf16),
        pltpu.VMEM(table.shape, bf16),
        pltpu.VMEM(table.shape, bf16),
    ]
    scratch += [pltpu.VMEM((slots, rows, 2 * FRAME), bf16) for rows in ROWS]
    scratch += [pltpu.VMEM((half, rows, 2 * FRAME), bf16) for rows in ROWS]
    scratch += [pltpu.VMEM((slots, depths, rows // depths, 2 * FRAME), bf16) for rows in ROWS]
    scratch += [pltpu.VMEM((slots, rows // depths, 2 * FRAME), bf16) for rows in ROWS]
    scratch += [pltpu.VMEM((depths, half, FRAME, 2 * FRAME), bf16)]
    scratch += [
        pltpu.VMEM((depths, half, FRAME // depths, FRAME), bf16),
        pltpu.VMEM((half, REACHES, angle_devs, reach, 2 * FRAME), bf16),
        pltpu.VMEM((angle_devs, REACHES, slots, reach, 2 * FRAME), bf16),
        pltpu.VMEM((angle_devs, REACHES, slots, FRAME, columns), bf16),
        pltpu.VMEM((angle_devs, REACHES, layers * share, depth_rows), bf16),
        pltpu.VMEM((depth_rows, 2 * columns), bf16),
        pltpu.VMEM((2 * FRAME, FRAME), jnp.float32),
        pltpu.VMEM((FRAME, 2 * FRAME), bf16),
        dma((2 * layers + 3,)),
        dma((REACHES, slots)),
        dma((REACHES, depths, half)),
        dma((REACHES, slots, depths)),
        dma((REACHES, slots, depths)),
        dma((slots,)),
        dma((depths, half)),
        dma((depths,)),
        dma((depths,)),
        dma((len(small),)),
        dma((angle_devs, len(tables))),
        dma((angle_devs, len(tables))),
        dma((angle_devs, len(tables))),
        dma((REACHES, half, angle_devs)),
        dma((angle_devs, REACHES, half, depths)),
        dma((angle_devs, REACHES, slots)),
    ]
    scaling = 1.0 / (shear.shape[0] * angle_devs)
    result, *_ = pl.pallas_call(
        functools.partial(kernel, sizes, scaling),
        out_shape=(jax.ShapeDtypeStruct((layers, 2, share, columns), jnp.float32),)
        + tuple(jax.ShapeDtypeStruct((angle_devs,) + x.shape, jnp.int32) for x in tables),
        in_specs=[hbm] * 11,
        out_specs=(vmem,) + (hbm,) * 4,
        scratch_shapes=scratch,
        compiler_params=pltpu.CompilerParams(
            collective_id=0, has_side_effects=True, vmem_limit_bytes=VMEM_LIMIT
        ),
    )(
        *(
            pltpu.with_memory_space_constraint(x, pltpu.HBM)
            for x in (crystal, probe, amplitude, table, table_t, *small)
        )
    )
    return result


def solution(mesh):
    placed = (
        P(("groups", "depth"), None, "strip", None),
        P(),
        P("angle", ("groups", "strip", "depth"), None),
        P(("groups", "angle"), "depth"),
        P(("groups", "angle"), None, None),
        P(("groups", "angle"), None, None),
        P(("groups", "angle"), None, None),
        P(("groups", "angle"), None, None),
        P(("groups", "angle"), None),
    )
    sizes_of = (mesh.shape["strip"], mesh.shape["angle"], mesh.shape["depth"])
    return jax.shard_map(
        functools.partial(body, sizes_of),
        mesh=mesh,
        in_specs=placed,
        out_specs=P(("groups", "depth"), None, ("strip", "angle"), None),
        check_vma=False,
    )
```

```python
import functools

import jax
import jax.numpy as jnp
import numpy as np
from jax import lax
from jax.experimental import pallas as pl
from jax.experimental.pallas import tpu as pltpu
from jax.sharding import PartitionSpec as P

FRAME = 256
WX = 128
SHEAR = 16
REACHES = 3
ROWS = (WX, FRAME, FRAME - WX)
BASES = (0, 0, WX)
VMEM_LIMIT = 44 * 2**20
MESH = pl.DeviceIdType.MESH


def dft_tables():
    index_row = np.arange(FRAME)
    phase = (index_row[:, None] * index_row[None, :] % FRAME) * (2.0 * np.pi / FRAME)
    real = np.cos(phase) / np.sqrt(FRAME)
    imag = -np.sin(phase) / np.sqrt(FRAME)
    table = np.block([[real, imag], [-imag, real]]).astype(np.float32)
    return jnp.asarray(np.stack([table, table.T]), jnp.bfloat16)


def dot(left, right):
    return jnp.dot(left, right, preferred_element_type=jnp.float32)


def differences(rows, columns):
    shape = (rows, columns)
    return lax.broadcasted_iota(jnp.int32, shape, 1) - lax.broadcasted_iota(jnp.int32, shape, 0)


def one_hot(mask):
    return jnp.where(mask, 1.0, 0.0).astype(jnp.bfloat16)


class Meta:
    def __init__(self, lifts, owner_slot, slots, lead):
        self.lifts, self.owner_slot = lifts, owner_slot
        self.slots, self.lead = slots, lead

    def shear(self, angle, z):
        return self.lifts[self.lead + (angle, z)]

    def pick(self, ref, home, quota):
        value = jnp.int32(0)
        for m in range(self.slots):
            at = self.lead + (0, m, home)
            value = value + jnp.where(self.owner_slot[at] == quota, ref[at], 0)
        return value

    def slot(self, home, quota):
        value = jnp.int32(0)
        for m in range(self.slots):
            at = self.lead + (0, m, home)
            value = value + jnp.where(self.owner_slot[at] == quota, m, 0)
        return value


def kernel(
    sizes,
    scaling,
    crystal,
    probe_in,
    amplitude,
    tables_in,
    shear_in,
    scan_x_in,
    scan_y_in,
    slot_angle_in,
    owner_slot_in,
    counts_in,
    out,
    shear_out,
    scan_y_out,
    slot_angle_out,
    owner_slot_out,
    shear,
    scan_x,
    scan_y,
    slot_angle,
    owner_slot,
    counts,
    shears,
    scans_y,
    slot_angles,
    owner_slots,
    film,
    probe,
    dft,
    sent0,
    sent1,
    sent2,
    got0,
    got1,
    got2,
    mix0,
    mix1,
    mix2,
    part0,
    part1,
    part2,
    own,
    measured,
    cuts,
    windows,
    dft_rot,
    probe_rot,
    picks,
    placed,
    spec,
    back,
    load_sem,
    film_send,
    film_recv,
    mix_send,
    mix_recv,
    own_send,
    own_recv,
    amp_send,
    amp_recv,
    meta_load,
    meta_send,
    meta_recv,
    meta_pull,
    cut_send,
    pass_send,
    win_recv,
):
    strips, angle_devs, depths, layers, slots, columns = sizes
    quarter = strips // 4
    half = slots // depths
    share = WX // angle_devs
    reach = share + SHEAR
    sent = (sent0, sent1, sent2)
    got = (got0, got1, got2)
    mix = (mix0, mix1, mix2)
    parts = (part0, part1, part2)
    s = lax.axis_index("strip")
    a = lax.axis_index("angle")
    d = lax.axis_index("depth")
    meta = Meta(shear, owner_slot, slots, ())
    margin = columns - FRAME

    def lanes(rows):
        return lax.broadcasted_iota(jnp.int32, (rows, margin), 1)

    def rcopy(source, target, send_sem, recv_sem, **where):
        return pltpu.make_async_remote_copy(
            source, target, send_sem, recv_sem, device_id=where, device_id_type=MESH
        )

    def wrap(strip):
        return lax.rem(strip + 4 * strips, strips)

    metas = [
        pltpu.make_async_copy(source, target, meta_load.at[i])
        for i, (source, target) in enumerate(
            (
                (shear_in, shear),
                (scan_x_in, scan_x),
                (scan_y_in, scan_y),
                (slot_angle_in, slot_angle),
                (owner_slot_in, owner_slot),
                (counts_in, counts),
            )
        )
    ]
    loads = [
        pltpu.make_async_copy(
            crystal.at[:, part],
            film.at[:, :, part * columns : (part + 1) * columns],
            load_sem.at[0],
        )
        for part in range(2)
    ]
    late = [
        pltpu.make_async_copy(source, target, load_sem.at[1 + i])
        for i, (source, target) in enumerate(((probe_in, probe), (tables_in, dft)))
    ]
    table, table_t = dft.at[0], dft.at[1]
    for copy in metas + loads:
        copy.start()

    barrier = pltpu.get_barrier_semaphore()
    shifts = set()
    for k in range(REACHES):
        for t in range(quarter):
            shifts |= {(1 - k + 4 * t) % strips, (k - 1 - 4 * t) % strips}
    expected = jnp.int32(0)
    for shift in sorted(shifts | {0}):
        peer = wrap(s + shift)
        if quarter == 1 and shift:
            close = jnp.abs(peer - s) == 1
        else:
            close = peer >= 0
        near = angle_devs + depths - 1 - (1 if shift == 0 else 0)
        expected = expected + jnp.where(close, near, 0)

        @pl.when(close)
        def _():
            for step in range(angle_devs):
                if shift or step:
                    place = {"strip": peer, "angle": lax.rem(a + step, angle_devs)}
                    pl.semaphore_signal(barrier, 1, device_id=place, device_id_type=MESH)
            for step in range(1, depths):
                place = {"strip": peer, "depth": lax.rem(d + step, depths)}
                pl.semaphore_signal(barrier, 1, device_id=place, device_id_type=MESH)

    out[...] = jnp.zeros(out.shape, jnp.float32)
    placed[...] = jnp.zeros(placed.shape, jnp.bfloat16)

    for copy in metas:
        copy.wait()
    pltpu.make_async_copy(film, film, load_sem.at[0]).wait()
    for copy in late:
        copy.start()

    def block(k, device):
        rows = ROWS[k] // depths
        return pl.ds(pl.multiple_of(device * rows, rows), rows)

    def mix_copy(k, q, step):
        target = lax.rem(d + step, depths)
        return rcopy(
            sent[k].at[q, block(k, target)],
            mix[k].at[q, step - 1],
            mix_send.at[k, step - 1],
            mix_recv.at[k, q, step - 1],
            depth=target,
        )

    def film_copy(k, q):
        return rcopy(
            parts[k].at[q],
            got[k].at[q % half, block(k, d)],
            film_send.at[k],
            film_recv.at[k, q % half],
            strip=wrap(s - k + 4 * (q % quarter) + 1),
            depth=q // half,
        )

    def own_copy(q):
        return rcopy(
            sent[1].at[q],
            own.at[d, q % half],
            own_send.at[q],
            own_recv.at[d, q % half],
            depth=q // half,
        )

    def exchange(k, q):
        for step in range(1, depths):
            mix_copy(k, q, step).start()

    def merge(k, q):
        value = sent[k][q, block(k, d)].astype(jnp.float32)
        for step in range(1, depths):
            mix_copy(k, q, step).wait_recv()
            value = value + mix[k][q, step - 1].astype(jnp.float32)
        parts[k][q] = value.astype(jnp.bfloat16)
        film_copy(k, q).start()

    def own_strip(k, q):
        return (1 - k + 4 * (q % quarter)) % strips == 0

    def project(k):
        home = s - k
        gap = differences(ROWS[k], WX)
        chosen = []
        for q in range(slots):
            offset = meta.pick(scan_x, home, q) - WX * k + BASES[k]
            angle = meta.pick(slot_angle, home, q)
            chosen.append(
                jnp.concatenate(
                    [one_hot(gap == offset + meta.shear(angle, z)) for z in range(layers)], axis=1
                )
            )
        flat = film[...].reshape(layers * WX, 2 * columns)
        tall = dot(jnp.concatenate(chosen, axis=0), flat)
        for q in range(slots):
            corner = meta.pick(scan_y, home, q)
            first = lanes(ROWS[k]) >= corner
            rows = tall[q * ROWS[k] : (q + 1) * ROWS[k]]
            wound = []
            for part in range(2):
                side = rows[:, part * columns : (part + 1) * columns]
                wound += [jnp.where(first, side[:, :margin], side[:, FRAME:]), side[:, margin:FRAME]]
            sent[k][q] = jnp.concatenate(wound, axis=1).astype(jnp.bfloat16)

    def reached(k):
        return (s - k >= 0) & (s - k <= strips - 3)

    for k in (0, 2):

        @pl.when(reached(k))
        def _():
            project(k)

    pl.semaphore_wait(barrier, expected)
    for k in (0, 2):

        @pl.when(reached(k))
        def _():
            for q in range(slots):
                exchange(k, q)


    def amp_copy(other):
        return rcopy(
            amplitude.at[other * half : (other + 1) * half],
            measured.at[d],
            amp_send.at[other],
            amp_recv.at[0],
            depth=other,
        )

    def amp_own(other):
        return pltpu.make_async_copy(
            amplitude.at[other * half : (other + 1) * half], measured.at[d], amp_recv.at[0]
        )

    tables = (
        (shear_in, shear_out, shears),
        (scan_y_in, scan_y_out, scans_y),
        (slot_angle_in, slot_angle_out, slot_angles),
        (owner_slot_in, owner_slot_out, owner_slots),
    )

    def meta_copies(step):
        return [
            rcopy(
                source,
                target.at[step],
                meta_send.at[step - 1, i],
                meta_recv.at[step - 1, i],
                angle=lax.rem(a + step, angle_devs),
            )
            for i, (source, target, _) in enumerate(tables)
        ]

    def meta_pulls(step):
        return [
            pltpu.make_async_copy(target.at[step], local.at[step], meta_pull.at[step - 1, i])
            for i, (_, target, local) in enumerate(tables)
        ]

    for step in range(1, angle_devs):
        for copy in meta_copies(step):
            copy.start()

    for other in range(depths):

        @pl.when(d != other)
        def _():
            amp_copy(other).start()

        @pl.when(d == other)
        def _():
            amp_own(other).start()

    for q in range(slots):
        for k in (0, 2):

            @pl.when(reached(k))
            def _():
                merge(k, q)


    @pl.when(reached(1))
    def _():
        project(1)
        for q in range(slots):
            if own_strip(1, q):

                @pl.when(d == q // half)
                def _():
                    own[d, q % half] = sent[1][q]

                @pl.when(d != q // half)
                def _():
                    own_copy(q).start()
            else:
                exchange(1, q)
        for q in range(slots):
            if not own_strip(1, q):
                merge(1, q)

    groups = [(meta, scan_y, slot_angle)]
    for step in range(1, angle_devs):
        lead = (step,)
        groups.append((Meta(shears, owner_slots, slots, lead), scans_y, slot_angles))
    depth_rows = placed.shape[0]

    def prepare(step, k):
        home = s - k
        source, _, angles = groups[step]
        lifts = []
        for q in range(slots):
            angle = source.pick(angles, home, q)
            lifts.append([source.shear(angle, z) for z in range(layers)])
        gap = differences(share, depth_rows)
        for z in range(layers):
            mask = gap == SHEAR - 1 - lifts[0][z]
            for q in range(1, slots):
                mask = mask | (gap == q * reach + SHEAR - 1 - lifts[q][z])
            picks[step, k, z * share : (z + 1) * share] = one_hot(mask)

    for k in range(REACHES):

        @pl.when(reached(k))
        def _():
            prepare(0, k)

    for copy in late:
        copy.wait()
    pltpu.make_async_copy(measured, measured, amp_recv.at[0]).wait()


    def cut_copy(k, lane, quota, home, step):
        target = lax.rem(a + step, angle_devs)
        return rcopy(
            cuts.at[lane, k, target],
            windows.at[step, k, quota],
            cut_send.at[k, lane],
            win_recv.at[step, k, quota],
            strip=wrap(home + k),
            angle=target,
        )

    def owned(act):
        for lane in range(half):
            quota = d * half + lane
            home = wrap(s - 1 - 4 * lax.rem(quota, quarter))

            @pl.when(home <= strips - 3)
            def _():
                act(lane, quota, home, wrap(home + 1) == s)

    def dispatch(k, lane, quota, home, local, act):
        for step in list(range(1, angle_devs)) + [0]:
            if k == 1 and step == 0:

                @pl.when(jnp.logical_not(local))
                def _():
                    act(cut_copy(k, lane, quota, home, step))
            else:
                act(cut_copy(k, lane, quota, home, step))

    def work(lane, quota, home, local):
        def arrive(k):
            pltpu.make_async_copy(got[k].at[lane], got[k].at[lane], film_recv.at[k, lane]).wait()

        corner = meta.pick(scan_y, home, quota)
        gap = differences(FRAME, FRAME)
        turn = one_hot((gap == -corner) | (gap == FRAME - corner))
        back_turn = one_hot((gap == corner) | (gap == corner - FRAME))
        for part in range(2):
            at = slice(part * FRAME, (part + 1) * FRAME)
            probe_rot[lane, part] = dot(probe[part], back_turn).astype(jnp.bfloat16)
            dft_rot[lane, 0, at] = dot(turn, table[at]).astype(jnp.bfloat16)
            dft_rot[lane, 1, :, at] = dot(table_t[:, at], back_turn).astype(jnp.bfloat16)

        @pl.when(local)
        def _():
            value = own[d, lane].astype(jnp.float32)
            for step in range(1, depths):
                source = lax.rem(d + step, depths)
                rcopy(
                    sent[1].at[lane],
                    own.at[source, lane],
                    own_send.at[lane],
                    own_recv.at[source, lane],
                    depth=source,
                ).wait_recv()
                value = value + own[source, lane].astype(jnp.float32)
            got[1][lane] = value.astype(jnp.bfloat16)

        @pl.when(jnp.logical_not(local))
        def _():
            arrive(1)

        def forward(low, high, extra):
            rows = slice(low, high)
            whole = got1[lane, rows].astype(jnp.float32) + extra.astype(jnp.float32)
            re, im = whole[:, :FRAME], whole[:, FRAME:]
            probe_re = probe_rot[lane, 0, rows].astype(jnp.float32)
            probe_im = probe_rot[lane, 1, rows].astype(jnp.float32)
            exit_wave = jnp.concatenate(
                [probe_re * re - probe_im * im, probe_re * im + probe_im * re], axis=1
            ).astype(jnp.bfloat16)
            section = dot(exit_wave, dft_rot[lane, 0]).astype(jnp.bfloat16)
            left = jnp.concatenate(
                [table_t[:, rows], table_t[:, FRAME + low : FRAME + high]], axis=1
            )
            return dot(left, jnp.concatenate([section[:, :FRAME], section[:, FRAME:]], axis=0))

        arrive(0)
        spec[...] = forward(0, WX, got0[lane])
        arrive(2)
        spectrum = spec[...] + forward(WX, FRAME, got2[lane])
        spec_re, spec_im = spectrum[:FRAME], spectrum[FRAME:]
        magnitude = jnp.sqrt(spec_re * spec_re + spec_im * spec_im)
        levels = jnp.concatenate(
            [measured[source, lane] for source in range(depths)], axis=0
        ).astype(jnp.float32)
        live = meta.slot(home, quota) < counts[0, home]
        live = jnp.where(live, 1.0, 0.0).astype(jnp.float32)
        factor = (1.0 - levels / jnp.maximum(magnitude, 1.0)) * live
        residual = jnp.concatenate([spec_re * factor, spec_im * factor], axis=1).astype(
            jnp.bfloat16
        )
        inverse = dot(residual, dft_rot[lane, 1]).astype(jnp.bfloat16)
        stacked = jnp.concatenate([inverse[:, :FRAME], inverse[:, FRAME:]], axis=0)
        offset = meta.pick(scan_x, home, quota)

        def backward(low, high):
            rows = slice(low, high)
            left = jnp.concatenate([table[rows], table[FRAME + low : FRAME + high]], axis=0)
            wave = dot(left, stacked)
            re, im = wave[: high - low], wave[high - low :]
            probe_re = probe_rot[lane, 0, rows].astype(jnp.float32)
            probe_im = probe_rot[lane, 1, rows].astype(jnp.float32)
            return jnp.concatenate(
                [probe_re * re + probe_im * im, probe_re * im - probe_im * re], axis=1
            ).astype(jnp.bfloat16)

        def cut(k, part, low, value):
            gap = differences(reach, value.shape[0])
            first = WX * k - offset + part * share - (SHEAR - 1) - low
            cuts[lane, k, part] = dot(one_hot(gap == first), value).astype(jnp.bfloat16)

        top = backward(0, WX)
        back[0:WX] = top
        for part in range(angle_devs):
            cut(0, part, 0, top)
        dispatch(0, lane, quota, home, local, lambda copy: copy.start())
        bottom = backward(WX, FRAME)
        back[WX:FRAME] = bottom
        for part in range(angle_devs):
            cut(1, part, 0, back[...])
        dispatch(1, lane, quota, home, local, lambda copy: copy.start())
        for part in range(angle_devs):
            cut(2, part, WX, bottom)
        dispatch(2, lane, quota, home, local, lambda copy: copy.start())

        @pl.when(local)
        def _():
            windows[0, 1, quota] = cuts[lane, 1, a]


    owned(work)

    for step in range(1, angle_devs):
        for copy in meta_copies(step):
            copy.wait_recv()
        for copy in meta_pulls(step):
            copy.start()
    for step in range(1, angle_devs):
        for copy in meta_pulls(step):
            copy.wait()
    for step in range(1, angle_devs):
        for k in range(REACHES):

            @pl.when(reached(k))
            def _():
                prepare(step, k)


    def pass_copy(step, k, q, other):
        return rcopy(
            windows.at[step, k, q],
            windows.at[step, k, q],
            pass_send.at[k, other],
            win_recv.at[step, k, q],
            depth=other,
        )

    def relay(step, k):
        for q in range(slots):

            @pl.when(d == q // half)
            def _():
                if not (step == 0 and own_strip(k, q)):
                    cut_copy(k, q % half, q, s - k, step).wait_recv()
                for other in range(depths):
                    if other != q // half:
                        pass_copy(step, k, q, other).start()

    def place(step, k, q, at):
        source, corners, _ = groups[step]
        first = lanes(reach) >= source.pick(corners, s - k, q)
        rows = pl.ds(pl.multiple_of(at, 16), reach)
        for part in range(2):
            head = windows[step, k, q, :, part * FRAME : part * FRAME + margin].astype(jnp.float32)
            left = part * columns
            placed[rows, left : left + margin] = jnp.where(first, head, 0.0).astype(jnp.bfloat16)
            placed[rows, left + margin : left + FRAME] = windows[
                step, k, q, :, part * FRAME + margin : (part + 1) * FRAME
            ]
            placed[rows, left + FRAME : left + columns] = jnp.where(first, 0.0, head).astype(
                jnp.bfloat16
            )

    def deposit(step, k):
        for lane in range(half):
            q = d * half + lane
            place(step, k, q, q * reach)
        for q in range(slots):

            @pl.when(d != q // half)
            def _():
                pass_copy(step, k, q, q // half).wait_recv()
                place(step, k, q, q * reach)

        value = dot(picks[step, k], placed[...]) * scaling
        for z in range(layers):
            for part in range(2):
                out[z, part] += value[
                    z * share : (z + 1) * share, part * columns : (part + 1) * columns
                ]

    later = range(1, angle_devs)
    stages = [[(0, 1)], [(step, 1) for step in later]]
    stages += [[(step, k) for step in later for k in (0, 2)], [(0, 0), (0, 2)]]

    def run(act, stage):
        for step, k in stages[stage]:

            @pl.when(reached(k))
            def _():
                act(step, k)

    run(relay, 0)
    run(deposit, 0)
    run(relay, 1)
    run(relay, 2)
    run(deposit, 1)
    run(relay, 3)
    run(deposit, 2)
    run(deposit, 3)

    for other in range(depths):

        @pl.when(d != other)
        def _():
            amp_copy(other).wait_send()

    for step in range(1, angle_devs):
        for copy in meta_copies(step):
            copy.wait_send()
    for k in range(REACHES):

        @pl.when(reached(k))
        def _():
            for q in range(slots):
                if own_strip(k, q):

                    @pl.when(d != q // half)
                    def _():
                        own_copy(q).wait_send()
            rest = [q for q in range(slots) if not own_strip(k, q)]
            if rest:
                whole = parts[k].at[slots - len(rest) :]
                pltpu.make_async_copy(whole, whole, film_send.at[k]).wait()
                for step in range(1, depths):
                    pltpu.make_async_copy(whole, whole, mix_send.at[k, step - 1]).wait()

    def drain(lane, quota, home, local):
        for k in range(REACHES):
            whole = cuts.at[lane, k]
            if k == 1:
                most = cuts.at[lane, k, 1:]

                @pl.when(local)
                def _():
                    pltpu.make_async_copy(most, most, cut_send.at[k, lane]).wait()

                @pl.when(jnp.logical_not(local))
                def _():
                    pltpu.make_async_copy(whole, whole, cut_send.at[k, lane]).wait()
            else:
                pltpu.make_async_copy(whole, whole, cut_send.at[k, lane]).wait()

    owned(drain)

    for k in range(REACHES):

        @pl.when(reached(k))
        def _():
            for other in range(depths):

                @pl.when(d != other)
                def _():
                    whole = windows.at[:, k, 0:half]
                    pltpu.make_async_copy(whole, whole, pass_send.at[k, other]).wait()


def body(sizes_of, crystal, probe, amplitude, shear, scan_x, scan_y, slot_angle, owner_slot, counts):
    strips, angle_devs, depths = sizes_of
    layers, _, _, columns = crystal.shape
    slots = owner_slot.shape[2]
    half = slots // depths
    share = WX // angle_devs
    reach = share + SHEAR
    depth_rows = -(-(slots * reach) // 128) * 128
    dft = dft_tables()
    bf16 = jnp.bfloat16
    scan_x, scan_y, slot_angle, owner_slot = [
        jnp.swapaxes(value, 1, 2) for value in (scan_x, scan_y, slot_angle, owner_slot)
    ]
    sizes = (strips, angle_devs, depths, layers, slots, columns)
    tables = (shear, scan_y, slot_angle, owner_slot)
    hbm = pl.BlockSpec(memory_space=pltpu.HBM)
    vmem = pl.BlockSpec(memory_space=pltpu.VMEM)
    dma = pltpu.SemaphoreType.DMA
    small = (shear, scan_x, scan_y, slot_angle, owner_slot, counts)
    scratch = [pltpu.SMEM(x.shape, jnp.int32) for x in small]
    scratch += [pltpu.SMEM((angle_devs,) + x.shape, jnp.int32) for x in tables]
    scratch += [
        pltpu.VMEM((layers, WX, 2 * columns), bf16),
        pltpu.VMEM(probe.shape, bf16),
        pltpu.VMEM(dft.shape, bf16),
    ]
    scratch += [pltpu.VMEM((slots, rows, 2 * FRAME), bf16) for rows in ROWS]
    scratch += [pltpu.VMEM((half, rows, 2 * FRAME), bf16) for rows in ROWS]
    scratch += [pltpu.VMEM((slots, depths - 1, rows // depths, 2 * FRAME), bf16) for rows in ROWS]
    scratch += [pltpu.VMEM((slots, rows // depths, 2 * FRAME), bf16) for rows in ROWS]
    scratch += [pltpu.VMEM((depths, half, FRAME, 2 * FRAME), bf16)]
    scratch += [
        pltpu.VMEM((depths, half, FRAME // depths, FRAME), bf16),
        pltpu.VMEM((half, REACHES, angle_devs, reach, 2 * FRAME), bf16),
        pltpu.VMEM((angle_devs, REACHES, slots, reach, 2 * FRAME), bf16),
        pltpu.VMEM((half,) + dft.shape, bf16),
        pltpu.VMEM((half,) + probe.shape, bf16),
        pltpu.VMEM((angle_devs, REACHES, layers * share, depth_rows), bf16),
        pltpu.VMEM((depth_rows, 2 * columns), bf16),
        pltpu.VMEM((2 * FRAME, FRAME), jnp.float32),
        pltpu.VMEM((FRAME, 2 * FRAME), bf16),
        dma((3,)),
        dma((REACHES,)),
        dma((REACHES, half)),
        dma((REACHES, depths - 1)),
        dma((REACHES, slots, depths - 1)),
        dma((slots,)),
        dma((depths, half)),
        dma((depths,)),
        dma((1,)),
        dma((len(small),)),
        dma((angle_devs - 1, len(tables))),
        dma((angle_devs - 1, len(tables))),
        dma((angle_devs - 1, len(tables))),
        dma((REACHES, half)),
        dma((REACHES, depths)),
        dma((angle_devs, REACHES, slots)),
    ]
    scaling = 1.0 / (shear.shape[0] * angle_devs)
    result, *_ = pl.pallas_call(
        functools.partial(kernel, sizes, scaling),
        out_shape=(jax.ShapeDtypeStruct((layers, 2, share, columns), jnp.float32),)
        + tuple(jax.ShapeDtypeStruct((angle_devs,) + x.shape, jnp.int32) for x in tables),
        in_specs=[hbm] * 10,
        out_specs=(vmem,) + (hbm,) * 4,
        scratch_shapes=scratch,
        compiler_params=pltpu.CompilerParams(
            collective_id=0, has_side_effects=True, vmem_limit_bytes=VMEM_LIMIT
        ),
    )(
        *(
            pltpu.with_memory_space_constraint(x, pltpu.HBM)
            for x in (crystal, probe, amplitude, dft, *small)
        )
    )
    return result


def solution(mesh):
    placed = (
        P(("groups", "depth"), None, "strip", None),
        P(),
        P("angle", ("groups", "strip", "depth"), None),
        P(("groups", "angle"), "depth"),
        P(("groups", "angle"), None, None),
        P(("groups", "angle"), None, None),
        P(("groups", "angle"), None, None),
        P(("groups", "angle"), None, None),
        P(("groups", "angle"), None),
    )
    sizes_of = (mesh.shape["strip"], mesh.shape["angle"], mesh.shape["depth"])
    return jax.shard_map(
        functools.partial(body, sizes_of),
        mesh=mesh,
        in_specs=placed,
        out_specs=P(("groups", "depth"), None, ("strip", "angle"), None),
        check_vma=False,
    )
```

```python
import functools

import jax
import jax.numpy as jnp
import numpy as np
from jax import lax
from jax.experimental import pallas as pl
from jax.experimental.pallas import tpu as pltpu
from jax.sharding import PartitionSpec as P

FRAME = 256
WX = 128
SHEAR = 16
REACHES = 3
ROWS = (WX, FRAME, FRAME - WX)
BASES = (0, 0, WX)
VMEM_LIMIT = 44 * 2**20
MESH = pl.DeviceIdType.MESH


def dft_tables():
    index_row = np.arange(FRAME)
    phase = (index_row[:, None] * index_row[None, :] % FRAME) * (2.0 * np.pi / FRAME)
    real = np.cos(phase) / np.sqrt(FRAME)
    imag = -np.sin(phase) / np.sqrt(FRAME)
    table = np.block([[real, imag], [-imag, real]]).astype(np.float32)
    return jnp.asarray(np.stack([table, table.T]), jnp.bfloat16)


def dot(left, right):
    return jnp.dot(left, right, preferred_element_type=jnp.float32)


def differences(rows, columns):
    shape = (rows, columns)
    return lax.broadcasted_iota(jnp.int32, shape, 1) - lax.broadcasted_iota(jnp.int32, shape, 0)


def one_hot(mask):
    return jnp.where(mask, 1.0, 0.0).astype(jnp.bfloat16)


class Meta:
    def __init__(self, lifts, owner_slot, slots, lead):
        self.lifts, self.owner_slot = lifts, owner_slot
        self.slots, self.lead = slots, lead

    def shear(self, angle, z):
        return self.lifts[self.lead + (angle, z)]

    def pick(self, ref, home, quota):
        value = jnp.int32(0)
        for m in range(self.slots):
            at = self.lead + (0, m, home)
            value = value + jnp.where(self.owner_slot[at] == quota, ref[at], 0)
        return value

    def slot(self, home, quota):
        value = jnp.int32(0)
        for m in range(self.slots):
            at = self.lead + (0, m, home)
            value = value + jnp.where(self.owner_slot[at] == quota, m, 0)
        return value


def bands(strips):
    return REACHES if strips - 3 >= 2 else 2


def batch_of(strips, angle_devs):
    every = [(step, k) for step in range(angle_devs) for k in range(bands(strips))]
    return [item for item in every if item != (0, 1)]


def kernel(
    sizes,
    scaling,
    crystal,
    probe_in,
    amplitude,
    tables_in,
    shear_in,
    scan_x_in,
    scan_y_in,
    slot_angle_in,
    owner_slot_in,
    counts_in,
    out,
    shear_out,
    scan_y_out,
    slot_angle_out,
    owner_slot_out,
    shear,
    scan_x,
    scan_y,
    slot_angle,
    owner_slot,
    counts,
    shears,
    scans_y,
    slot_angles,
    owner_slots,
    film,
    probe,
    dft,
    sent0,
    sent1,
    sent2,
    got0,
    got1,
    got2,
    mix0,
    mix1,
    mix2,
    part0,
    part1,
    part2,
    own,
    measured,
    cuts,
    windows,
    dft_rot,
    probe_rot,
    picks_local,
    picks_mine,
    picks_theirs,
    placed_local,
    placed_mine,
    placed_theirs,
    spec,
    back,
    load_sem,
    film_send,
    film_recv,
    mix_send,
    mix_recv,
    own_send,
    own_recv,
    amp_send,
    amp_recv,
    meta_load,
    meta_send,
    meta_recv,
    meta_pull,
    cut_send,
    pass_send,
    win_recv,
):
    strips, angle_devs, depths, layers, slots, columns = sizes
    quarter = strips // 4
    half = slots // depths
    share = WX // angle_devs
    reach = share + SHEAR
    sent = (sent0, sent1, sent2)
    got = (got0, got1, got2)
    mix = (mix0, mix1, mix2)
    parts = (part0, part1, part2)
    s = lax.axis_index("strip")
    a = lax.axis_index("angle")
    d = lax.axis_index("depth")
    meta = Meta(shear, owner_slot, slots, ())
    margin = columns - FRAME
    kinds = bands(strips)
    batch = batch_of(strips, angle_devs)
    rows_of = dict(zip(batch, range(len(batch))))

    def kind(k):
        return k % kinds

    def seat(device):
        return 0 if depths == 2 else device


    def lanes(rows):
        return lax.broadcasted_iota(jnp.int32, (rows, margin), 1)

    def rcopy(source, target, send_sem, recv_sem, **where):
        return pltpu.make_async_remote_copy(
            source, target, send_sem, recv_sem, device_id=where, device_id_type=MESH
        )

    def wrap(strip):
        return lax.rem(strip + 4 * strips, strips)

    metas = [
        pltpu.make_async_copy(source, target, meta_load.at[i])
        for i, (source, target) in enumerate(
            (
                (shear_in, shear),
                (scan_x_in, scan_x),
                (scan_y_in, scan_y),
                (slot_angle_in, slot_angle),
                (owner_slot_in, owner_slot),
                (counts_in, counts),
            )
        )
    ]
    loads = [
        pltpu.make_async_copy(
            crystal.at[:, part],
            film.at[:, :, part * columns : (part + 1) * columns],
            load_sem.at[0],
        )
        for part in range(2)
    ]
    late = [
        pltpu.make_async_copy(source, target, load_sem.at[1 + i])
        for i, (source, target) in enumerate(((probe_in, probe), (tables_in, dft)))
    ]
    table, table_t = dft.at[0], dft.at[1]
    for copy in metas + loads:
        copy.start()

    barrier = pltpu.get_barrier_semaphore()
    shifts = set()
    for k in range(REACHES):
        for t in range(quarter):
            shifts |= {(1 - k + 4 * t) % strips, (k - 1 - 4 * t) % strips}
    expected = jnp.int32(0)
    for shift in sorted(shifts | {0}):
        peer = wrap(s + shift)
        if quarter == 1 and shift:
            close = jnp.abs(peer - s) == 1
        else:
            close = peer >= 0
        near = angle_devs + depths - 1 - (1 if shift == 0 else 0)
        expected = expected + jnp.where(close, near, 0)

        @pl.when(close)
        def _():
            for step in range(angle_devs):
                if shift or step:
                    place = {"strip": peer, "angle": lax.rem(a + step, angle_devs)}
                    pl.semaphore_signal(barrier, 1, device_id=place, device_id_type=MESH)
            for step in range(1, depths):
                place = {"strip": peer, "depth": lax.rem(d + step, depths)}
                pl.semaphore_signal(barrier, 1, device_id=place, device_id_type=MESH)

    out[...] = jnp.zeros(out.shape, jnp.float32)
    for ref in (placed_local, placed_mine, placed_theirs):
        ref[...] = jnp.zeros(ref.shape, jnp.bfloat16)

    for copy in metas:
        copy.wait()
    pltpu.make_async_copy(film, film, load_sem.at[0]).wait()
    for copy in late:
        copy.start()

    def block(k, device):
        rows = ROWS[k] // depths
        return pl.ds(pl.multiple_of(device * rows, rows), rows)

    def mix_copy(k, q, step):
        target = lax.rem(d + step, depths)
        return rcopy(
            sent[k].at[q, block(k, target)],
            mix[k].at[q, step - 1],
            mix_send.at[kind(k), step - 1],
            mix_recv.at[kind(k), q, step - 1],
            depth=target,
        )

    def film_copy(k, q):
        return rcopy(
            parts[k].at[q],
            got[k].at[q % half, block(k, d)],
            film_send.at[kind(k)],
            film_recv.at[k, q % half],
            strip=wrap(s - k + 4 * (q % quarter) + 1),
            depth=q // half,
        )

    def own_copy(q):
        return rcopy(
            sent[1].at[q],
            own.at[d, q % half],
            own_send.at[q % half, seat(q // half)],
            own_recv.at[q % half, seat(d)],
            depth=q // half,
        )

    def exchange(k, q):
        for step in range(1, depths):
            mix_copy(k, q, step).start()

    def merge(k, q):
        value = sent[k][q, block(k, d)].astype(jnp.float32)
        for step in range(1, depths):
            mix_copy(k, q, step).wait_recv()
            value = value + mix[k][q, step - 1].astype(jnp.float32)
        parts[k][q] = value.astype(jnp.bfloat16)
        film_copy(k, q).start()

    def own_strip(k, q):
        return (1 - k + 4 * (q % quarter)) % strips == 0

    def project(k):
        home = s - k
        gap = differences(ROWS[k], WX)
        chosen = []
        for q in range(slots):
            offset = meta.pick(scan_x, home, q) - WX * k + BASES[k]
            angle = meta.pick(slot_angle, home, q)
            chosen.append(
                jnp.concatenate(
                    [one_hot(gap == offset + meta.shear(angle, z)) for z in range(layers)], axis=1
                )
            )
        flat = film[...].reshape(layers * WX, 2 * columns)
        tall = dot(jnp.concatenate(chosen, axis=0), flat)
        for q in range(slots):
            corner = meta.pick(scan_y, home, q)
            first = lanes(ROWS[k]) >= corner
            rows = tall[q * ROWS[k] : (q + 1) * ROWS[k]]
            wound = []
            for part in range(2):
                side = rows[:, part * columns : (part + 1) * columns]
                wound += [jnp.where(first, side[:, :margin], side[:, FRAME:]), side[:, margin:FRAME]]
            sent[k][q] = jnp.concatenate(wound, axis=1).astype(jnp.bfloat16)

    def reached(k):
        return (s - k >= 0) & (s - k <= strips - 3)

    for k in (0, 2):

        @pl.when(reached(k))
        def _():
            project(k)

    pl.semaphore_wait(barrier, expected)
    for k in (0, 2):

        @pl.when(reached(k))
        def _():
            for q in range(slots):
                exchange(k, q)


    def amp_copy(other):
        return rcopy(
            amplitude.at[other * half : (other + 1) * half],
            measured.at[d],
            amp_send.at[seat(other)],
            amp_recv.at[0],
            depth=other,
        )

    def amp_own(other):
        return pltpu.make_async_copy(
            amplitude.at[other * half : (other + 1) * half], measured.at[d], amp_recv.at[0]
        )

    tables = (
        (shear_in, shear_out, shears),
        (scan_y_in, scan_y_out, scans_y),
        (slot_angle_in, slot_angle_out, slot_angles),
        (owner_slot_in, owner_slot_out, owner_slots),
    )

    def meta_copies(step):
        return [
            rcopy(
                source,
                target.at[step],
                meta_send.at[step - 1, i],
                meta_recv.at[step - 1, i],
                angle=lax.rem(a + step, angle_devs),
            )
            for i, (source, target, _) in enumerate(tables)
        ]

    def meta_pulls(step):
        return [
            pltpu.make_async_copy(target.at[step], local.at[step], meta_pull.at[step - 1, i])
            for i, (_, target, local) in enumerate(tables)
        ]

    for step in range(1, angle_devs):
        for copy in meta_copies(step):
            copy.start()

    for other in range(depths):

        @pl.when(d != other)
        def _():
            amp_copy(other).start()

        @pl.when(d == other)
        def _():
            amp_own(other).start()

    for q in range(slots):
        for k in (0, 2):

            @pl.when(reached(k))
            def _():
                merge(k, q)


    @pl.when(reached(1))
    def _():
        project(1)
        for q in range(slots):
            if own_strip(1, q):

                @pl.when(d == q // half)
                def _():
                    own[d, q % half] = sent[1][q]

                @pl.when(d != q // half)
                def _():
                    own_copy(q).start()
            else:
                exchange(1, q)
        for q in range(slots):
            if not own_strip(1, q):
                merge(1, q)

    groups = [(meta, scan_y, slot_angle)]
    for step in range(1, angle_devs):
        lead = (step,)
        groups.append((Meta(shears, owner_slots, slots, lead), scans_y, slot_angles))

    def prepare(target, items):
        wanted = []
        for step, k, q, at in items:
            home = jnp.clip(s - k, 0, strips - 1)
            source, _, angles = groups[step]
            angle = source.pick(angles, home, q)
            base = jnp.where(reached(k), at + SHEAR, -4 * target.shape[1])
            wanted.append([base - source.shear(angle, z) for z in range(layers)])
        gap = differences(share, target.shape[1])
        for z in range(layers):
            mask = gap == wanted[0][z]
            for want in wanted[1:]:
                mask = mask | (gap == want[z])
            target[z * share : (z + 1) * share] = one_hot(mask)

    locals_ = [(0, 1, q, q * reach) for q in range(slots)]

    def items_of(depth):
        return [
            (step, k, depth * half + lane, (lane * len(batch) + rows_of[step, kind(k)]) * reach)
            for lane in range(half)
            for step in list(range(1, angle_devs)) + [0]
            for k in (1, 0, 2)
            if (step, k) != (0, 1)
        ]

    prepare(picks_local, locals_)

    for copy in late:
        copy.wait()
    pltpu.make_async_copy(measured, measured, amp_recv.at[0]).wait()


    def cut_copy(k, lane, quota, home, part):
        step = lax.rem(part - a + angle_devs, angle_devs)
        return rcopy(
            cuts.at[lane, k, part],
            windows.at[step, kind(k), quota],
            cut_send.at[k, lane],
            win_recv.at[step, kind(k), quota],
            strip=wrap(home + k),
            angle=part,
        )

    def owned(act):
        for lane in range(half):
            quota = d * half + lane
            home = wrap(s - 1 - 4 * lax.rem(quota, quarter))

            @pl.when(home <= strips - 3)
            def _():
                act(lane, quota, home, wrap(home + 1) == s)

    def work(lane, quota, home, local):
        def arrive(k):
            pltpu.make_async_copy(got[k].at[lane], got[k].at[lane], film_recv.at[k, lane]).wait()

        corner = meta.pick(scan_y, home, quota)
        gap = differences(FRAME, FRAME)
        turn = one_hot((gap == -corner) | (gap == FRAME - corner))
        back_turn = one_hot((gap == corner) | (gap == corner - FRAME))
        for part in range(2):
            at = slice(part * FRAME, (part + 1) * FRAME)
            probe_rot[lane, part] = dot(probe[part], back_turn).astype(jnp.bfloat16)
            dft_rot[lane, 0, at] = dot(turn, table[at]).astype(jnp.bfloat16)
            dft_rot[lane, 1, :, at] = dot(table_t[:, at], back_turn).astype(jnp.bfloat16)

        @pl.when(local)
        def _():
            value = own[d, lane].astype(jnp.float32)
            for step in range(1, depths):
                source = lax.rem(d + step, depths)
                rcopy(
                    sent[1].at[lane],
                    own.at[source, lane],
                    own_send.at[lane, seat(source)],
                    own_recv.at[lane, seat(source)],
                    depth=source,
                ).wait_recv()
                value = value + own[source, lane].astype(jnp.float32)
            got[1][lane] = value.astype(jnp.bfloat16)

        @pl.when(jnp.logical_not(local))
        def _():
            arrive(1)

        def forward(low, high, extra):
            rows = slice(low, high)
            whole = got1[lane, rows].astype(jnp.float32) + extra.astype(jnp.float32)
            re, im = whole[:, :FRAME], whole[:, FRAME:]
            probe_re = probe_rot[lane, 0, rows].astype(jnp.float32)
            probe_im = probe_rot[lane, 1, rows].astype(jnp.float32)
            exit_wave = jnp.concatenate(
                [probe_re * re - probe_im * im, probe_re * im + probe_im * re], axis=1
            ).astype(jnp.bfloat16)
            section = dot(exit_wave, dft_rot[lane, 0]).astype(jnp.bfloat16)
            left = jnp.concatenate(
                [table_t[:, rows], table_t[:, FRAME + low : FRAME + high]], axis=1
            )
            return dot(left, jnp.concatenate([section[:, :FRAME], section[:, FRAME:]], axis=0))

        arrive(0)
        spec[...] = forward(0, WX, got0[lane])
        arrive(2)
        spectrum = spec[...] + forward(WX, FRAME, got2[lane])
        spec_re, spec_im = spectrum[:FRAME], spectrum[FRAME:]
        magnitude = jnp.sqrt(spec_re * spec_re + spec_im * spec_im)
        levels = jnp.concatenate(
            [measured[source, lane] for source in range(depths)], axis=0
        ).astype(jnp.float32)
        live = meta.slot(home, quota) < counts[0, home]
        live = jnp.where(live, 1.0, 0.0).astype(jnp.float32)
        factor = (1.0 - levels / jnp.maximum(magnitude, 1.0)) * live
        residual = jnp.concatenate([spec_re * factor, spec_im * factor], axis=1).astype(
            jnp.bfloat16
        )
        inverse = dot(residual, dft_rot[lane, 1]).astype(jnp.bfloat16)
        stacked = jnp.concatenate([inverse[:, :FRAME], inverse[:, FRAME:]], axis=0)
        offset = meta.pick(scan_x, home, quota)

        def backward(low, high):
            rows = slice(low, high)
            left = jnp.concatenate([table[rows], table[FRAME + low : FRAME + high]], axis=0)
            wave = dot(left, stacked)
            re, im = wave[: high - low], wave[high - low :]
            probe_re = probe_rot[lane, 0, rows].astype(jnp.float32)
            probe_im = probe_rot[lane, 1, rows].astype(jnp.float32)
            return jnp.concatenate(
                [probe_re * re + probe_im * im, probe_re * im - probe_im * re], axis=1
            ).astype(jnp.bfloat16)

        def cut(k, part, low, value):
            gap = differences(reach, value.shape[0])
            first = WX * k - offset + part * share - SHEAR - low
            cuts[lane, k, part] = dot(one_hot(gap == first), value).astype(jnp.bfloat16)

        def send(k, low, value):
            for part in range(angle_devs):
                cut(k, part, low, value)
                copy = cut_copy(k, lane, quota, home, part)
                if k == 1:

                    @pl.when(jnp.logical_not(local & (a == part)))
                    def _():
                        copy.start()
                else:
                    copy.start()

        top = backward(0, WX)
        back[0:WX] = top
        send(0, 0, top)
        bottom = backward(WX, FRAME)
        back[WX:FRAME] = bottom
        send(1, 0, back[...])
        send(2, WX, bottom)

        @pl.when(local)
        def _():
            windows[0, kind(1), quota] = cuts[lane, 1, a]


    owned(work)

    for step in range(1, angle_devs):
        for copy in meta_copies(step):
            copy.wait_recv()
        for copy in meta_pulls(step):
            copy.start()
    for step in range(1, angle_devs):
        for copy in meta_pulls(step):
            copy.wait()
    mine = items_of(d)
    theirs = [items_of(lax.rem(d + step, depths)) for step in range(1, depths)]
    prepare(picks_mine, mine)
    for step in range(1, depths):
        prepare(picks_theirs.at[step - 1], theirs[step - 1])


    def pass_copy(step, k, q, other):
        return rcopy(
            windows.at[step, kind(k), q],
            windows.at[step, kind(k), q],
            pass_send.at[kind(k), seat(other)],
            win_recv.at[step, kind(k), q],
            depth=other,
        )

    def recv(step, k, q):
        window = windows.at[step, kind(k), q]
        pltpu.make_async_copy(window, window, win_recv.at[step, kind(k), q]).wait()

    def relay(step, k):
        for q in range(slots):

            @pl.when(d == q // half)
            def _():
                if not (step == 0 and own_strip(k, q)):
                    recv(step, k, q)
                for other in range(depths):
                    if other != q // half:
                        pass_copy(step, k, q, other).start()

    def place(target, step, k, q, at):
        source, corners, _ = groups[step]
        first = lanes(reach) >= source.pick(corners, s - k, q)
        window = windows.at[step, kind(k), q]
        rows = slice(at, at + reach)
        for part in range(2):
            head = window[:, part * FRAME : part * FRAME + margin].astype(jnp.float32)
            left = part * columns
            target[rows, left : left + margin] = jnp.where(first, head, 0.0).astype(jnp.bfloat16)
            target[rows, left + margin : left + FRAME] = window[
                :, part * FRAME + margin : (part + 1) * FRAME
            ]
            target[rows, left + FRAME : left + columns] = jnp.where(first, 0.0, head).astype(
                jnp.bfloat16
            )

    def add(chosen, target):
        value = dot(chosen[...], target[...]) * scaling
        for z in range(layers):
            for part in range(2):
                out[z, part] += value[
                    z * share : (z + 1) * share, part * columns : (part + 1) * columns
                ]

    @pl.when(reached(1))
    def _():
        relay(0, 1)
        for q in range(slots):

            @pl.when(d != q // half)
            def _():
                pass_copy(0, 1, q, q // half).wait_recv()

        for item in locals_:
            place(placed_local, *item)
        add(picks_local, placed_local)

    for step, k in [(step, k) for step in list(range(1, angle_devs)) + [0] for k in (1, 0, 2)]:
        if (step, k) != (0, 1):

            @pl.when(reached(k))
            def _():
                relay(step, k)
                for item in mine:
                    if item[:2] == (step, k):
                        place(placed_mine, *item)

    add(picks_mine, placed_mine)
    for i in range(1, depths):
        for step, k, q, at in theirs[i - 1]:

            @pl.when(reached(k))
            def _():
                recv(step, k, q)
                place(placed_theirs.at[i - 1], step, k, q, at)

        add(picks_theirs.at[i - 1], placed_theirs.at[i - 1])

    for other in range(depths):

        @pl.when(d != other)
        def _():
            amp_copy(other).wait_send()

    for step in range(1, angle_devs):
        for copy in meta_copies(step):
            copy.wait_send()
    for k in range(REACHES):

        @pl.when(reached(k))
        def _():
            for q in range(slots):
                if own_strip(k, q):

                    @pl.when(d != q // half)
                    def _():
                        own_copy(q).wait_send()
            rest = [q for q in range(slots) if not own_strip(k, q)]
            if rest:
                whole = parts[k].at[slots - len(rest) :]
                pltpu.make_async_copy(whole, whole, film_send.at[kind(k)]).wait()
                for step in range(1, depths):
                    pltpu.make_async_copy(whole, whole, mix_send.at[kind(k), step - 1]).wait()

    def drain(lane, quota, home, local):
        for k in range(REACHES):
            whole = cuts.at[lane, k]
            if k == 1:
                most = cuts.at[lane, k, 1:]

                @pl.when(local)
                def _():
                    pltpu.make_async_copy(most, most, cut_send.at[k, lane]).wait()

                @pl.when(jnp.logical_not(local))
                def _():
                    pltpu.make_async_copy(whole, whole, cut_send.at[k, lane]).wait()
            else:
                pltpu.make_async_copy(whole, whole, cut_send.at[k, lane]).wait()

    owned(drain)

    for k in range(REACHES):

        @pl.when(reached(k))
        def _():
            for other in range(depths):

                @pl.when(d != other)
                def _():
                    whole = windows.at[:, kind(k), 0:half]
                    pltpu.make_async_copy(whole, whole, pass_send.at[kind(k), seat(other)]).wait()


def body(sizes_of, crystal, probe, amplitude, shear, scan_x, scan_y, slot_angle, owner_slot, counts):
    strips, angle_devs, depths = sizes_of
    layers, _, _, columns = crystal.shape
    slots = owner_slot.shape[2]
    half = slots // depths
    share = WX // angle_devs
    reach = share + SHEAR
    kinds = bands(strips)
    seats = 1 if depths == 2 else depths
    local_rows = -(-(slots * reach) // 128) * 128
    batch_rows = -(-(half * len(batch_of(strips, angle_devs)) * reach) // 128) * 128
    dft = dft_tables()
    bf16 = jnp.bfloat16
    scan_x, scan_y, slot_angle, owner_slot = [
        jnp.swapaxes(value, 1, 2) for value in (scan_x, scan_y, slot_angle, owner_slot)
    ]
    sizes = (strips, angle_devs, depths, layers, slots, columns)
    tables = (shear, scan_y, slot_angle, owner_slot)
    hbm = pl.BlockSpec(memory_space=pltpu.HBM)
    vmem = pl.BlockSpec(memory_space=pltpu.VMEM)
    dma = pltpu.SemaphoreType.DMA
    small = (shear, scan_x, scan_y, slot_angle, owner_slot, counts)
    scratch = [pltpu.SMEM(x.shape, jnp.int32) for x in small]
    scratch += [pltpu.SMEM((angle_devs,) + x.shape, jnp.int32) for x in tables]
    scratch += [
        pltpu.VMEM((layers, WX, 2 * columns), bf16),
        pltpu.VMEM(probe.shape, bf16),
        pltpu.VMEM(dft.shape, bf16),
    ]
    scratch += [pltpu.VMEM((slots, rows, 2 * FRAME), bf16) for rows in ROWS]
    scratch += [pltpu.VMEM((half, rows, 2 * FRAME), bf16) for rows in ROWS]
    scratch += [pltpu.VMEM((slots, depths - 1, rows // depths, 2 * FRAME), bf16) for rows in ROWS]
    scratch += [pltpu.VMEM((slots, rows // depths, 2 * FRAME), bf16) for rows in ROWS]
    scratch += [pltpu.VMEM((depths, half, FRAME, 2 * FRAME), bf16)]
    scratch += [
        pltpu.VMEM((depths, half, FRAME // depths, FRAME), bf16),
        pltpu.VMEM((half, REACHES, angle_devs, reach, 2 * FRAME), bf16),
        pltpu.VMEM((angle_devs, kinds, slots, reach, 2 * FRAME), bf16),
        pltpu.VMEM((half,) + dft.shape, bf16),
        pltpu.VMEM((half,) + probe.shape, bf16),
        pltpu.VMEM((layers * share, local_rows), bf16),
        pltpu.VMEM((layers * share, batch_rows), bf16),
        pltpu.VMEM((depths - 1, layers * share, batch_rows), bf16),
        pltpu.VMEM((local_rows, 2 * columns), bf16),
        pltpu.VMEM((batch_rows, 2 * columns), bf16),
        pltpu.VMEM((depths - 1, batch_rows, 2 * columns), bf16),
        pltpu.VMEM((2 * FRAME, FRAME), jnp.float32),
        pltpu.VMEM((FRAME, 2 * FRAME), bf16),
        dma((3,)),
        dma((kinds,)),
        dma((REACHES, half)),
        dma((kinds, depths - 1)),
        dma((kinds, slots, depths - 1)),
        dma((half, seats)),
        dma((half, seats)),
        dma((seats,)),
        dma((1,)),
        dma((len(small),)),
        dma((angle_devs - 1, len(tables))),
        dma((angle_devs - 1, len(tables))),
        dma((angle_devs - 1, len(tables))),
        dma((REACHES, half)),
        dma((kinds, seats)),
        dma((angle_devs, kinds, slots)),
    ]
    scaling = 1.0 / (shear.shape[0] * angle_devs)
    result, *_ = pl.pallas_call(
        functools.partial(kernel, sizes, scaling),
        out_shape=(jax.ShapeDtypeStruct((layers, 2, share, columns), jnp.float32),)
        + tuple(jax.ShapeDtypeStruct((angle_devs,) + x.shape, jnp.int32) for x in tables),
        in_specs=[hbm] * 10,
        out_specs=(vmem,) + (hbm,) * 4,
        scratch_shapes=scratch,
        compiler_params=pltpu.CompilerParams(
            collective_id=0, has_side_effects=True, vmem_limit_bytes=VMEM_LIMIT
        ),
    )(
        *(
            pltpu.with_memory_space_constraint(x, pltpu.HBM)
            for x in (crystal, probe, amplitude, dft, *small)
        )
    )
    return result


def solution(mesh):
    placed = (
        P(("groups", "depth"), None, "strip", None),
        P(),
        P("angle", ("groups", "strip", "depth"), None),
        P(("groups", "angle"), "depth"),
        P(("groups", "angle"), None, None),
        P(("groups", "angle"), None, None),
        P(("groups", "angle"), None, None),
        P(("groups", "angle"), None, None),
        P(("groups", "angle"), None),
    )
    sizes_of = (mesh.shape["strip"], mesh.shape["angle"], mesh.shape["depth"])
    return jax.shard_map(
        functools.partial(body, sizes_of),
        mesh=mesh,
        in_specs=placed,
        out_specs=P(("groups", "depth"), None, ("strip", "angle"), None),
        check_vma=False,
    )
```

```python
import functools

import jax
import jax.numpy as jnp
import numpy as np
from jax import lax
from jax.experimental import pallas as pl
from jax.experimental.pallas import tpu as pltpu
from jax.sharding import PartitionSpec as P

FRAME = 256
WX = 128
SHEAR = 16
REACHES = 3
ROWS = (WX, FRAME, FRAME - WX)
BASES = (0, 0, WX)
VMEM_LIMIT = 44 * 2**20
MESH = pl.DeviceIdType.MESH


def dft_tables():
    index_row = np.arange(FRAME)
    phase = (index_row[:, None] * index_row[None, :] % FRAME) * (2.0 * np.pi / FRAME)
    real = np.cos(phase) / np.sqrt(FRAME)
    imag = -np.sin(phase) / np.sqrt(FRAME)
    table = np.block([[real, imag], [-imag, real]]).astype(np.float32)
    return jnp.asarray(np.stack([table, table.T]), jnp.bfloat16)


def dot(left, right):
    return jnp.dot(left, right, preferred_element_type=jnp.float32)


def differences(rows, columns):
    shape = (rows, columns)
    return lax.broadcasted_iota(jnp.int32, shape, 1) - lax.broadcasted_iota(jnp.int32, shape, 0)


def one_hot(mask):
    return jnp.where(mask, 1.0, 0.0).astype(jnp.bfloat16)


class Meta:
    def __init__(self, lifts, owner_slot, slots, lead):
        self.lifts, self.owner_slot = lifts, owner_slot
        self.slots, self.lead = slots, lead

    def shear(self, angle, z):
        return self.lifts[self.lead + (angle, z)]

    def pick(self, ref, home, quota):
        value = jnp.int32(0)
        for m in range(self.slots):
            at = self.lead + (0, m, home)
            value = value + jnp.where(self.owner_slot[at] == quota, ref[at], 0)
        return value

    def slot(self, home, quota):
        value = jnp.int32(0)
        for m in range(self.slots):
            at = self.lead + (0, m, home)
            value = value + jnp.where(self.owner_slot[at] == quota, m, 0)
        return value


def bands(strips):
    return REACHES if strips - 3 >= 2 else 2


def batch_of(strips, angle_devs):
    every = [(step, k) for step in range(angle_devs) for k in range(bands(strips))]
    return [item for item in every if item != (0, 1)]


def kernel(
    sizes,
    scaling,
    crystal,
    probe_in,
    amplitude,
    tables_in,
    shear_in,
    scan_x_in,
    scan_y_in,
    slot_angle_in,
    owner_slot_in,
    counts_in,
    out,
    shear_out,
    items_out,
    shear,
    items,
    counts,
    shears,
    others,
    film,
    probe,
    dft,
    sent0,
    sent1,
    sent2,
    got0,
    got1,
    got2,
    mix0,
    mix1,
    mix2,
    part0,
    part1,
    part2,
    own,
    measured,
    cuts,
    windows,
    dft_rot,
    probe_rot,
    picks_local,
    picks_mine,
    picks_theirs,
    placed_local,
    placed_mine,
    placed_theirs,
    spec,
    back,
    load_sem,
    film_send,
    film_recv,
    mix_send,
    mix_recv,
    own_send,
    own_recv,
    amp_send,
    amp_recv,
    meta_load,
    meta_send,
    meta_recv,
    meta_pull,
    cut_send,
    pass_send,
    win_recv,
):
    strips, angle_devs, depths, layers, slots, columns = sizes
    quarter = strips // 4
    half = slots // depths
    share = WX // angle_devs
    reach = share + SHEAR
    sent = (sent0, sent1, sent2)
    got = (got0, got1, got2)
    mix = (mix0, mix1, mix2)
    parts = (part0, part1, part2)
    s = lax.axis_index("strip")
    a = lax.axis_index("angle")
    d = lax.axis_index("depth")
    scan_x, owner_slot, scan_y, slot_angle = [items.at[i] for i in range(4)]
    meta = Meta(shear, owner_slot, slots, ())
    margin = columns - FRAME
    kinds = bands(strips)
    batch = batch_of(strips, angle_devs)
    rows_of = dict(zip(batch, range(len(batch))))

    def kind(k):
        return k % kinds

    def seat(device):
        return 0 if depths == 2 else device


    def lanes(rows):
        return lax.broadcasted_iota(jnp.int32, (rows, margin), 1)

    def rcopy(source, target, send_sem, recv_sem, **where):
        return pltpu.make_async_remote_copy(
            source, target, send_sem, recv_sem, device_id=where, device_id_type=MESH
        )

    def wrap(strip):
        return lax.rem(strip + 4 * strips, strips)

    same = (scan_x_in, owner_slot_in, scan_y_in, slot_angle_in)
    metas = [
        pltpu.make_async_copy(shear_in, shear, meta_load.at[0]),
        pltpu.make_async_copy(counts_in, counts, meta_load.at[1]),
    ]
    several = [pltpu.make_async_copy(x, items.at[i], meta_load.at[2]) for i, x in enumerate(same)]
    loads = [
        pltpu.make_async_copy(
            crystal.at[:, part],
            film.at[:, :, part * columns : (part + 1) * columns],
            load_sem.at[0],
        )
        for part in range(2)
    ]
    late = [
        pltpu.make_async_copy(source, target, load_sem.at[1 + i])
        for i, (source, target) in enumerate(((probe_in, probe), (tables_in, dft)))
    ]
    table, table_t = dft.at[0], dft.at[1]
    for copy in metas + several + loads:
        copy.start()

    blank = jnp.zeros(windows.shape[:3] + (SHEAR, 2 * FRAME), jnp.bfloat16)
    windows[:, :, :, 0:SHEAR] = blank
    windows[:, :, :, share:reach] = blank

    barrier = pltpu.get_barrier_semaphore()
    shifts = set()
    for k in range(REACHES):
        for t in range(quarter):
            shifts |= {(1 - k + 4 * t) % strips, (k - 1 - 4 * t) % strips}
    expected = jnp.int32(0)
    for shift in sorted(shifts | {0}):
        peer = wrap(s + shift)
        if quarter == 1 and shift:
            close = jnp.abs(peer - s) == 1
        else:
            close = peer >= 0
        near = angle_devs + depths - 1 - (1 if shift == 0 else 0)
        expected = expected + jnp.where(close, near, 0)

        @pl.when(close)
        def _():
            for step in range(angle_devs):
                if shift or step:
                    place = {"strip": peer, "angle": lax.rem(a + step, angle_devs)}
                    pl.semaphore_signal(barrier, 1, device_id=place, device_id_type=MESH)
            for step in range(1, depths):
                place = {"strip": peer, "depth": lax.rem(d + step, depths)}
                pl.semaphore_signal(barrier, 1, device_id=place, device_id_type=MESH)

    out[...] = jnp.zeros(out.shape, jnp.float32)
    for ref in (placed_local, placed_mine, placed_theirs):
        ref[...] = jnp.zeros(ref.shape, jnp.bfloat16)

    for copy in metas:
        copy.wait()
    pltpu.make_async_copy(items, items, meta_load.at[2]).wait()
    pltpu.make_async_copy(film, film, load_sem.at[0]).wait()
    for copy in late:
        copy.start()

    def block(k, device):
        rows = ROWS[k] // depths
        return pl.ds(pl.multiple_of(device * rows, rows), rows)

    def mix_copy(k, q, step):
        target = lax.rem(d + step, depths)
        return rcopy(
            sent[k].at[q, block(k, target)],
            mix[k].at[q, step - 1],
            mix_send.at[kind(k), step - 1],
            mix_recv.at[kind(k), q, step - 1],
            depth=target,
        )

    def film_copy(k, q):
        return rcopy(
            parts[k].at[q],
            got[k].at[q % half, block(k, d)],
            film_send.at[kind(k)],
            film_recv.at[k, q % half],
            strip=wrap(s - k + 4 * (q % quarter) + 1),
            depth=q // half,
        )

    def own_copy(q):
        return rcopy(
            sent[1].at[q],
            own.at[d, q % half],
            own_send.at[q % half, seat(q // half)],
            own_recv.at[q % half, seat(d)],
            depth=q // half,
        )

    def exchange(k, q):
        for step in range(1, depths):
            mix_copy(k, q, step).start()

    def merge(k, q):
        value = sent[k][q, block(k, d)].astype(jnp.float32)
        for step in range(1, depths):
            mix_copy(k, q, step).wait_recv()
            value = value + mix[k][q, step - 1].astype(jnp.float32)
        parts[k][q] = value.astype(jnp.bfloat16)
        film_copy(k, q).start()

    def own_strip(k, q):
        return (1 - k + 4 * (q % quarter)) % strips == 0

    def project(k):
        home = s - k
        gap = differences(ROWS[k], WX)
        chosen = []
        for q in range(slots):
            offset = meta.pick(scan_x, home, q) - WX * k + BASES[k]
            angle = meta.pick(slot_angle, home, q)
            chosen.append(
                jnp.concatenate(
                    [one_hot(gap == offset + meta.shear(angle, z)) for z in range(layers)], axis=1
                )
            )
        flat = film[...].reshape(layers * WX, 2 * columns)
        tall = dot(jnp.concatenate(chosen, axis=0), flat)
        for q in range(slots):
            corner = meta.pick(scan_y, home, q)
            first = lanes(ROWS[k]) >= corner
            rows = tall[q * ROWS[k] : (q + 1) * ROWS[k]]
            wound = []
            for part in range(2):
                side = rows[:, part * columns : (part + 1) * columns]
                wound += [jnp.where(first, side[:, :margin], side[:, FRAME:]), side[:, margin:FRAME]]
            sent[k][q] = jnp.concatenate(wound, axis=1).astype(jnp.bfloat16)

    def reached(k):
        return (s - k >= 0) & (s - k <= strips - 3)

    for k in (0, 2):

        @pl.when(reached(k))
        def _():
            project(k)

    pl.semaphore_wait(barrier, expected)
    for k in (0, 2):

        @pl.when(reached(k))
        def _():
            for q in range(slots):
                exchange(k, q)


    def amp_copy(other):
        return rcopy(
            amplitude.at[other * half : (other + 1) * half],
            measured.at[d],
            amp_send.at[seat(other)],
            amp_recv.at[0],
            depth=other,
        )

    def amp_own(other):
        return pltpu.make_async_copy(
            amplitude.at[other * half : (other + 1) * half], measured.at[d], amp_recv.at[0]
        )

    def meta_copies(step):
        def send(source, target, i):
            return rcopy(
                source,
                target,
                meta_send.at[step - 1, i],
                meta_recv.at[step - 1, i],
                angle=lax.rem(a + step, angle_devs),
            )

        first = [send(shear_in, shear_out.at[step], 0)]
        return first + [send(x, items_out.at[step, i], 1) for i, x in enumerate(same[1:])]

    def meta_waits(step, sem):
        for i, ref in enumerate((shear_out.at[step], items_out.at[step])):
            pltpu.make_async_copy(ref, ref, sem.at[step - 1, i]).wait()

    def meta_pulls(step):
        return [
            pltpu.make_async_copy(shear_out.at[step], shears.at[step], meta_pull.at[step - 1, 0]),
            pltpu.make_async_copy(items_out.at[step], others.at[step], meta_pull.at[step - 1, 1]),
        ]

    for step in range(1, angle_devs):
        for copy in meta_copies(step):
            copy.start()

    for other in range(depths):

        @pl.when(d != other)
        def _():
            amp_copy(other).start()

        @pl.when(d == other)
        def _():
            amp_own(other).start()

    for q in range(slots):
        for k in (0, 2):

            @pl.when(reached(k))
            def _():
                merge(k, q)


    @pl.when(reached(1))
    def _():
        project(1)
        for q in range(slots):
            if own_strip(1, q):

                @pl.when(d == q // half)
                def _():
                    own[d, q % half] = sent[1][q]

                @pl.when(d != q // half)
                def _():
                    own_copy(q).start()
            else:
                exchange(1, q)
        for q in range(slots):
            if not own_strip(1, q):
                merge(1, q)

    groups = [(meta, scan_y, slot_angle)]
    for step in range(1, angle_devs):
        owner_slots, scans_y, slot_angles = [others.at[step, i] for i in range(3)]
        groups.append((Meta(shears.at[step], owner_slots, slots, ()), scans_y, slot_angles))

    def prepare(target, items):
        wanted = []
        for step, k, q, at in items:
            home = jnp.clip(s - k, 0, strips - 1)
            source, _, angles = groups[step]
            angle = source.pick(angles, home, q)
            base = jnp.where(reached(k), at + SHEAR, -4 * target.shape[1])
            wanted.append([base - source.shear(angle, z) for z in range(layers)])
        gap = differences(share, target.shape[1])
        for z in range(layers):
            mask = gap == wanted[0][z]
            for want in wanted[1:]:
                mask = mask | (gap == want[z])
            target[z * share : (z + 1) * share] = one_hot(mask)

    locals_ = [(0, 1, q, q * reach) for q in range(slots)]

    def items_of(depth):
        return [
            (step, k, depth * half + lane, (lane * len(batch) + rows_of[step, kind(k)]) * reach)
            for lane in range(half)
            for step in list(range(1, angle_devs)) + [0]
            for k in (1, 0, 2)
            if (step, k) != (0, 1)
        ]

    prepare(picks_local, locals_)

    for copy in late:
        copy.wait()
    pltpu.make_async_copy(measured, measured, amp_recv.at[0]).wait()


    def edge(k, part):
        return (k == 0 and part == 0) or (k == 2 and part == angle_devs - 1)

    def filled(k, narrow):
        low = SHEAR if narrow and k == 0 else 0
        return slice(low, low + (share if narrow else reach))

    def cut_copy(k, lane, quota, home, part):
        step = lax.rem(part - a + angle_devs, angle_devs)
        narrow = edge(k, part)
        return rcopy(
            cuts.at[lane, k, part, filled(k, narrow)],
            windows.at[step, kind(k), quota, filled(k, narrow)],
            cut_send.at[REACHES + k // 2 if narrow else k, lane],
            win_recv.at[step, kind(k), quota],
            strip=wrap(home + k),
            angle=part,
        )

    def owned(act):
        for lane in range(half):
            quota = d * half + lane
            home = wrap(s - 1 - 4 * lax.rem(quota, quarter))

            @pl.when(home <= strips - 3)
            def _():
                act(lane, quota, home, wrap(home + 1) == s)

    def work(lane, quota, home, local):
        def arrive(k):
            pltpu.make_async_copy(got[k].at[lane], got[k].at[lane], film_recv.at[k, lane]).wait()

        corner = meta.pick(scan_y, home, quota)
        gap = differences(FRAME, FRAME)
        turn = one_hot((gap == -corner) | (gap == FRAME - corner))
        back_turn = one_hot((gap == corner) | (gap == corner - FRAME))
        for part in range(2):
            at = slice(part * FRAME, (part + 1) * FRAME)
            probe_rot[lane, part] = dot(probe[part], back_turn).astype(jnp.bfloat16)
            dft_rot[lane, 0, at] = dot(turn, table[at]).astype(jnp.bfloat16)
            dft_rot[lane, 1, :, at] = dot(table_t[:, at], back_turn).astype(jnp.bfloat16)

        @pl.when(local)
        def _():
            value = own[d, lane].astype(jnp.float32)
            for step in range(1, depths):
                source = lax.rem(d + step, depths)
                rcopy(
                    sent[1].at[lane],
                    own.at[source, lane],
                    own_send.at[lane, seat(source)],
                    own_recv.at[lane, seat(source)],
                    depth=source,
                ).wait_recv()
                value = value + own[source, lane].astype(jnp.float32)
            got[1][lane] = value.astype(jnp.bfloat16)

        @pl.when(jnp.logical_not(local))
        def _():
            arrive(1)

        def forward(low, high, extra):
            rows = slice(low, high)
            whole = got1[lane, rows].astype(jnp.float32) + extra.astype(jnp.float32)
            re, im = whole[:, :FRAME], whole[:, FRAME:]
            probe_re = probe_rot[lane, 0, rows].astype(jnp.float32)
            probe_im = probe_rot[lane, 1, rows].astype(jnp.float32)
            exit_wave = jnp.concatenate(
                [probe_re * re - probe_im * im, probe_re * im + probe_im * re], axis=1
            ).astype(jnp.bfloat16)
            section = dot(exit_wave, dft_rot[lane, 0]).astype(jnp.bfloat16)
            left = jnp.concatenate(
                [table_t[:, rows], table_t[:, FRAME + low : FRAME + high]], axis=1
            )
            return dot(left, jnp.concatenate([section[:, :FRAME], section[:, FRAME:]], axis=0))

        arrive(0)
        spec[...] = forward(0, WX, got0[lane])
        arrive(2)
        spectrum = spec[...] + forward(WX, FRAME, got2[lane])
        spec_re, spec_im = spectrum[:FRAME], spectrum[FRAME:]
        power = spec_re * spec_re + spec_im * spec_im
        levels = jnp.concatenate(
            [measured[source, lane] for source in range(depths)], axis=0
        ).astype(jnp.float32)
        live = meta.slot(home, quota) < counts[0, home]
        live = jnp.where(live, 1.0, 0.0).astype(jnp.float32)
        factor = (1.0 - levels * lax.rsqrt(jnp.maximum(power, 1.0))) * live
        residual = jnp.concatenate([spec_re * factor, spec_im * factor], axis=1).astype(
            jnp.bfloat16
        )
        inverse = dot(residual, dft_rot[lane, 1]).astype(jnp.bfloat16)
        stacked = jnp.concatenate([inverse[:, :FRAME], inverse[:, FRAME:]], axis=0)
        offset = meta.pick(scan_x, home, quota)

        def backward(low, high):
            rows = slice(low, high)
            left = jnp.concatenate([table[rows], table[FRAME + low : FRAME + high]], axis=0)
            wave = dot(left, stacked)
            re, im = wave[: high - low], wave[high - low :]
            probe_re = probe_rot[lane, 0, rows].astype(jnp.float32)
            probe_im = probe_rot[lane, 1, rows].astype(jnp.float32)
            return jnp.concatenate(
                [probe_re * re + probe_im * im, probe_re * im - probe_im * re], axis=1
            ).astype(jnp.bfloat16)

        def cut(k, part, low, value):
            gap = differences(reach, value.shape[0])
            first = WX * k - offset + part * share - SHEAR - low
            cuts[lane, k, part] = dot(one_hot(gap == first), value).astype(jnp.bfloat16)

        def send(k, low, value):
            for part in range(angle_devs):
                cut(k, part, low, value)
                copy = cut_copy(k, lane, quota, home, part)
                if k == 1:

                    @pl.when(jnp.logical_not(local & (a == part)))
                    def _():
                        copy.start()
                else:
                    copy.start()

        top = backward(0, WX)
        back[0:WX] = top
        send(0, 0, top)
        bottom = backward(WX, FRAME)
        back[WX:FRAME] = bottom
        send(1, 0, back[...])
        send(2, WX, bottom)

        @pl.when(local)
        def _():
            windows[0, kind(1), quota] = cuts[lane, 1, a]


    owned(work)

    for step in range(1, angle_devs):
        meta_waits(step, meta_recv)
        for copy in meta_pulls(step):
            copy.start()
    for step in range(1, angle_devs):
        for copy in meta_pulls(step):
            copy.wait()
    mine = items_of(d)
    theirs = [items_of(lax.rem(d + step, depths)) for step in range(1, depths)]
    prepare(picks_mine, mine)
    for step in range(1, depths):
        prepare(picks_theirs.at[step - 1], theirs[step - 1])


    def sized(k, act):
        if k == 1:
            act(filled(k, False))
        else:
            narrow = a == (0 if k == 0 else angle_devs - 1)

            @pl.when(narrow)
            def _():
                act(filled(k, True))

            @pl.when(jnp.logical_not(narrow))
            def _():
                act(filled(k, False))

    def recv(step, k, q):
        def act(rows):
            window = windows.at[step, kind(k), q, rows]
            pltpu.make_async_copy(window, window, win_recv.at[step, kind(k), q]).wait()

        sized(k, act)

    def relay(step, k):
        for q in range(slots):

            @pl.when(d == q // half)
            def _():
                def act(rows):
                    window = windows.at[step, kind(k), q, rows]
                    if not (step == 0 and own_strip(k, q)):
                        pltpu.make_async_copy(window, window, win_recv.at[step, kind(k), q]).wait()
                    for other in range(depths):
                        if other != q // half:
                            rcopy(
                                window,
                                window,
                                pass_send.at[kind(k), seat(other)],
                                win_recv.at[step, kind(k), q],
                                depth=other,
                            ).start()

                sized(k, act)

    def place(target, step, k, q, at):
        source, corners, _ = groups[step]
        first = lanes(reach) >= source.pick(corners, s - k, q)
        window = windows.at[step, kind(k), q]
        rows = slice(at, at + reach)
        for part in range(2):
            head = window[:, part * FRAME : part * FRAME + margin].astype(jnp.float32)
            left = part * columns
            target[rows, left : left + margin] = jnp.where(first, head, 0.0).astype(jnp.bfloat16)
            target[rows, left + margin : left + FRAME] = window[
                :, part * FRAME + margin : (part + 1) * FRAME
            ]
            target[rows, left + FRAME : left + columns] = jnp.where(first, 0.0, head).astype(
                jnp.bfloat16
            )

    def add(chosen, target):
        value = dot(chosen[...], target[...]) * scaling
        for z in range(layers):
            for part in range(2):
                out[z, part] += value[
                    z * share : (z + 1) * share, part * columns : (part + 1) * columns
                ]

    @pl.when(reached(1))
    def _():
        relay(0, 1)
        for q in range(slots):

            @pl.when(d != q // half)
            def _():
                recv(0, 1, q)

        for item in locals_:
            place(placed_local, *item)
        add(picks_local, placed_local)

    for step, k in [(step, k) for step in list(range(1, angle_devs)) + [0] for k in (1, 0, 2)]:
        if (step, k) != (0, 1):

            @pl.when(reached(k))
            def _():
                relay(step, k)
                for item in mine:
                    if item[:2] == (step, k):
                        place(placed_mine, *item)

    add(picks_mine, placed_mine)
    for i in range(1, depths):
        for step, k, q, at in theirs[i - 1]:

            @pl.when(reached(k))
            def _():
                recv(step, k, q)
                place(placed_theirs.at[i - 1], step, k, q, at)

        add(picks_theirs.at[i - 1], placed_theirs.at[i - 1])

    for other in range(depths):

        @pl.when(d != other)
        def _():
            amp_copy(other).wait_send()

    for step in range(1, angle_devs):
        meta_waits(step, meta_send)
    for k in range(REACHES):

        @pl.when(reached(k))
        def _():
            for q in range(slots):
                if own_strip(k, q):

                    @pl.when(d != q // half)
                    def _():
                        own_copy(q).wait_send()
            rest = [q for q in range(slots) if not own_strip(k, q)]
            if rest:
                whole = parts[k].at[slots - len(rest) :]
                pltpu.make_async_copy(whole, whole, film_send.at[kind(k)]).wait()
                for step in range(1, depths):
                    pltpu.make_async_copy(whole, whole, mix_send.at[kind(k), step - 1]).wait()

    def drain(lane, quota, home, local):
        for k in range(REACHES):
            whole = cuts.at[lane, k]
            if k != 1:
                narrow = cuts.at[lane, k, 0, 0:share]
                pltpu.make_async_copy(narrow, narrow, cut_send.at[REACHES + k // 2, lane]).wait()
                if angle_devs > 1:
                    most = cuts.at[lane, k, 1:]
                    pltpu.make_async_copy(most, most, cut_send.at[k, lane]).wait()
            else:
                most = cuts.at[lane, k, 1:]

                @pl.when(local)
                def _():
                    pltpu.make_async_copy(most, most, cut_send.at[k, lane]).wait()

                @pl.when(jnp.logical_not(local))
                def _():
                    pltpu.make_async_copy(whole, whole, cut_send.at[k, lane]).wait()

    owned(drain)

    for k in range(REACHES):

        @pl.when(reached(k))
        def _():
            for other in range(depths):

                @pl.when(d != other)
                def _():
                    def act(rows):
                        whole = windows.at[:, kind(k), 0:half, rows]
                        pltpu.make_async_copy(
                            whole, whole, pass_send.at[kind(k), seat(other)]
                        ).wait()

                    sized(k, act)


def body(sizes_of, crystal, probe, amplitude, shear, scan_x, scan_y, slot_angle, owner_slot, counts):
    strips, angle_devs, depths = sizes_of
    layers, _, _, columns = crystal.shape
    slots = owner_slot.shape[2]
    half = slots // depths
    share = WX // angle_devs
    reach = share + SHEAR
    kinds = bands(strips)
    seats = 1 if depths == 2 else depths
    local_rows = -(-(slots * reach) // 128) * 128
    batch_rows = -(-(half * len(batch_of(strips, angle_devs)) * reach) // 128) * 128
    dft = dft_tables()
    bf16 = jnp.bfloat16
    scan_x, scan_y, slot_angle, owner_slot = [
        jnp.swapaxes(value, 1, 2) for value in (scan_x, scan_y, slot_angle, owner_slot)
    ]
    sizes = (strips, angle_devs, depths, layers, slots, columns)
    hbm = pl.BlockSpec(memory_space=pltpu.HBM)
    vmem = pl.BlockSpec(memory_space=pltpu.VMEM)
    dma = pltpu.SemaphoreType.DMA
    small = (shear, scan_x, scan_y, slot_angle, owner_slot, counts)
    gathered = ((angle_devs,) + shear.shape, (angle_devs, 3) + scan_x.shape)
    scratch = [pltpu.SMEM(x, jnp.int32) for x in (shear.shape, (4,) + scan_x.shape, counts.shape)]
    scratch += [pltpu.SMEM(x, jnp.int32) for x in gathered]
    scratch += [
        pltpu.VMEM((layers, WX, 2 * columns), bf16),
        pltpu.VMEM(probe.shape, bf16),
        pltpu.VMEM(dft.shape, bf16),
    ]
    scratch += [pltpu.VMEM((slots, rows, 2 * FRAME), bf16) for rows in ROWS]
    scratch += [pltpu.VMEM((half, rows, 2 * FRAME), bf16) for rows in ROWS]
    scratch += [pltpu.VMEM((slots, depths - 1, rows // depths, 2 * FRAME), bf16) for rows in ROWS]
    scratch += [pltpu.VMEM((slots, rows // depths, 2 * FRAME), bf16) for rows in ROWS]
    scratch += [pltpu.VMEM((depths, half, FRAME, 2 * FRAME), bf16)]
    scratch += [
        pltpu.VMEM((depths, half, FRAME // depths, FRAME), bf16),
        pltpu.VMEM((half, REACHES, angle_devs, reach, 2 * FRAME), bf16),
        pltpu.VMEM((angle_devs, kinds, slots, reach, 2 * FRAME), bf16),
        pltpu.VMEM((half,) + dft.shape, bf16),
        pltpu.VMEM((half,) + probe.shape, bf16),
        pltpu.VMEM((layers * share, local_rows), bf16),
        pltpu.VMEM((layers * share, batch_rows), bf16),
        pltpu.VMEM((depths - 1, layers * share, batch_rows), bf16),
        pltpu.VMEM((local_rows, 2 * columns), bf16),
        pltpu.VMEM((batch_rows, 2 * columns), bf16),
        pltpu.VMEM((depths - 1, batch_rows, 2 * columns), bf16),
        pltpu.VMEM((2 * FRAME, FRAME), jnp.float32),
        pltpu.VMEM((FRAME, 2 * FRAME), bf16),
        dma((3,)),
        dma((kinds,)),
        dma((REACHES, half)),
        dma((kinds, depths - 1)),
        dma((kinds, slots, depths - 1)),
        dma((half, seats)),
        dma((half, seats)),
        dma((seats,)),
        dma((1,)),
        dma((3,)),
        dma((angle_devs - 1, 2)),
        dma((angle_devs - 1, 2)),
        dma((angle_devs - 1, 2)),
        dma((REACHES + 2, half)),
        dma((kinds, seats)),
        dma((angle_devs, kinds, slots)),
    ]
    scaling = 1.0 / (shear.shape[0] * angle_devs)
    result, *_ = pl.pallas_call(
        functools.partial(kernel, sizes, scaling),
        out_shape=(jax.ShapeDtypeStruct((layers, 2, share, columns), jnp.float32),)
        + tuple(jax.ShapeDtypeStruct(x, jnp.int32) for x in gathered),
        in_specs=[hbm] * 10,
        out_specs=(vmem,) + (hbm,) * 2,
        scratch_shapes=scratch,
        compiler_params=pltpu.CompilerParams(
            collective_id=0, has_side_effects=True, vmem_limit_bytes=VMEM_LIMIT
        ),
    )(
        *(
            pltpu.with_memory_space_constraint(x, pltpu.HBM)
            for x in (crystal, probe, amplitude, dft, *small)
        )
    )
    return result


def solution(mesh):
    placed = (
        P(("groups", "depth"), None, "strip", None),
        P(),
        P("angle", ("groups", "strip", "depth"), None),
        P(("groups", "angle"), "depth"),
        P(("groups", "angle"), None, None),
        P(("groups", "angle"), None, None),
        P(("groups", "angle"), None, None),
        P(("groups", "angle"), None, None),
        P(("groups", "angle"), None),
    )
    sizes_of = (mesh.shape["strip"], mesh.shape["angle"], mesh.shape["depth"])
    return jax.shard_map(
        functools.partial(body, sizes_of),
        mesh=mesh,
        in_specs=placed,
        out_specs=P(("groups", "depth"), None, ("strip", "angle"), None),
        check_vma=False,
    )
```

```python
import functools

import jax
import jax.numpy as jnp
import numpy as np
from jax import lax
from jax.experimental import pallas as pl
from jax.experimental.pallas import tpu as pltpu
from jax.sharding import PartitionSpec as P

FRAME = 256
WX = 128
SHEAR = 16
REACHES = 3
ROWS = (WX, FRAME, FRAME - WX)
BASES = (0, 0, WX)
EARLY = 32
VMEM_LIMIT = 44 * 2**20
MESH = pl.DeviceIdType.MESH


def dft_tables():
    index_row = np.arange(FRAME)
    phase = (index_row[:, None] * index_row[None, :] % FRAME) * (2.0 * np.pi / FRAME)
    real = np.cos(phase) / np.sqrt(FRAME)
    imag = -np.sin(phase) / np.sqrt(FRAME)
    table = np.block([[real, imag], [-imag, real]]).astype(np.float32)
    return jnp.asarray(np.stack([table, table.T]), jnp.bfloat16)


def dot(left, right):
    return jnp.dot(left, right, preferred_element_type=jnp.float32)


def differences(rows, columns):
    shape = (rows, columns)
    return lax.broadcasted_iota(jnp.int32, shape, 1) - lax.broadcasted_iota(jnp.int32, shape, 0)


def one_hot(mask):
    return jnp.where(mask, 1.0, 0.0).astype(jnp.bfloat16)


class Meta:
    def __init__(self, lifts, owner_slot, slots, lead):
        self.lifts, self.owner_slot = lifts, owner_slot
        self.slots, self.lead = slots, lead

    def shear(self, angle, z):
        return self.lifts[self.lead + (angle, z)]

    def pick(self, ref, home, quota):
        value = jnp.int32(0)
        for m in range(self.slots):
            at = self.lead + (0, m, home)
            value = value + jnp.where(self.owner_slot[at] == quota, ref[at], 0)
        return value

    def slot(self, home, quota):
        value = jnp.int32(0)
        for m in range(self.slots):
            at = self.lead + (0, m, home)
            value = value + jnp.where(self.owner_slot[at] == quota, m, 0)
        return value


def bands(strips):
    return REACHES if strips - 3 >= 2 else 2


def batch_of(strips, angle_devs):
    every = [(step, k) for step in range(angle_devs) for k in range(bands(strips))]
    return [item for item in every if item != (0, 1)]


def kernel(
    sizes,
    scaling,
    crystal,
    probe_in,
    amplitude,
    tables_in,
    shear_in,
    scan_x_in,
    scan_y_in,
    slot_angle_in,
    owner_slot_in,
    counts_in,
    out,
    shear_out,
    items_out,
    shear,
    items,
    counts,
    shears,
    others,
    film,
    probe,
    dft,
    sent0,
    sent1,
    sent2,
    got0,
    got1,
    got2,
    mix0,
    mix1,
    mix2,
    part0,
    part1,
    part2,
    own,
    measured,
    cuts,
    windows,
    dft_rot,
    probe_rot,
    picks_local,
    picks_mine,
    picks_theirs,
    placed_local,
    placed_mine,
    placed_theirs,
    spec,
    back,
    load_sem,
    early_send,
    film_send,
    film_recv,
    mix_send,
    mix_recv,
    own_send,
    own_recv,
    amp_send,
    amp_recv,
    meta_load,
    meta_send,
    meta_recv,
    meta_pull,
    cut_send,
    pass_send,
    win_recv,
):
    strips, angle_devs, depths, layers, slots, columns = sizes
    quarter = strips // 4
    half = slots // depths
    share = WX // angle_devs
    reach = share + SHEAR
    sent = (sent0, sent1, sent2)
    got = (got0, got1, got2)
    mix = (mix0, mix1, mix2)
    parts = (part0, part1, part2)
    s = lax.axis_index("strip")
    a = lax.axis_index("angle")
    d = lax.axis_index("depth")
    scan_x, owner_slot, scan_y, slot_angle = [items.at[i] for i in range(4)]
    meta = Meta(shear, owner_slot, slots, ())
    margin = columns - FRAME
    kinds = bands(strips)
    batch = batch_of(strips, angle_devs)
    rows_of = dict(zip(batch, range(len(batch))))

    def kind(k):
        return k % kinds

    def seat(device):
        return 0 if depths == 2 else device


    def lanes(rows):
        return lax.broadcasted_iota(jnp.int32, (rows, margin), 1)

    def rcopy(source, target, send_sem, recv_sem, **where):
        return pltpu.make_async_remote_copy(
            source, target, send_sem, recv_sem, device_id=where, device_id_type=MESH
        )

    def wrap(strip):
        return lax.rem(strip + 4 * strips, strips)

    same = (scan_x_in, owner_slot_in, scan_y_in, slot_angle_in)
    metas = [
        pltpu.make_async_copy(shear_in, shear, meta_load.at[0]),
        pltpu.make_async_copy(counts_in, counts, meta_load.at[1]),
    ]
    several = [pltpu.make_async_copy(x, items.at[i], meta_load.at[2]) for i, x in enumerate(same)]
    loads = [
        pltpu.make_async_copy(
            crystal.at[:, part],
            film.at[:, :, part * columns : (part + 1) * columns],
            load_sem.at[0],
        )
        for part in range(2)
    ]
    late = [
        pltpu.make_async_copy(source, target, load_sem.at[1 + i])
        for i, (source, target) in enumerate(((probe_in, probe), (tables_in, dft)))
    ]
    table, table_t = dft.at[0], dft.at[1]
    for copy in metas + several + loads:
        copy.start()

    blank = jnp.zeros(windows.shape[:3] + (SHEAR, 2 * FRAME), jnp.bfloat16)
    windows[:, :, :, 0:SHEAR] = blank
    windows[:, :, :, share:reach] = blank

    barrier = pltpu.get_barrier_semaphore()
    shifts = set()
    for k in range(REACHES):
        for t in range(quarter):
            shifts |= {(1 - k + 4 * t) % strips, (k - 1 - 4 * t) % strips}
    expected = jnp.int32(0)
    for shift in sorted(shifts | {0}):
        peer = wrap(s + shift)
        if quarter == 1 and shift:
            close = jnp.abs(peer - s) == 1
        else:
            close = peer >= 0
        near = angle_devs + depths - 1 - (1 if shift == 0 else 0)
        expected = expected + jnp.where(close, near, 0)

        @pl.when(close)
        def _():
            for step in range(angle_devs):
                if shift or step:
                    place = {"strip": peer, "angle": lax.rem(a + step, angle_devs)}
                    pl.semaphore_signal(barrier, 1, device_id=place, device_id_type=MESH)
            for step in range(1, depths):
                place = {"strip": peer, "depth": lax.rem(d + step, depths)}
                pl.semaphore_signal(barrier, 1, device_id=place, device_id_type=MESH)

    out[...] = jnp.zeros(out.shape, jnp.float32)
    for ref in (placed_local, placed_mine, placed_theirs):
        ref[...] = jnp.zeros(ref.shape, jnp.bfloat16)

    for copy in metas:
        copy.wait()
    pltpu.make_async_copy(items, items, meta_load.at[2]).wait()
    pltpu.make_async_copy(film, film, load_sem.at[0]).wait()
    for copy in late:
        copy.start()

    def ahead(k, q):
        return k != 1 and q == 0

    def size(k, q):
        return (ROWS[k] - (EARLY if ahead(k, q) else 0)) // depths

    def block(k, q, device):
        rows = size(k, q)
        low = EARLY if ahead(k, q) else 0
        return pl.ds(pl.multiple_of(low + device * rows, 16), rows)

    def crossing(k):
        return 0 if quarter == 1 else kind(k)

    def mix_copy(k, q, step):
        target = lax.rem(d + step, depths)
        return rcopy(
            sent[k].at[q, block(k, q, target)],
            mix[k].at[q, step - 1, 0 : size(k, q)],
            early_send.at[kind(k)] if ahead(k, q) else mix_send.at[crossing(k), step - 1],
            mix_recv.at[crossing(k), q, step - 1],
            depth=target,
        )

    def film_copy(k, q):
        return rcopy(
            parts[k].at[q, 0 : size(k, q)],
            got[k].at[q % half, block(k, q, d)],
            early_send.at[kind(k)] if ahead(k, q) else film_send.at[crossing(k)],
            film_recv.at[k, q % half],
            strip=wrap(s - k + 4 * (q % quarter) + 1),
            depth=q // half,
        )

    def early_copy(k):
        low = jnp.where(d == 0, 0, ROWS[k] + (d - 1) * EARLY)
        return rcopy(
            sent[k].at[0, 0:EARLY],
            got[k].at[0, pl.ds(pl.multiple_of(low, 16), EARLY)],
            early_send.at[kind(k)],
            film_recv.at[k, 0],
            strip=wrap(s - k + 1),
            depth=0,
        )

    def own_copy(q):
        return rcopy(
            sent[1].at[q],
            own.at[d, q % half],
            own_send.at[q % half, seat(q // half)],
            own_recv.at[q % half, seat(d)],
            depth=q // half,
        )

    def exchange(k, q):
        for step in range(1, depths):
            mix_copy(k, q, step).start()

    def merge(k, q):
        rows = size(k, q)
        value = sent[k][q, block(k, q, d)].astype(jnp.float32)
        for step in range(1, depths):
            mix_copy(k, q, step).wait_recv()
            value = value + mix[k][q, step - 1, 0:rows].astype(jnp.float32)
        parts[k][q, 0:rows] = value.astype(jnp.bfloat16)
        film_copy(k, q).start()

    def own_strip(k, q):
        return (1 - k + 4 * (q % quarter)) % strips == 0

    def project(k):
        home = s - k
        gap = differences(ROWS[k], WX)
        chosen = []
        for q in range(slots):
            offset = meta.pick(scan_x, home, q) - WX * k + BASES[k]
            angle = meta.pick(slot_angle, home, q)
            chosen.append(
                jnp.concatenate(
                    [one_hot(gap == offset + meta.shear(angle, z)) for z in range(layers)], axis=1
                )
            )
        flat = film[...].reshape(layers * WX, 2 * columns)
        tall = dot(jnp.concatenate(chosen, axis=0), flat)
        for q in range(slots):
            corner = meta.pick(scan_y, home, q)
            first = lanes(ROWS[k]) >= corner
            rows = tall[q * ROWS[k] : (q + 1) * ROWS[k]]
            wound = []
            for part in range(2):
                side = rows[:, part * columns : (part + 1) * columns]
                wound += [jnp.where(first, side[:, :margin], side[:, FRAME:]), side[:, margin:FRAME]]
            sent[k][q] = jnp.concatenate(wound, axis=1).astype(jnp.bfloat16)

    def reached(k):
        return (s - k >= 0) & (s - k <= strips - 3)

    for k in (0, 2):

        @pl.when(reached(k))
        def _():
            project(k)

    pl.semaphore_wait(barrier, expected)
    for k in (0, 2):

        @pl.when(reached(k))
        def _():
            exchange(k, 0)
            early_copy(k).start()
            for q in range(1, slots):
                exchange(k, q)


    def amp_copy(other):
        return rcopy(
            amplitude.at[other * half : (other + 1) * half],
            measured.at[d],
            amp_send.at[seat(other)],
            amp_recv.at[0],
            depth=other,
        )

    def amp_own(other):
        return pltpu.make_async_copy(
            amplitude.at[other * half : (other + 1) * half], measured.at[d], amp_recv.at[0]
        )

    def meta_copies(step):
        def send(source, target, i):
            return rcopy(
                source,
                target,
                meta_send.at[step - 1, i],
                meta_recv.at[step - 1, i],
                angle=lax.rem(a + step, angle_devs),
            )

        first = [send(shear_in, shear_out.at[step], 0)]
        return first + [send(x, items_out.at[step, i], 1) for i, x in enumerate(same[1:])]

    def meta_waits(step, sem):
        for i, ref in enumerate((shear_out.at[step], items_out.at[step])):
            pltpu.make_async_copy(ref, ref, sem.at[step - 1, i]).wait()

    def meta_pulls(step):
        return [
            pltpu.make_async_copy(shear_out.at[step], shears.at[step], meta_pull.at[step - 1, 0]),
            pltpu.make_async_copy(items_out.at[step], others.at[step], meta_pull.at[step - 1, 1]),
        ]

    for step in range(1, angle_devs):
        for copy in meta_copies(step):
            copy.start()

    for other in range(depths):

        @pl.when(d != other)
        def _():
            amp_copy(other).start()

        @pl.when(d == other)
        def _():
            amp_own(other).start()

    for q in range(slots):
        for k in (0, 2):

            @pl.when(reached(k))
            def _():
                merge(k, q)


    @pl.when(reached(1))
    def _():
        project(1)
        for q in range(slots):
            if own_strip(1, q):

                @pl.when(d == q // half)
                def _():
                    own[d, q % half] = sent[1][q]

                @pl.when(d != q // half)
                def _():
                    own_copy(q).start()
            else:
                exchange(1, q)
        for q in range(slots):
            if not own_strip(1, q):
                merge(1, q)

    groups = [(meta, scan_y, slot_angle)]
    for step in range(1, angle_devs):
        owner_slots, scans_y, slot_angles = [others.at[step, i] for i in range(3)]
        groups.append((Meta(shears.at[step], owner_slots, slots, ()), scans_y, slot_angles))

    def prepare(target, items):
        wanted = []
        for step, k, q, at in items:
            home = jnp.clip(s - k, 0, strips - 1)
            source, _, angles = groups[step]
            angle = source.pick(angles, home, q)
            base = jnp.where(reached(k), at + SHEAR, -4 * target.shape[1])
            wanted.append([base - source.shear(angle, z) for z in range(layers)])
        gap = differences(share, target.shape[1])
        for z in range(layers):
            mask = gap == wanted[0][z]
            for want in wanted[1:]:
                mask = mask | (gap == want[z])
            target[z * share : (z + 1) * share] = one_hot(mask)

    locals_ = [(0, 1, q, q * reach) for q in range(slots)]

    def items_of(depth):
        return [
            (step, k, depth * half + lane, (lane * len(batch) + rows_of[step, kind(k)]) * reach)
            for lane in range(half)
            for step in list(range(1, angle_devs)) + [0]
            for k in (1, 0, 2)
            if (step, k) != (0, 1)
        ]

    prepare(picks_local, locals_)

    for copy in late:
        copy.wait()
    pltpu.make_async_copy(measured, measured, amp_recv.at[0]).wait()


    def edge(k, part):
        return (k == 0 and part == 0) or (k == 2 and part == angle_devs - 1)

    def filled(k, narrow):
        low = SHEAR if narrow and k == 0 else 0
        return slice(low, low + (share if narrow else reach))

    def cut_copy(k, lane, quota, home, part):
        step = lax.rem(part - a + angle_devs, angle_devs)
        narrow = edge(k, part)
        return rcopy(
            cuts.at[lane, k, part, filled(k, narrow)],
            windows.at[step, kind(k), quota, filled(k, narrow)],
            cut_send.at[REACHES + k // 2 if narrow else k, lane],
            win_recv.at[step, kind(k), quota],
            strip=wrap(home + k),
            angle=part,
        )

    def owned(act):
        for lane in range(half):
            quota = d * half + lane
            home = wrap(s - 1 - 4 * lax.rem(quota, quarter))

            @pl.when(home <= strips - 3)
            def _():
                act(lane, quota, home, wrap(home + 1) == s)

    def work(lane, quota, home, local):
        def arrive(k):
            whole = got[k].at[lane, 0 : ROWS[k]]
            if lane or k == 1:
                pltpu.make_async_copy(whole, whole, film_recv.at[k, lane]).wait()
            else:

                @pl.when(quota == 0)
                def _():
                    full = got[k].at[lane]
                    pltpu.make_async_copy(full, full, film_recv.at[k, lane]).wait()
                    value = got[k][lane, 0:EARLY].astype(jnp.float32)
                    for source in range(1, depths):
                        low = ROWS[k] + (source - 1) * EARLY
                        value = value + got[k][lane, low : low + EARLY].astype(jnp.float32)
                    got[k][lane, 0:EARLY] = value.astype(jnp.bfloat16)

                @pl.when(quota != 0)
                def _():
                    pltpu.make_async_copy(whole, whole, film_recv.at[k, lane]).wait()

        corner = meta.pick(scan_y, home, quota)
        gap = differences(FRAME, FRAME)
        turn = one_hot((gap == -corner) | (gap == FRAME - corner))
        back_turn = one_hot((gap == corner) | (gap == corner - FRAME))
        for part in range(2):
            at = slice(part * FRAME, (part + 1) * FRAME)
            probe_rot[lane, part] = dot(probe[part], back_turn).astype(jnp.bfloat16)
            dft_rot[lane, 0, at] = dot(turn, table[at]).astype(jnp.bfloat16)
            dft_rot[lane, 1, :, at] = dot(table_t[:, at], back_turn).astype(jnp.bfloat16)

        @pl.when(local)
        def _():
            value = own[d, lane].astype(jnp.float32)
            for step in range(1, depths):
                source = lax.rem(d + step, depths)
                rcopy(
                    sent[1].at[lane],
                    own.at[source, lane],
                    own_send.at[lane, seat(source)],
                    own_recv.at[lane, seat(source)],
                    depth=source,
                ).wait_recv()
                value = value + own[source, lane].astype(jnp.float32)
            got[1][lane] = value.astype(jnp.bfloat16)

        @pl.when(jnp.logical_not(local))
        def _():
            arrive(1)

        def forward(low, high, extra):
            rows = slice(low, high)
            whole = got1[lane, rows].astype(jnp.float32) + extra.astype(jnp.float32)
            re, im = whole[:, :FRAME], whole[:, FRAME:]
            probe_re = probe_rot[lane, 0, rows].astype(jnp.float32)
            probe_im = probe_rot[lane, 1, rows].astype(jnp.float32)
            exit_wave = jnp.concatenate(
                [probe_re * re - probe_im * im, probe_re * im + probe_im * re], axis=1
            ).astype(jnp.bfloat16)
            section = dot(exit_wave, dft_rot[lane, 0]).astype(jnp.bfloat16)
            left = jnp.concatenate(
                [table_t[:, rows], table_t[:, FRAME + low : FRAME + high]], axis=1
            )
            return dot(left, jnp.concatenate([section[:, :FRAME], section[:, FRAME:]], axis=0))

        arrive(0)
        spec[...] = forward(0, WX, got0[lane, 0:WX])
        arrive(2)
        spectrum = spec[...] + forward(WX, FRAME, got2[lane, 0 : FRAME - WX])
        spec_re, spec_im = spectrum[:FRAME], spectrum[FRAME:]
        power = spec_re * spec_re + spec_im * spec_im
        levels = jnp.concatenate(
            [measured[source, lane] for source in range(depths)], axis=0
        ).astype(jnp.float32)
        live = meta.slot(home, quota) < counts[0, home]
        live = jnp.where(live, 1.0, 0.0).astype(jnp.float32)
        factor = (1.0 - levels * lax.rsqrt(jnp.maximum(power, 1.0))) * live
        residual = jnp.concatenate([spec_re * factor, spec_im * factor], axis=1).astype(
            jnp.bfloat16
        )
        inverse = dot(residual, dft_rot[lane, 1]).astype(jnp.bfloat16)
        stacked = jnp.concatenate([inverse[:, :FRAME], inverse[:, FRAME:]], axis=0)
        offset = meta.pick(scan_x, home, quota)

        def backward(low, high):
            rows = slice(low, high)
            left = jnp.concatenate([table[rows], table[FRAME + low : FRAME + high]], axis=0)
            wave = dot(left, stacked)
            re, im = wave[: high - low], wave[high - low :]
            probe_re = probe_rot[lane, 0, rows].astype(jnp.float32)
            probe_im = probe_rot[lane, 1, rows].astype(jnp.float32)
            return jnp.concatenate(
                [probe_re * re + probe_im * im, probe_re * im - probe_im * re], axis=1
            ).astype(jnp.bfloat16)

        def cut(k, part, low, value):
            gap = differences(reach, value.shape[0])
            first = WX * k - offset + part * share - SHEAR - low
            cuts[lane, k, part] = dot(one_hot(gap == first), value).astype(jnp.bfloat16)

        def send(k, low, value):
            for part in range(angle_devs):
                cut(k, part, low, value)
                copy = cut_copy(k, lane, quota, home, part)
                if k == 1:

                    @pl.when(jnp.logical_not(local & (a == part)))
                    def _():
                        copy.start()
                else:
                    copy.start()

        top = backward(0, WX)
        back[0:WX] = top
        send(0, 0, top)
        bottom = backward(WX, FRAME)
        back[WX:FRAME] = bottom
        send(1, 0, back[...])
        send(2, WX, bottom)

        @pl.when(local)
        def _():
            windows[0, kind(1), quota] = cuts[lane, 1, a]


    owned(work)

    for step in range(1, angle_devs):
        meta_waits(step, meta_recv)
        for copy in meta_pulls(step):
            copy.start()
    for step in range(1, angle_devs):
        for copy in meta_pulls(step):
            copy.wait()
    mine = items_of(d)
    theirs = [items_of(lax.rem(d + step, depths)) for step in range(1, depths)]
    prepare(picks_mine, mine)
    for step in range(1, depths):
        prepare(picks_theirs.at[step - 1], theirs[step - 1])


    def sized(k, act):
        if k == 1:
            act(filled(k, False))
        else:
            narrow = a == (0 if k == 0 else angle_devs - 1)

            @pl.when(narrow)
            def _():
                act(filled(k, True))

            @pl.when(jnp.logical_not(narrow))
            def _():
                act(filled(k, False))

    def recv(step, k, q):
        def act(rows):
            window = windows.at[step, kind(k), q, rows]
            pltpu.make_async_copy(window, window, win_recv.at[step, kind(k), q]).wait()

        sized(k, act)

    def relay(step, k):
        for q in range(slots):

            @pl.when(d == q // half)
            def _():
                def act(rows):
                    window = windows.at[step, kind(k), q, rows]
                    if not (step == 0 and own_strip(k, q)):
                        pltpu.make_async_copy(window, window, win_recv.at[step, kind(k), q]).wait()
                    for other in range(depths):
                        if other != q // half:
                            rcopy(
                                window,
                                window,
                                pass_send.at[kind(k), seat(other)],
                                win_recv.at[step, kind(k), q],
                                depth=other,
                            ).start()

                sized(k, act)

    def place(target, step, k, q, at):
        source, corners, _ = groups[step]
        first = lanes(reach) >= source.pick(corners, s - k, q)
        window = windows.at[step, kind(k), q]
        rows = slice(at, at + reach)
        for part in range(2):
            head = window[:, part * FRAME : part * FRAME + margin].astype(jnp.float32)
            left = part * columns
            target[rows, left : left + margin] = jnp.where(first, head, 0.0).astype(jnp.bfloat16)
            target[rows, left + margin : left + FRAME] = window[
                :, part * FRAME + margin : (part + 1) * FRAME
            ]
            target[rows, left + FRAME : left + columns] = jnp.where(first, 0.0, head).astype(
                jnp.bfloat16
            )

    def add(chosen, target):
        value = dot(chosen[...], target[...]) * scaling
        for z in range(layers):
            for part in range(2):
                out[z, part] += value[
                    z * share : (z + 1) * share, part * columns : (part + 1) * columns
                ]

    @pl.when(reached(1))
    def _():
        relay(0, 1)
        for q in range(slots):

            @pl.when(d != q // half)
            def _():
                recv(0, 1, q)

        for item in locals_:
            place(placed_local, *item)
        add(picks_local, placed_local)

    for step, k in [(step, k) for step in list(range(1, angle_devs)) + [0] for k in (1, 0, 2)]:
        if (step, k) != (0, 1):

            @pl.when(reached(k))
            def _():
                relay(step, k)
                for item in mine:
                    if item[:2] == (step, k):
                        place(placed_mine, *item)

    add(picks_mine, placed_mine)
    for i in range(1, depths):
        for step, k, q, at in theirs[i - 1]:

            @pl.when(reached(k))
            def _():
                recv(step, k, q)
                place(placed_theirs.at[i - 1], step, k, q, at)

        add(picks_theirs.at[i - 1], placed_theirs.at[i - 1])

    for other in range(depths):

        @pl.when(d != other)
        def _():
            amp_copy(other).wait_send()

    for step in range(1, angle_devs):
        meta_waits(step, meta_send)
    for k in range(REACHES):

        @pl.when(reached(k))
        def _():
            for q in range(slots):
                if own_strip(k, q):

                    @pl.when(d != q // half)
                    def _():
                        own_copy(q).wait_send()
            rest = [q for q in range(slots) if not own_strip(k, q)]
            if ahead(k, 0):
                first = sent[k].at[0]
                pltpu.make_async_copy(first, first, early_send.at[kind(k)]).wait()
                rest = rest[1:]
            if rest:
                whole = parts[k].at[slots - len(rest) :]
                pltpu.make_async_copy(whole, whole, film_send.at[crossing(k)]).wait()
                for step in range(1, depths):
                    pltpu.make_async_copy(whole, whole, mix_send.at[crossing(k), step - 1]).wait()

    def drain(lane, quota, home, local):
        for k in range(REACHES):
            whole = cuts.at[lane, k]
            if k != 1:
                narrow = cuts.at[lane, k, 0, 0:share]
                pltpu.make_async_copy(narrow, narrow, cut_send.at[REACHES + k // 2, lane]).wait()
                if angle_devs > 1:
                    most = cuts.at[lane, k, 1:]
                    pltpu.make_async_copy(most, most, cut_send.at[k, lane]).wait()
            else:
                most = cuts.at[lane, k, 1:]

                @pl.when(local)
                def _():
                    pltpu.make_async_copy(most, most, cut_send.at[k, lane]).wait()

                @pl.when(jnp.logical_not(local))
                def _():
                    pltpu.make_async_copy(whole, whole, cut_send.at[k, lane]).wait()

    owned(drain)

    for k in range(REACHES):

        @pl.when(reached(k))
        def _():
            for other in range(depths):

                @pl.when(d != other)
                def _():
                    def act(rows):
                        whole = windows.at[:, kind(k), 0:half, rows]
                        pltpu.make_async_copy(
                            whole, whole, pass_send.at[kind(k), seat(other)]
                        ).wait()

                    sized(k, act)


def body(sizes_of, crystal, probe, amplitude, shear, scan_x, scan_y, slot_angle, owner_slot, counts):
    strips, angle_devs, depths = sizes_of
    layers, _, _, columns = crystal.shape
    slots = owner_slot.shape[2]
    half = slots // depths
    share = WX // angle_devs
    reach = share + SHEAR
    kinds = bands(strips)
    seats = 1 if depths == 2 else depths
    crossings = 1 if strips == 4 else kinds
    local_rows = -(-(slots * reach) // 128) * 128
    batch_rows = -(-(half * len(batch_of(strips, angle_devs)) * reach) // 128) * 128
    dft = dft_tables()
    bf16 = jnp.bfloat16
    scan_x, scan_y, slot_angle, owner_slot = [
        jnp.swapaxes(value, 1, 2) for value in (scan_x, scan_y, slot_angle, owner_slot)
    ]
    sizes = (strips, angle_devs, depths, layers, slots, columns)
    hbm = pl.BlockSpec(memory_space=pltpu.HBM)
    vmem = pl.BlockSpec(memory_space=pltpu.VMEM)
    dma = pltpu.SemaphoreType.DMA
    small = (shear, scan_x, scan_y, slot_angle, owner_slot, counts)
    gathered = ((angle_devs,) + shear.shape, (angle_devs, 3) + scan_x.shape)
    scratch = [pltpu.SMEM(x, jnp.int32) for x in (shear.shape, (4,) + scan_x.shape, counts.shape)]
    scratch += [pltpu.SMEM(x, jnp.int32) for x in gathered]
    scratch += [
        pltpu.VMEM((layers, WX, 2 * columns), bf16),
        pltpu.VMEM(probe.shape, bf16),
        pltpu.VMEM(dft.shape, bf16),
    ]
    scratch += [pltpu.VMEM((slots, rows, 2 * FRAME), bf16) for rows in ROWS]
    extra = (depths - 1) * EARLY
    scratch += [
        pltpu.VMEM((half, rows + (0 if k == 1 else extra), 2 * FRAME), bf16)
        for k, rows in enumerate(ROWS)
    ]
    scratch += [pltpu.VMEM((slots, depths - 1, rows // depths, 2 * FRAME), bf16) for rows in ROWS]
    scratch += [pltpu.VMEM((slots, rows // depths, 2 * FRAME), bf16) for rows in ROWS]
    scratch += [pltpu.VMEM((depths, half, FRAME, 2 * FRAME), bf16)]
    scratch += [
        pltpu.VMEM((depths, half, FRAME // depths, FRAME), bf16),
        pltpu.VMEM((half, REACHES, angle_devs, reach, 2 * FRAME), bf16),
        pltpu.VMEM((angle_devs, kinds, slots, reach, 2 * FRAME), bf16),
        pltpu.VMEM((half,) + dft.shape, bf16),
        pltpu.VMEM((half,) + probe.shape, bf16),
        pltpu.VMEM((layers * share, local_rows), bf16),
        pltpu.VMEM((layers * share, batch_rows), bf16),
        pltpu.VMEM((depths - 1, layers * share, batch_rows), bf16),
        pltpu.VMEM((local_rows, 2 * columns), bf16),
        pltpu.VMEM((batch_rows, 2 * columns), bf16),
        pltpu.VMEM((depths - 1, batch_rows, 2 * columns), bf16),
        pltpu.VMEM((2 * FRAME, FRAME), jnp.float32),
        pltpu.VMEM((FRAME, 2 * FRAME), bf16),
        dma((3,)),
        dma((kinds,)),
        dma((crossings,)),
        dma((REACHES, half)),
        dma((crossings, depths - 1)),
        dma((crossings, slots, depths - 1)),
        dma((half, seats)),
        dma((half, seats)),
        dma((seats,)),
        dma((1,)),
        dma((3,)),
        dma((angle_devs - 1, 2)),
        dma((angle_devs - 1, 2)),
        dma((angle_devs - 1, 2)),
        dma((REACHES + 2, half)),
        dma((kinds, seats)),
        dma((angle_devs, kinds, slots)),
    ]
    scaling = 1.0 / (shear.shape[0] * angle_devs)
    result, *_ = pl.pallas_call(
        functools.partial(kernel, sizes, scaling),
        out_shape=(jax.ShapeDtypeStruct((layers, 2, share, columns), jnp.float32),)
        + tuple(jax.ShapeDtypeStruct(x, jnp.int32) for x in gathered),
        in_specs=[hbm] * 10,
        out_specs=(vmem,) + (hbm,) * 2,
        scratch_shapes=scratch,
        compiler_params=pltpu.CompilerParams(
            collective_id=0, has_side_effects=True, vmem_limit_bytes=VMEM_LIMIT
        ),
    )(
        *(
            pltpu.with_memory_space_constraint(x, pltpu.HBM)
            for x in (crystal, probe, amplitude, dft, *small)
        )
    )
    return result


def solution(mesh):
    placed = (
        P(("groups", "depth"), None, "strip", None),
        P(),
        P("angle", ("groups", "strip", "depth"), None),
        P(("groups", "angle"), "depth"),
        P(("groups", "angle"), None, None),
        P(("groups", "angle"), None, None),
        P(("groups", "angle"), None, None),
        P(("groups", "angle"), None, None),
        P(("groups", "angle"), None),
    )
    sizes_of = (mesh.shape["strip"], mesh.shape["angle"], mesh.shape["depth"])
    return jax.shard_map(
        functools.partial(body, sizes_of),
        mesh=mesh,
        in_specs=placed,
        out_specs=P(("groups", "depth"), None, ("strip", "angle"), None),
        check_vma=False,
    )
```

```python
import functools

import jax
import jax.numpy as jnp
import numpy as np
from jax import lax
from jax.experimental import pallas as pl
from jax.experimental.pallas import tpu as pltpu
from jax.sharding import PartitionSpec as P

FRAME = 256
WX = 128
SHEAR = 16
REACHES = 3
ROWS = (WX, FRAME, FRAME - WX)
BASES = (0, 0, WX)
EARLY = 32
VMEM_LIMIT = 44 * 2**20
MESH = pl.DeviceIdType.MESH


def dft_tables():
    index_row = np.arange(FRAME)
    phase = (index_row[:, None] * index_row[None, :] % FRAME) * (2.0 * np.pi / FRAME)
    real = np.cos(phase) / np.sqrt(FRAME)
    imag = -np.sin(phase) / np.sqrt(FRAME)
    table = np.block([[real, imag], [-imag, real]]).astype(np.float32)
    return jnp.asarray(np.stack([table, table.T]), jnp.bfloat16)


def dot(left, right):
    return jnp.dot(left, right, preferred_element_type=jnp.float32)


def differences(rows, columns):
    shape = (rows, columns)
    return lax.broadcasted_iota(jnp.int32, shape, 1) - lax.broadcasted_iota(jnp.int32, shape, 0)


def one_hot(mask):
    return jnp.where(mask, 1.0, 0.0).astype(jnp.bfloat16)


class Meta:
    def __init__(self, lifts, owner_slot, slots, lead):
        self.lifts, self.owner_slot = lifts, owner_slot
        self.slots, self.lead = slots, lead

    def shear(self, angle, z):
        return self.lifts[self.lead + (angle, z)]

    def pick(self, ref, home, quota):
        value = jnp.int32(0)
        for m in range(self.slots):
            at = self.lead + (0, m, home)
            value = value + jnp.where(self.owner_slot[at] == quota, ref[at], 0)
        return value

    def slot(self, home, quota):
        value = jnp.int32(0)
        for m in range(self.slots):
            at = self.lead + (0, m, home)
            value = value + jnp.where(self.owner_slot[at] == quota, m, 0)
        return value


def bands(strips):
    return REACHES if strips - 3 >= 2 else 2


def batch_of(strips, angle_devs):
    every = [(step, k) for step in range(angle_devs) for k in range(bands(strips))]
    return [item for item in every if item != (0, 1)]


def kernel(
    sizes,
    scaling,
    crystal,
    probe_in,
    amplitude,
    tables_in,
    shear_in,
    scan_x_in,
    scan_y_in,
    slot_angle_in,
    owner_slot_in,
    counts_in,
    out,
    shear_out,
    items_out,
    shear,
    items,
    counts,
    shears,
    others,
    film,
    probe,
    dft,
    sent0,
    sent1,
    sent2,
    got0,
    got1,
    got2,
    mix0,
    mix1,
    mix2,
    part0,
    part1,
    part2,
    own,
    measured,
    cuts,
    windows,
    dft_rot,
    probe_rot,
    inner,
    picks_local,
    picks_mine,
    picks_theirs,
    placed_local,
    placed_mine,
    placed_theirs,
    spec,
    back,
    load_sem,
    early_send,
    film_send,
    film_recv,
    mix_send,
    mix_recv,
    own_send,
    own_recv,
    amp_send,
    amp_recv,
    meta_load,
    meta_send,
    meta_recv,
    meta_pull,
    cut_send,
    pass_send,
    win_recv,
):
    strips, angle_devs, depths, layers, slots, columns = sizes
    quarter = strips // 4
    half = slots // depths
    share = WX // angle_devs
    reach = share + SHEAR
    sent = (sent0, sent1, sent2)
    got = (got0, got1, got2)
    mix = (mix0, mix1, mix2)
    parts = (part0, part1, part2)
    s = lax.axis_index("strip")
    a = lax.axis_index("angle")
    d = lax.axis_index("depth")
    scan_x, owner_slot, scan_y, slot_angle = [items.at[i] for i in range(4)]
    meta = Meta(shear, owner_slot, slots, ())
    margin = columns - FRAME
    kinds = bands(strips)
    batch = batch_of(strips, angle_devs)
    rows_of = dict(zip(batch, range(len(batch))))

    outer = strips - 3
    spread = (1, None) if kinds == 2 else (1, 0, 2)

    def kind(k):
        return 0 if k is None else k % kinds

    def home_of(k):
        return jnp.where(s <= outer, s, s - 2) if k is None else s - k

    def seat(device):
        return 0 if depths == 2 else device


    def lanes(rows):
        return lax.broadcasted_iota(jnp.int32, (rows, margin), 1)

    def rcopy(source, target, send_sem, recv_sem, **where):
        return pltpu.make_async_remote_copy(
            source, target, send_sem, recv_sem, device_id=where, device_id_type=MESH
        )

    def wrap(strip):
        return lax.rem(strip + 4 * strips, strips)

    same = (scan_x_in, owner_slot_in, scan_y_in, slot_angle_in)
    metas = [
        pltpu.make_async_copy(shear_in, shear, meta_load.at[0]),
        pltpu.make_async_copy(counts_in, counts, meta_load.at[1]),
    ]
    several = [pltpu.make_async_copy(x, items.at[i], meta_load.at[2]) for i, x in enumerate(same)]
    loads = [
        pltpu.make_async_copy(
            crystal.at[:, part],
            film.at[:, :, part * columns : (part + 1) * columns],
            load_sem.at[0],
        )
        for part in range(2)
    ]
    late = [
        pltpu.make_async_copy(source, target, load_sem.at[1 + i])
        for i, (source, target) in enumerate(((probe_in, probe), (tables_in, dft)))
    ]
    table, table_t = dft.at[0], dft.at[1]
    for copy in metas + several + loads:
        copy.start()

    blank = jnp.zeros(windows.shape[:3] + (SHEAR, 2 * FRAME), jnp.bfloat16)
    windows[:, :, :, 0:SHEAR] = blank
    windows[:, :, :, share:reach] = blank

    barrier = pltpu.get_barrier_semaphore()
    shifts = set()
    for k in range(REACHES):
        for t in range(quarter):
            shifts |= {(1 - k + 4 * t) % strips, (k - 1 - 4 * t) % strips}
    expected = jnp.int32(0)
    for shift in sorted(shifts | {0}):
        peer = wrap(s + shift)
        if quarter == 1 and shift:
            close = jnp.abs(peer - s) == 1
        else:
            close = peer >= 0
        near = angle_devs + depths - 1 - (1 if shift == 0 else 0)
        expected = expected + jnp.where(close, near, 0)

        @pl.when(close)
        def _():
            for step in range(angle_devs):
                if shift or step:
                    place = {"strip": peer, "angle": lax.rem(a + step, angle_devs)}
                    pl.semaphore_signal(barrier, 1, device_id=place, device_id_type=MESH)
            for step in range(1, depths):
                place = {"strip": peer, "depth": lax.rem(d + step, depths)}
                pl.semaphore_signal(barrier, 1, device_id=place, device_id_type=MESH)

    out[...] = jnp.zeros(out.shape, jnp.float32)
    for ref in (placed_local, placed_mine, placed_theirs):
        ref[...] = jnp.zeros(ref.shape, jnp.bfloat16)

    for copy in metas:
        copy.wait()
    pltpu.make_async_copy(items, items, meta_load.at[2]).wait()
    pltpu.make_async_copy(film, film, load_sem.at[0]).wait()
    for copy in late:
        copy.start()

    def ahead(k, q):
        return k != 1 and q == 0

    def size(k, q):
        return (ROWS[k] - (EARLY if ahead(k, q) else 0)) // depths

    def block(k, q, device):
        rows = size(k, q)
        low = EARLY if ahead(k, q) else 0
        return pl.ds(pl.multiple_of(low + device * rows, 16), rows)

    def crossing(k):
        return 0 if quarter == 1 else kind(k)

    def mix_copy(k, q, step):
        target = lax.rem(d + step, depths)
        return rcopy(
            sent[k].at[q, block(k, q, target)],
            mix[k].at[q, step - 1, 0 : size(k, q)],
            early_send.at[kind(k)] if ahead(k, q) else mix_send.at[crossing(k), step - 1],
            mix_recv.at[crossing(k), q, step - 1],
            depth=target,
        )

    def film_copy(k, q):
        return rcopy(
            parts[k].at[q, 0 : size(k, q)],
            got[k].at[q % half, block(k, q, d)],
            early_send.at[kind(k)] if ahead(k, q) else film_send.at[crossing(k)],
            film_recv.at[k, q % half],
            strip=wrap(s - k + 4 * (q % quarter) + 1),
            depth=q // half,
        )

    def early_copy(k):
        low = jnp.where(d == 0, 0, ROWS[k] + (d - 1) * EARLY)
        return rcopy(
            sent[k].at[0, 0:EARLY],
            got[k].at[0, pl.ds(pl.multiple_of(low, 16), EARLY)],
            early_send.at[kind(k)],
            film_recv.at[k, 0],
            strip=wrap(s - k + 1),
            depth=0,
        )

    def own_copy(q):
        return rcopy(
            sent[1].at[q],
            own.at[d, q % half],
            own_send.at[q % half, seat(q // half)],
            own_recv.at[q % half, seat(d)],
            depth=q // half,
        )

    def exchange(k, q):
        for step in range(1, depths):
            mix_copy(k, q, step).start()

    def merge(k, q):
        rows = size(k, q)
        value = sent[k][q, block(k, q, d)].astype(jnp.float32)
        for step in range(1, depths):
            mix_copy(k, q, step).wait_recv()
            value = value + mix[k][q, step - 1, 0:rows].astype(jnp.float32)
        parts[k][q, 0:rows] = value.astype(jnp.bfloat16)
        film_copy(k, q).start()

    def own_strip(k, q):
        return (1 - k + 4 * (q % quarter)) % strips == 0

    def project(k):
        home = s - k
        gap = differences(ROWS[k], WX)
        chosen = []
        for q in range(slots):
            offset = meta.pick(scan_x, home, q) - WX * k + BASES[k]
            angle = meta.pick(slot_angle, home, q)
            chosen.append(
                jnp.concatenate(
                    [one_hot(gap == offset + meta.shear(angle, z)) for z in range(layers)], axis=1
                )
            )
        flat = film[...].reshape(layers * WX, 2 * columns)
        tall = dot(jnp.concatenate(chosen, axis=0), flat)
        for q in range(slots):
            corner = meta.pick(scan_y, home, q)
            first = lanes(ROWS[k]) >= corner
            rows = tall[q * ROWS[k] : (q + 1) * ROWS[k]]
            wound = []
            for part in range(2):
                side = rows[:, part * columns : (part + 1) * columns]
                wound += [jnp.where(first, side[:, :margin], side[:, FRAME:]), side[:, margin:FRAME]]
            sent[k][q] = jnp.concatenate(wound, axis=1).astype(jnp.bfloat16)

    def reached(k):
        return (s - k >= 0) & (s - k <= outer)

    def guarded(k, act):
        if k is None:
            act()
        else:
            pl.when(reached(k))(act)

    for k in (0, 2):

        @pl.when(reached(k))
        def _():
            project(k)

    pl.semaphore_wait(barrier, expected)
    for k in (0, 2):

        @pl.when(reached(k))
        def _():
            exchange(k, 0)
            early_copy(k).start()
            for q in range(1, slots):
                exchange(k, q)


    def amp_copy(other):
        return rcopy(
            amplitude.at[other * half : (other + 1) * half],
            measured.at[d],
            amp_send.at[seat(other)],
            amp_recv.at[0],
            depth=other,
        )

    def amp_own(other):
        return pltpu.make_async_copy(
            amplitude.at[other * half : (other + 1) * half], measured.at[d], amp_recv.at[0]
        )

    def meta_copies(step):
        def send(source, target, i):
            return rcopy(
                source,
                target,
                meta_send.at[step - 1, i],
                meta_recv.at[step - 1, i],
                angle=lax.rem(a + step, angle_devs),
            )

        first = [send(shear_in, shear_out.at[step], 0)]
        return first + [send(x, items_out.at[step, i], 1) for i, x in enumerate(same[1:])]

    def meta_waits(step, sem):
        for i, ref in enumerate((shear_out.at[step], items_out.at[step])):
            pltpu.make_async_copy(ref, ref, sem.at[step - 1, i]).wait()

    def meta_pulls(step):
        return [
            pltpu.make_async_copy(shear_out.at[step], shears.at[step], meta_pull.at[step - 1, 0]),
            pltpu.make_async_copy(items_out.at[step], others.at[step], meta_pull.at[step - 1, 1]),
        ]

    for step in range(1, angle_devs):
        for copy in meta_copies(step):
            copy.start()

    for other in range(depths):

        @pl.when(d != other)
        def _():
            amp_copy(other).start()

        @pl.when(d == other)
        def _():
            amp_own(other).start()

    for q in range(slots):
        for k in (0, 2):

            @pl.when(reached(k))
            def _():
                merge(k, q)


    @pl.when(reached(1))
    def _():
        project(1)
        for q in range(slots):
            if own_strip(1, q):

                @pl.when(d == q // half)
                def _():
                    own[d, q % half] = sent[1][q]

                @pl.when(d != q // half)
                def _():
                    own_copy(q).start()
            else:
                exchange(1, q)
        for q in range(slots):
            if not own_strip(1, q):
                merge(1, q)

    groups = [(meta, scan_y, slot_angle)]
    for step in range(1, angle_devs):
        owner_slots, scans_y, slot_angles = [others.at[step, i] for i in range(3)]
        groups.append((Meta(shears.at[step], owner_slots, slots, ()), scans_y, slot_angles))

    def prepare(target, items):
        wanted = []
        for step, k, q, at in items:
            home = jnp.clip(home_of(k), 0, strips - 1)
            source, corners, angles = groups[step]

            def fill():
                first = lanes(reach) >= source.pick(corners, home, q)
                inner[step, kind(k), q] = one_hot(first)

            guarded(k, fill)
            angle = source.pick(angles, home, q)
            base = at + SHEAR
            if k is not None:
                base = jnp.where(reached(k), base, -4 * target.shape[1])
            wanted.append([base - source.shear(angle, z) for z in range(layers)])
        gap = differences(share, target.shape[1])
        for z in range(layers):
            mask = gap == wanted[0][z]
            for want in wanted[1:]:
                mask = mask | (gap == want[z])
            target[z * share : (z + 1) * share] = one_hot(mask)

    locals_ = [(0, 1, q, q * reach) for q in range(slots)]

    def items_of(depth):
        return [
            (step, k, depth * half + lane, (lane * len(batch) + rows_of[step, kind(k)]) * reach)
            for lane in range(half)
            for step in list(range(1, angle_devs)) + [0]
            for k in spread
            if (step, k) != (0, 1)
        ]

    prepare(picks_local, locals_)

    for copy in late:
        copy.wait()
    pltpu.make_async_copy(measured, measured, amp_recv.at[0]).wait()


    def edge(k, part):
        return (k == 0 and part == 0) or (k == 2 and part == angle_devs - 1)

    def filled(k, narrow):
        low = SHEAR if narrow and k == 0 else 0
        return slice(low, low + (share if narrow else reach))

    def cut_sem(k, narrow, lane, part):
        if k == 1 and quarter > 1:
            return cut_send.at[2, lane]
        return cut_send.at[1 if narrow else 0, lane]

    def cut_copy(k, lane, quota, home, part):
        step = lax.rem(part - a + angle_devs, angle_devs)
        narrow = edge(k, part)
        return rcopy(
            cuts.at[lane, k, part, filled(k, narrow)],
            windows.at[step, kind(k), quota, filled(k, narrow)],
            cut_sem(k, narrow, lane, part),
            win_recv.at[step, kind(k), quota],
            strip=wrap(home + k),
            angle=part,
        )

    def owned(act):
        for lane in range(half):
            quota = d * half + lane
            home = wrap(s - 1 - 4 * lax.rem(quota, quarter))

            @pl.when(home <= strips - 3)
            def _():
                act(lane, quota, home, wrap(home + 1) == s)

    def work(lane, quota, home, local):
        def arrive(k):
            whole = got[k].at[lane, 0 : ROWS[k]]
            if lane or k == 1:
                pltpu.make_async_copy(whole, whole, film_recv.at[k, lane]).wait()
            else:

                @pl.when(quota == 0)
                def _():
                    full = got[k].at[lane]
                    pltpu.make_async_copy(full, full, film_recv.at[k, lane]).wait()
                    value = got[k][lane, 0:EARLY].astype(jnp.float32)
                    for source in range(1, depths):
                        low = ROWS[k] + (source - 1) * EARLY
                        value = value + got[k][lane, low : low + EARLY].astype(jnp.float32)
                    got[k][lane, 0:EARLY] = value.astype(jnp.bfloat16)

                @pl.when(quota != 0)
                def _():
                    pltpu.make_async_copy(whole, whole, film_recv.at[k, lane]).wait()

        corner = meta.pick(scan_y, home, quota)
        gap = differences(FRAME, FRAME)
        turn = one_hot((gap == -corner) | (gap == FRAME - corner))
        back_turn = one_hot((gap == corner) | (gap == corner - FRAME))
        for part in range(2):
            at = slice(part * FRAME, (part + 1) * FRAME)
            probe_rot[lane, part] = dot(probe[part], back_turn).astype(jnp.bfloat16)
            dft_rot[lane, 0, at] = dot(turn, table[at]).astype(jnp.bfloat16)
            dft_rot[lane, 1, :, at] = dot(table_t[:, at], back_turn).astype(jnp.bfloat16)

        @pl.when(local)
        def _():
            value = own[d, lane].astype(jnp.float32)
            for step in range(1, depths):
                source = lax.rem(d + step, depths)
                rcopy(
                    sent[1].at[lane],
                    own.at[source, lane],
                    own_send.at[lane, seat(source)],
                    own_recv.at[lane, seat(source)],
                    depth=source,
                ).wait_recv()
                value = value + own[source, lane].astype(jnp.float32)
            got[1][lane] = value.astype(jnp.bfloat16)

        @pl.when(jnp.logical_not(local))
        def _():
            arrive(1)

        def forward(low, high, extra):
            rows = slice(low, high)
            whole = got1[lane, rows].astype(jnp.float32) + extra.astype(jnp.float32)
            re, im = whole[:, :FRAME], whole[:, FRAME:]
            probe_re = probe_rot[lane, 0, rows].astype(jnp.float32)
            probe_im = probe_rot[lane, 1, rows].astype(jnp.float32)
            exit_wave = jnp.concatenate(
                [probe_re * re - probe_im * im, probe_re * im + probe_im * re], axis=1
            ).astype(jnp.bfloat16)
            section = dot(exit_wave, dft_rot[lane, 0]).astype(jnp.bfloat16)
            left = jnp.concatenate(
                [table_t[:, rows], table_t[:, FRAME + low : FRAME + high]], axis=1
            )
            return dot(left, jnp.concatenate([section[:, :FRAME], section[:, FRAME:]], axis=0))

        arrive(0)
        spec[...] = forward(0, WX, got0[lane, 0:WX])
        arrive(2)
        spectrum = spec[...] + forward(WX, FRAME, got2[lane, 0 : FRAME - WX])
        spec_re, spec_im = spectrum[:FRAME], spectrum[FRAME:]
        power = spec_re * spec_re + spec_im * spec_im
        levels = jnp.concatenate(
            [measured[source, lane] for source in range(depths)], axis=0
        ).astype(jnp.float32)
        live = meta.slot(home, quota) < counts[0, home]
        live = jnp.where(live, 1.0, 0.0).astype(jnp.float32)
        factor = (1.0 - levels * lax.rsqrt(jnp.maximum(power, 1.0))) * live
        residual = jnp.concatenate([spec_re * factor, spec_im * factor], axis=1).astype(
            jnp.bfloat16
        )
        inverse = dot(residual, dft_rot[lane, 1]).astype(jnp.bfloat16)
        stacked = jnp.concatenate([inverse[:, :FRAME], inverse[:, FRAME:]], axis=0)
        offset = meta.pick(scan_x, home, quota)

        def backward(low, high):
            rows = slice(low, high)
            left = jnp.concatenate([table[rows], table[FRAME + low : FRAME + high]], axis=0)
            wave = dot(left, stacked)
            re, im = wave[: high - low], wave[high - low :]
            probe_re = probe_rot[lane, 0, rows].astype(jnp.float32)
            probe_im = probe_rot[lane, 1, rows].astype(jnp.float32)
            return jnp.concatenate(
                [probe_re * re + probe_im * im, probe_re * im - probe_im * re], axis=1
            ).astype(jnp.bfloat16)

        def send(k, low, value):
            gap = differences(reach, value.shape[0])
            first = WX * k - offset - SHEAR - low
            chosen = [one_hot(gap == first + part * share) for part in range(angle_devs)]
            pieces = dot(jnp.concatenate(chosen, axis=0), value).astype(jnp.bfloat16)
            for part in range(angle_devs):
                cuts[lane, k, part] = pieces[part * reach : (part + 1) * reach]
                copy = cut_copy(k, lane, quota, home, part)
                if k == 1:

                    @pl.when(jnp.logical_not(local & (a == part)))
                    def _():
                        copy.start()
                else:
                    copy.start()

        top = backward(0, WX)
        back[0:WX] = top
        send(0, 0, top)
        bottom = backward(WX, FRAME)
        back[WX:FRAME] = bottom
        send(1, 0, back[...])
        send(2, WX, bottom)

        @pl.when(local)
        def _():
            windows[0, kind(1), quota] = cuts[lane, 1, a]


    owned(work)

    for step in range(1, angle_devs):
        meta_waits(step, meta_recv)
        for copy in meta_pulls(step):
            copy.start()
    for step in range(1, angle_devs):
        for copy in meta_pulls(step):
            copy.wait()
    mine = items_of(d)
    theirs = [items_of(lax.rem(d + step, depths)) for step in range(1, depths)]
    prepare(picks_mine, mine)
    for step in range(1, depths):
        prepare(picks_theirs.at[step - 1], theirs[step - 1])


    def sized(k, act):
        if k == 1:
            act(filled(k, False))
        else:
            narrow = a == (0 if k == 0 else angle_devs - 1)

            @pl.when(narrow)
            def _():
                act(filled(k, True))

            @pl.when(jnp.logical_not(narrow))
            def _():
                act(filled(k, False))

    def recv(step, k, q):
        def act(rows):
            window = windows.at[step, kind(k), q, rows]
            pltpu.make_async_copy(window, window, win_recv.at[step, kind(k), q]).wait()

        if k is None:
            narrow = a == jnp.where(s <= outer, 0, angle_devs - 1)

            @pl.when(narrow)
            def _():
                act(slice(0, share))

            @pl.when(jnp.logical_not(narrow))
            def _():
                act(slice(0, reach))
        else:
            sized(k, act)

    def relay(step, k):
        for q in range(slots):

            @pl.when(d == q // half)
            def _():
                def act(rows):
                    window = windows.at[step, kind(k), q, rows]
                    if not (step == 0 and own_strip(k, q)):
                        pltpu.make_async_copy(window, window, win_recv.at[step, kind(k), q]).wait()
                    for other in range(depths):
                        if other != q // half:
                            rcopy(
                                window,
                                window,
                                pass_send.at[kind(k), seat(other)],
                                win_recv.at[step, kind(k), q],
                                depth=other,
                            ).start()

                sized(k, act)

    def place(target, step, k, q, at):
        inside = inner[step, kind(k), q]
        window = windows.at[step, kind(k), q]
        rows = slice(at, at + reach)
        for part in range(2):
            head = window[:, part * FRAME : part * FRAME + margin]
            kept = head * inside
            left = part * columns
            target[rows, left : left + margin] = kept
            target[rows, left + margin : left + FRAME] = window[
                :, part * FRAME + margin : (part + 1) * FRAME
            ]
            target[rows, left + FRAME : left + columns] = head - kept

    def add(chosen, target):
        value = dot(chosen[...], target[...]) * scaling
        for z in range(layers):
            for part in range(2):
                out[z, part] += value[
                    z * share : (z + 1) * share, part * columns : (part + 1) * columns
                ]

    @pl.when(reached(1))
    def _():
        relay(0, 1)
        for q in range(slots):

            @pl.when(d != q // half)
            def _():
                recv(0, 1, q)

        for item in locals_:
            place(placed_local, *item)
        add(picks_local, placed_local)

    for k, step in [(k, step) for k in range(REACHES) for step in range(angle_devs)]:
        if (step, k) != (0, 1):

            @pl.when(reached(k))
            def _():
                relay(step, k)

    for item in sorted(mine, key=lambda item: item[1] is None):
        guarded(item[1], lambda: place(placed_mine, *item))

    add(picks_mine, placed_mine)
    for i in range(1, depths):
        held = sorted(theirs[i - 1], key=lambda item: item[1] is None)
        for item in held:

            def take():
                recv(*item[:3])
                if item[1] is not None:
                    place(placed_theirs.at[i - 1], *item)

            guarded(item[1], take)
        for item in held:
            if item[1] is None:
                place(placed_theirs.at[i - 1], *item)

        add(picks_theirs.at[i - 1], placed_theirs.at[i - 1])

    for other in range(depths):

        @pl.when(d != other)
        def _():
            amp_copy(other).wait_send()

    for step in range(1, angle_devs):
        meta_waits(step, meta_send)
    for k in range(REACHES):

        @pl.when(reached(k))
        def _():
            for q in range(slots):
                if own_strip(k, q):

                    @pl.when(d != q // half)
                    def _():
                        own_copy(q).wait_send()
            rest = [q for q in range(slots) if not own_strip(k, q)]
            if ahead(k, 0):
                first = sent[k].at[0]
                pltpu.make_async_copy(first, first, early_send.at[kind(k)]).wait()
                rest = rest[1:]
            if rest:
                whole = parts[k].at[slots - len(rest) :]
                pltpu.make_async_copy(whole, whole, film_send.at[crossing(k)]).wait()
                for step in range(1, depths):
                    pltpu.make_async_copy(whole, whole, mix_send.at[crossing(k), step - 1]).wait()

    def finish(ref, sem):
        pltpu.make_async_copy(ref, ref, sem).wait()

    def drain(lane, quota, home, local):
        finish(cuts.at[lane, 0:2, 0, 0:share], cut_send.at[1, lane])
        if quarter == 1:
            if angle_devs > 1:
                finish(cuts.at[lane, :, 1:], cut_send.at[0, lane])
        else:
            if angle_devs > 1:
                finish(cuts.at[lane, 0:2, 1:], cut_send.at[0, lane])

            @pl.when(local)
            def _():
                if angle_devs > 1:
                    finish(cuts.at[lane, 1, 1:], cut_send.at[2, lane])

            @pl.when(jnp.logical_not(local))
            def _():
                finish(cuts.at[lane, 1], cut_send.at[2, lane])

    owned(drain)

    for k in range(REACHES):

        @pl.when(reached(k))
        def _():
            for other in range(depths):

                @pl.when(d != other)
                def _():
                    def act(rows):
                        whole = windows.at[:, kind(k), 0:half, rows]
                        pltpu.make_async_copy(
                            whole, whole, pass_send.at[kind(k), seat(other)]
                        ).wait()

                    sized(k, act)


def body(sizes_of, crystal, probe, amplitude, shear, scan_x, scan_y, slot_angle, owner_slot, counts):
    strips, angle_devs, depths = sizes_of
    layers, _, _, columns = crystal.shape
    slots = owner_slot.shape[2]
    half = slots // depths
    share = WX // angle_devs
    reach = share + SHEAR
    kinds = bands(strips)
    seats = 1 if depths == 2 else depths
    crossings = 1 if strips == 4 else kinds
    local_rows = -(-(slots * reach) // 128) * 128
    batch_rows = -(-(half * len(batch_of(strips, angle_devs)) * reach) // 128) * 128
    dft = dft_tables()
    bf16 = jnp.bfloat16
    scan_x, scan_y, slot_angle, owner_slot = [
        jnp.swapaxes(value, 1, 2) for value in (scan_x, scan_y, slot_angle, owner_slot)
    ]
    sizes = (strips, angle_devs, depths, layers, slots, columns)
    hbm = pl.BlockSpec(memory_space=pltpu.HBM)
    vmem = pl.BlockSpec(memory_space=pltpu.VMEM)
    dma = pltpu.SemaphoreType.DMA
    small = (shear, scan_x, scan_y, slot_angle, owner_slot, counts)
    gathered = ((angle_devs,) + shear.shape, (angle_devs, 3) + scan_x.shape)
    scratch = [pltpu.SMEM(x, jnp.int32) for x in (shear.shape, (4,) + scan_x.shape, counts.shape)]
    scratch += [pltpu.SMEM(x, jnp.int32) for x in gathered]
    scratch += [
        pltpu.VMEM((layers, WX, 2 * columns), bf16),
        pltpu.VMEM(probe.shape, bf16),
        pltpu.VMEM(dft.shape, bf16),
    ]
    scratch += [pltpu.VMEM((slots, rows, 2 * FRAME), bf16) for rows in ROWS]
    extra = (depths - 1) * EARLY
    scratch += [
        pltpu.VMEM((half, rows + (0 if k == 1 else extra), 2 * FRAME), bf16)
        for k, rows in enumerate(ROWS)
    ]
    scratch += [pltpu.VMEM((slots, depths - 1, rows // depths, 2 * FRAME), bf16) for rows in ROWS]
    scratch += [pltpu.VMEM((slots, rows // depths, 2 * FRAME), bf16) for rows in ROWS]
    scratch += [pltpu.VMEM((depths, half, FRAME, 2 * FRAME), bf16)]
    scratch += [
        pltpu.VMEM((depths, half, FRAME // depths, FRAME), bf16),
        pltpu.VMEM((half, REACHES, angle_devs, reach, 2 * FRAME), bf16),
        pltpu.VMEM((angle_devs, kinds, slots, reach, 2 * FRAME), bf16),
        pltpu.VMEM((half,) + dft.shape, bf16),
        pltpu.VMEM((half,) + probe.shape, bf16),
        pltpu.VMEM((angle_devs, kinds, slots, reach, columns - FRAME), bf16),
        pltpu.VMEM((layers * share, local_rows), bf16),
        pltpu.VMEM((layers * share, batch_rows), bf16),
        pltpu.VMEM((depths - 1, layers * share, batch_rows), bf16),
        pltpu.VMEM((local_rows, 2 * columns), bf16),
        pltpu.VMEM((batch_rows, 2 * columns), bf16),
        pltpu.VMEM((depths - 1, batch_rows, 2 * columns), bf16),
        pltpu.VMEM((2 * FRAME, FRAME), jnp.float32),
        pltpu.VMEM((FRAME, 2 * FRAME), bf16),
        dma((3,)),
        dma((kinds,)),
        dma((crossings,)),
        dma((REACHES, half)),
        dma((crossings, depths - 1)),
        dma((crossings, slots, depths - 1)),
        dma((half, seats)),
        dma((half, seats)),
        dma((seats,)),
        dma((1,)),
        dma((3,)),
        dma((angle_devs - 1, 2)),
        dma((angle_devs - 1, 2)),
        dma((angle_devs - 1, 2)),
        dma((2 if strips == 4 else 3, half)),
        dma((kinds, seats)),
        dma((angle_devs, kinds, slots)),
    ]
    scaling = 1.0 / (shear.shape[0] * angle_devs)
    result, *_ = pl.pallas_call(
        functools.partial(kernel, sizes, scaling),
        out_shape=(jax.ShapeDtypeStruct((layers, 2, share, columns), jnp.float32),)
        + tuple(jax.ShapeDtypeStruct(x, jnp.int32) for x in gathered),
        in_specs=[hbm] * 10,
        out_specs=(vmem,) + (hbm,) * 2,
        scratch_shapes=scratch,
        compiler_params=pltpu.CompilerParams(
            collective_id=0, has_side_effects=True, vmem_limit_bytes=VMEM_LIMIT
        ),
    )(
        *(
            pltpu.with_memory_space_constraint(x, pltpu.HBM)
            for x in (crystal, probe, amplitude, dft, *small)
        )
    )
    return result


def solution(mesh):
    placed = (
        P(("groups", "depth"), None, "strip", None),
        P(),
        P("angle", ("groups", "strip", "depth"), None),
        P(("groups", "angle"), "depth"),
        P(("groups", "angle"), None, None),
        P(("groups", "angle"), None, None),
        P(("groups", "angle"), None, None),
        P(("groups", "angle"), None, None),
        P(("groups", "angle"), None),
    )
    sizes_of = (mesh.shape["strip"], mesh.shape["angle"], mesh.shape["depth"])
    return jax.shard_map(
        functools.partial(body, sizes_of),
        mesh=mesh,
        in_specs=placed,
        out_specs=P(("groups", "depth"), None, ("strip", "angle"), None),
        check_vma=False,
    )
```

```python
import functools

import jax
import jax.numpy as jnp
import numpy as np
from jax import lax
from jax.experimental import pallas as pl
from jax.experimental.pallas import tpu as pltpu
from jax.sharding import PartitionSpec as P

FRAME = 256
WX = 128
SHEAR = 16
REACHES = 3
ROWS = (WX, FRAME, FRAME - WX)
BASES = (0, 0, WX)
EARLY = 32
VMEM_LIMIT = 44 * 2**20
MESH = pl.DeviceIdType.MESH


def dft_tables():
    index_row = np.arange(FRAME)
    phase = (index_row[:, None] * index_row[None, :] % FRAME) * (2.0 * np.pi / FRAME)
    real = np.cos(phase) / np.sqrt(FRAME)
    imag = -np.sin(phase) / np.sqrt(FRAME)
    table = np.block([[real, imag], [-imag, real]]).astype(np.float32)
    return jnp.asarray(np.stack([table, table.T]), jnp.bfloat16)


def dot(left, right):
    return jnp.dot(left, right, preferred_element_type=jnp.float32)


def differences(rows, columns):
    shape = (rows, columns)
    return lax.broadcasted_iota(jnp.int32, shape, 1) - lax.broadcasted_iota(jnp.int32, shape, 0)


def one_hot(mask):
    return jnp.where(mask, 1.0, 0.0).astype(jnp.bfloat16)


class Meta:
    def __init__(self, lifts, owner_slot, slots, lead):
        self.lifts, self.owner_slot = lifts, owner_slot
        self.slots, self.lead = slots, lead

    def shear(self, angle, z):
        return self.lifts[self.lead + (angle, z)]

    def pick(self, ref, home, quota):
        value = jnp.int32(0)
        for m in range(self.slots):
            at = self.lead + (0, m, home)
            value = value + jnp.where(self.owner_slot[at] == quota, ref[at], 0)
        return value

    def slot(self, home, quota):
        value = jnp.int32(0)
        for m in range(self.slots):
            at = self.lead + (0, m, home)
            value = value + jnp.where(self.owner_slot[at] == quota, m, 0)
        return value


def bands(strips):
    return REACHES if strips - 3 >= 2 else 2


def batch_of(strips, angle_devs):
    every = [(step, k) for step in range(angle_devs) for k in range(bands(strips))]
    return [item for item in every if item != (0, 1)]


def kernel(
    sizes,
    scaling,
    crystal,
    probe_in,
    amplitude,
    tables_in,
    shear_in,
    scan_x_in,
    scan_y_in,
    slot_angle_in,
    owner_slot_in,
    counts_in,
    out,
    picks_theirs,
    placed_theirs,
    shear_out,
    items_out,
    shear,
    items,
    counts,
    shears,
    others,
    film,
    probe,
    dft,
    sent0,
    sent1,
    sent2,
    got0,
    got1,
    got2,
    mix0,
    mix1,
    mix2,
    part0,
    part1,
    part2,
    own,
    measured,
    cuts,
    windows,
    dft_rot,
    probe_rot,
    inner,
    picks_local,
    picks_mine,
    placed_local,
    placed_mine,
    spec,
    back,
    load_sem,
    early_send,
    film_send,
    film_recv,
    mix_send,
    mix_recv,
    own_send,
    own_recv,
    amp_send,
    amp_recv,
    meta_load,
    meta_send,
    meta_recv,
    meta_pull,
    cut_send,
    pass_send,
    win_recv,
):
    strips, angle_devs, depths, layers, slots, columns = sizes
    quarter = strips // 4
    half = slots // depths
    share = WX // angle_devs
    reach = share + SHEAR
    sent = (sent0, sent1, sent2)
    got = (got0, got1, got2)
    mix = (mix0, mix1, mix2)
    parts = (part0, part1, part2)
    s = lax.axis_index("strip")
    a = lax.axis_index("angle")
    d = lax.axis_index("depth")
    scan_x, owner_slot, scan_y, slot_angle = [items.at[i] for i in range(4)]
    meta = Meta(shear, owner_slot, slots, ())
    margin = columns - FRAME
    kinds = bands(strips)
    batch = batch_of(strips, angle_devs)
    rows_of = dict(zip(batch, range(len(batch))))

    outer = strips - 3
    spread = (1, None) if kinds == 2 else (1, 0, 2)

    def kind(k):
        return 0 if k is None else k % kinds

    def home_of(k):
        return jnp.where(s <= outer, s, s - 2) if k is None else s - k

    def seat(device):
        return 0 if depths == 2 else device


    def lanes(rows):
        return lax.broadcasted_iota(jnp.int32, (rows, margin), 1)

    def rcopy(source, target, send_sem, recv_sem, **where):
        return pltpu.make_async_remote_copy(
            source, target, send_sem, recv_sem, device_id=where, device_id_type=MESH
        )

    def wrap(strip):
        return lax.rem(strip + 4 * strips, strips)

    same = (scan_x_in, owner_slot_in, scan_y_in, slot_angle_in)
    metas = [
        pltpu.make_async_copy(shear_in, shear, meta_load.at[0]),
        pltpu.make_async_copy(counts_in, counts, meta_load.at[1]),
    ]
    several = [pltpu.make_async_copy(x, items.at[i], meta_load.at[2]) for i, x in enumerate(same)]
    loads = [
        pltpu.make_async_copy(
            crystal.at[:, part],
            film.at[:, :, part * columns : (part + 1) * columns],
            load_sem.at[0],
        )
        for part in range(2)
    ]
    late = [
        pltpu.make_async_copy(source, target, load_sem.at[1 + i])
        for i, (source, target) in enumerate(((probe_in, probe), (tables_in, dft)))
    ]
    table, table_t = dft.at[0], dft.at[1]
    for copy in metas + several + loads:
        copy.start()

    blank = jnp.zeros(windows.shape[:3] + (SHEAR, 2 * FRAME), jnp.bfloat16)
    windows[:, :, :, 0:SHEAR] = blank
    windows[:, :, :, share:reach] = blank

    barrier = pltpu.get_barrier_semaphore()
    shifts = set()
    for k in range(REACHES):
        for t in range(quarter):
            shifts |= {(1 - k + 4 * t) % strips, (k - 1 - 4 * t) % strips}
    expected = jnp.int32(0)
    for shift in sorted(shifts | {0}):
        peer = wrap(s + shift)
        if quarter == 1 and shift:
            close = jnp.abs(peer - s) == 1
        else:
            close = peer >= 0
        near = angle_devs + depths - 1 - (1 if shift == 0 else 0)
        expected = expected + jnp.where(close, near, 0)

        @pl.when(close)
        def _():
            for step in range(angle_devs):
                if shift or step:
                    place = {"strip": peer, "angle": lax.rem(a + step, angle_devs)}
                    pl.semaphore_signal(barrier, 1, device_id=place, device_id_type=MESH)
            for step in range(1, depths):
                place = {"strip": peer, "depth": lax.rem(d + step, depths)}
                pl.semaphore_signal(barrier, 1, device_id=place, device_id_type=MESH)

    out[...] = jnp.zeros(out.shape, jnp.float32)
    for ref in (placed_local, placed_mine, placed_theirs):
        ref[...] = jnp.zeros(ref.shape, jnp.bfloat16)

    for copy in metas:
        copy.wait()
    pltpu.make_async_copy(items, items, meta_load.at[2]).wait()
    pltpu.make_async_copy(film, film, load_sem.at[0]).wait()
    for copy in late:
        copy.start()

    def ahead(k, q):
        return k != 1 and q == 0

    def size(k, q):
        return (ROWS[k] - (EARLY if ahead(k, q) else 0)) // depths

    def block(k, q, device):
        rows = size(k, q)
        low = EARLY if ahead(k, q) else 0
        return pl.ds(pl.multiple_of(low + device * rows, 16), rows)

    def crossing(k):
        return 0 if quarter == 1 else kind(k)

    def mix_copy(k, q, step):
        target = lax.rem(d + step, depths)
        return rcopy(
            sent[k].at[q, block(k, q, target)],
            mix[k].at[q, step - 1, 0 : size(k, q)],
            early_send.at[kind(k)] if ahead(k, q) else mix_send.at[crossing(k), step - 1],
            mix_recv.at[crossing(k), q, step - 1],
            depth=target,
        )

    def film_copy(k, q):
        return rcopy(
            parts[k].at[q, 0 : size(k, q)],
            got[k].at[q % half, block(k, q, d)],
            early_send.at[kind(k)] if ahead(k, q) else film_send.at[crossing(k)],
            film_recv.at[k, q % half],
            strip=wrap(s - k + 4 * (q % quarter) + 1),
            depth=q // half,
        )

    def early_copy(k):
        low = jnp.where(d == 0, 0, ROWS[k] + (d - 1) * EARLY)
        return rcopy(
            sent[k].at[0, 0:EARLY],
            got[k].at[0, pl.ds(pl.multiple_of(low, 16), EARLY)],
            early_send.at[kind(k)],
            film_recv.at[k, 0],
            strip=wrap(s - k + 1),
            depth=0,
        )

    def own_copy(q):
        return rcopy(
            sent[1].at[q],
            own.at[d, q % half],
            own_send.at[q % half, seat(q // half)],
            own_recv.at[q % half, seat(d)],
            depth=q // half,
        )

    def exchange(k, q):
        for step in range(1, depths):
            mix_copy(k, q, step).start()

    def merge(k, q):
        rows = size(k, q)
        value = sent[k][q, block(k, q, d)].astype(jnp.float32)
        for step in range(1, depths):
            mix_copy(k, q, step).wait_recv()
            value = value + mix[k][q, step - 1, 0:rows].astype(jnp.float32)
        parts[k][q, 0:rows] = value.astype(jnp.bfloat16)
        film_copy(k, q).start()

    def own_strip(k, q):
        return (1 - k + 4 * (q % quarter)) % strips == 0

    def project(k):
        home = s - k
        gap = differences(ROWS[k], WX)
        chosen = []
        for q in range(slots):
            offset = meta.pick(scan_x, home, q) - WX * k + BASES[k]
            angle = meta.pick(slot_angle, home, q)
            chosen.append(
                jnp.concatenate(
                    [one_hot(gap == offset + meta.shear(angle, z)) for z in range(layers)], axis=1
                )
            )
        flat = film[...].reshape(layers * WX, 2 * columns)
        tall = dot(jnp.concatenate(chosen, axis=0), flat)
        for q in range(slots):
            corner = meta.pick(scan_y, home, q)
            first = lanes(ROWS[k]) >= corner
            rows = tall[q * ROWS[k] : (q + 1) * ROWS[k]]
            wound = []
            for part in range(2):
                side = rows[:, part * columns : (part + 1) * columns]
                wound += [jnp.where(first, side[:, :margin], side[:, FRAME:]), side[:, margin:FRAME]]
            sent[k][q] = jnp.concatenate(wound, axis=1).astype(jnp.bfloat16)

    def reached(k):
        return (s - k >= 0) & (s - k <= outer)

    def guarded(k, act):
        if k is None:
            act()
        else:
            pl.when(reached(k))(act)

    for k in (0, 2):

        @pl.when(reached(k))
        def _():
            project(k)

    pl.semaphore_wait(barrier, expected)
    for k in (0, 2):

        @pl.when(reached(k))
        def _():
            exchange(k, 0)
            early_copy(k).start()
            for q in range(1, slots):
                exchange(k, q)


    def amp_copy(other):
        return rcopy(
            amplitude.at[other * half : (other + 1) * half],
            measured.at[d],
            amp_send.at[seat(other)],
            amp_recv.at[0],
            depth=other,
        )

    def amp_own(other):
        return pltpu.make_async_copy(
            amplitude.at[other * half : (other + 1) * half], measured.at[d], amp_recv.at[0]
        )

    def meta_copies(step):
        def send(source, target, i):
            return rcopy(
                source,
                target,
                meta_send.at[step - 1, i],
                meta_recv.at[step - 1, i],
                angle=lax.rem(a + step, angle_devs),
            )

        first = [send(shear_in, shear_out.at[step], 0)]
        return first + [send(x, items_out.at[step, i], 1) for i, x in enumerate(same[1:])]

    def meta_waits(step, sem):
        for i, ref in enumerate((shear_out.at[step], items_out.at[step])):
            pltpu.make_async_copy(ref, ref, sem.at[step - 1, i]).wait()

    def meta_pulls(step):
        return [
            pltpu.make_async_copy(shear_out.at[step], shears.at[step], meta_pull.at[step - 1, 0]),
            pltpu.make_async_copy(items_out.at[step], others.at[step], meta_pull.at[step - 1, 1]),
        ]

    for step in range(1, angle_devs):
        for copy in meta_copies(step):
            copy.start()

    for other in range(depths):

        @pl.when(d != other)
        def _():
            amp_copy(other).start()

        @pl.when(d == other)
        def _():
            amp_own(other).start()

    for q in range(slots):
        for k in (0, 2):

            @pl.when(reached(k))
            def _():
                merge(k, q)


    @pl.when(reached(1))
    def _():
        project(1)
        for q in range(slots):
            if own_strip(1, q):

                @pl.when(d == q // half)
                def _():
                    own[d, q % half] = sent[1][q]

                @pl.when(d != q // half)
                def _():
                    own_copy(q).start()
            else:
                exchange(1, q)
        for q in range(slots):
            if not own_strip(1, q):
                merge(1, q)

    groups = [(meta, scan_y, slot_angle)]
    for step in range(1, angle_devs):
        owner_slots, scans_y, slot_angles = [others.at[step, i] for i in range(3)]
        groups.append((Meta(shears.at[step], owner_slots, slots, ()), scans_y, slot_angles))

    def prepare(target, items):
        wanted = []
        for step, k, q, at in items:
            home = jnp.clip(home_of(k), 0, strips - 1)
            source, corners, angles = groups[step]

            def fill():
                first = lanes(reach) >= source.pick(corners, home, q)
                inner[step, kind(k), q] = one_hot(first)

            guarded(k, fill)
            angle = source.pick(angles, home, q)
            base = at + SHEAR
            if k is not None:
                base = jnp.where(reached(k), base, -4 * target.shape[1])
            wanted.append([base - source.shear(angle, z) for z in range(layers)])
        gap = differences(share, target.shape[1])
        for z in range(layers):
            mask = gap == wanted[0][z]
            for want in wanted[1:]:
                mask = mask | (gap == want[z])
            target[z * share : (z + 1) * share] = one_hot(mask)

    locals_ = [(0, 1, q, q * reach) for q in range(slots)]

    def items_of(depth):
        return [
            (step, k, depth * half + lane, (lane * len(batch) + rows_of[step, kind(k)]) * reach)
            for lane in range(half)
            for step in list(range(1, angle_devs)) + [0]
            for k in spread
            if (step, k) != (0, 1)
        ]

    prepare(picks_local, locals_)

    for copy in late:
        copy.wait()
    pltpu.make_async_copy(measured, measured, amp_recv.at[0]).wait()


    def edge(k, part):
        return (k == 0 and part == 0) or (k == 2 and part == angle_devs - 1)

    def filled(k, narrow):
        low = SHEAR if narrow and k == 0 else 0
        return slice(low, low + (share if narrow else reach))

    def cut_sem(k, narrow, lane, part):
        if k == 1 and quarter > 1:
            return cut_send.at[2, lane]
        return cut_send.at[1 if narrow else 0, lane]

    def cut_copy(k, lane, quota, home, part):
        step = lax.rem(part - a + angle_devs, angle_devs)
        narrow = edge(k, part)
        return rcopy(
            cuts.at[lane, k, part, filled(k, narrow)],
            windows.at[step, kind(k), quota, filled(k, narrow)],
            cut_sem(k, narrow, lane, part),
            win_recv.at[step, kind(k), quota],
            strip=wrap(home + k),
            angle=part,
        )

    def owned(act):
        for lane in range(half):
            quota = d * half + lane
            home = wrap(s - 1 - 4 * lax.rem(quota, quarter))

            @pl.when(home <= strips - 3)
            def _():
                act(lane, quota, home, wrap(home + 1) == s)

    def work(lane, quota, home, local):
        def arrive(k):
            whole = got[k].at[lane, 0 : ROWS[k]]
            if lane or k == 1:
                pltpu.make_async_copy(whole, whole, film_recv.at[k, lane]).wait()
            else:

                @pl.when(quota == 0)
                def _():
                    full = got[k].at[lane]
                    pltpu.make_async_copy(full, full, film_recv.at[k, lane]).wait()
                    value = got[k][lane, 0:EARLY].astype(jnp.float32)
                    for source in range(1, depths):
                        low = ROWS[k] + (source - 1) * EARLY
                        value = value + got[k][lane, low : low + EARLY].astype(jnp.float32)
                    got[k][lane, 0:EARLY] = value.astype(jnp.bfloat16)

                @pl.when(quota != 0)
                def _():
                    pltpu.make_async_copy(whole, whole, film_recv.at[k, lane]).wait()

        corner = meta.pick(scan_y, home, quota)
        gap = differences(FRAME, FRAME)
        turn = one_hot((gap == -corner) | (gap == FRAME - corner))
        back_turn = one_hot((gap == corner) | (gap == corner - FRAME))
        for part in range(2):
            at = slice(part * FRAME, (part + 1) * FRAME)
            probe_rot[lane, part] = dot(probe[part], back_turn).astype(jnp.bfloat16)
            dft_rot[lane, 0, at] = dot(turn, table[at]).astype(jnp.bfloat16)
            dft_rot[lane, 1, :, at] = dot(table_t[:, at], back_turn).astype(jnp.bfloat16)

        @pl.when(local)
        def _():
            value = own[d, lane].astype(jnp.float32)
            for step in range(1, depths):
                source = lax.rem(d + step, depths)
                rcopy(
                    sent[1].at[lane],
                    own.at[source, lane],
                    own_send.at[lane, seat(source)],
                    own_recv.at[lane, seat(source)],
                    depth=source,
                ).wait_recv()
                value = value + own[source, lane].astype(jnp.float32)
            got[1][lane] = value.astype(jnp.bfloat16)

        @pl.when(jnp.logical_not(local))
        def _():
            arrive(1)

        def forward(low, high, extra):
            rows = slice(low, high)
            whole = got1[lane, rows].astype(jnp.float32) + extra.astype(jnp.float32)
            re, im = whole[:, :FRAME], whole[:, FRAME:]
            probe_re = probe_rot[lane, 0, rows].astype(jnp.float32)
            probe_im = probe_rot[lane, 1, rows].astype(jnp.float32)
            exit_wave = jnp.concatenate(
                [probe_re * re - probe_im * im, probe_re * im + probe_im * re], axis=1
            ).astype(jnp.bfloat16)
            section = dot(exit_wave, dft_rot[lane, 0]).astype(jnp.bfloat16)
            left = jnp.concatenate(
                [table_t[:, rows], table_t[:, FRAME + low : FRAME + high]], axis=1
            )
            return dot(left, jnp.concatenate([section[:, :FRAME], section[:, FRAME:]], axis=0))

        arrive(0)
        spec[...] = forward(0, WX, got0[lane, 0:WX])
        arrive(2)
        spectrum = spec[...] + forward(WX, FRAME, got2[lane, 0 : FRAME - WX])
        spec_re, spec_im = spectrum[:FRAME], spectrum[FRAME:]
        power = spec_re * spec_re + spec_im * spec_im
        levels = jnp.concatenate(
            [measured[source, lane] for source in range(depths)], axis=0
        ).astype(jnp.float32)
        live = meta.slot(home, quota) < counts[0, home]
        live = jnp.where(live, 1.0, 0.0).astype(jnp.float32)
        factor = (1.0 - levels * lax.rsqrt(jnp.maximum(power, 1.0))) * live
        residual = jnp.concatenate([spec_re * factor, spec_im * factor], axis=1).astype(
            jnp.bfloat16
        )
        inverse = dot(residual, dft_rot[lane, 1]).astype(jnp.bfloat16)
        stacked = jnp.concatenate([inverse[:, :FRAME], inverse[:, FRAME:]], axis=0)
        offset = meta.pick(scan_x, home, quota)

        def backward(low, high):
            rows = slice(low, high)
            left = jnp.concatenate([table[rows], table[FRAME + low : FRAME + high]], axis=0)
            wave = dot(left, stacked)
            re, im = wave[: high - low], wave[high - low :]
            probe_re = probe_rot[lane, 0, rows].astype(jnp.float32)
            probe_im = probe_rot[lane, 1, rows].astype(jnp.float32)
            return jnp.concatenate(
                [probe_re * re + probe_im * im, probe_re * im - probe_im * re], axis=1
            ).astype(jnp.bfloat16)

        def send(k, low, value):
            gap = differences(reach, value.shape[0])
            first = WX * k - offset - SHEAR - low
            chosen = [one_hot(gap == first + part * share) for part in range(angle_devs)]
            pieces = dot(jnp.concatenate(chosen, axis=0), value).astype(jnp.bfloat16)
            for part in range(angle_devs):
                cuts[lane, k, part] = pieces[part * reach : (part + 1) * reach]
                copy = cut_copy(k, lane, quota, home, part)
                if k == 1:

                    @pl.when(jnp.logical_not(local & (a == part)))
                    def _():
                        copy.start()
                else:
                    copy.start()

        top = backward(0, WX)
        back[0:WX] = top
        send(0, 0, top)
        bottom = backward(WX, FRAME)
        back[WX:FRAME] = bottom
        send(1, 0, back[...])
        send(2, WX, bottom)

        @pl.when(local)
        def _():
            windows[0, kind(1), quota] = cuts[lane, 1, a]


    owned(work)

    for step in range(1, angle_devs):
        meta_waits(step, meta_recv)
        for copy in meta_pulls(step):
            copy.start()
    for step in range(1, angle_devs):
        for copy in meta_pulls(step):
            copy.wait()
    mine = items_of(d)
    theirs = [items_of(lax.rem(d + step, depths)) for step in range(1, depths)]
    prepare(picks_mine, mine)
    for step in range(1, depths):
        prepare(picks_theirs.at[step - 1], theirs[step - 1])


    def sized(k, act):
        if k == 1:
            act(filled(k, False))
        else:
            narrow = a == (0 if k == 0 else angle_devs - 1)

            @pl.when(narrow)
            def _():
                act(filled(k, True))

            @pl.when(jnp.logical_not(narrow))
            def _():
                act(filled(k, False))

    def recv(step, k, q):
        def act(rows):
            window = windows.at[step, kind(k), q, rows]
            pltpu.make_async_copy(window, window, win_recv.at[step, kind(k), q]).wait()

        if k is None:
            narrow = a == jnp.where(s <= outer, 0, angle_devs - 1)

            @pl.when(narrow)
            def _():
                act(slice(0, share))

            @pl.when(jnp.logical_not(narrow))
            def _():
                act(slice(0, reach))
        else:
            sized(k, act)

    def relay(step, k):
        for q in range(slots):

            @pl.when(d == q // half)
            def _():
                def act(rows):
                    window = windows.at[step, kind(k), q, rows]
                    if not (step == 0 and own_strip(k, q)):
                        pltpu.make_async_copy(window, window, win_recv.at[step, kind(k), q]).wait()
                    for other in range(depths):
                        if other != q // half:
                            rcopy(
                                window,
                                window,
                                pass_send.at[kind(k), seat(other)],
                                win_recv.at[step, kind(k), q],
                                depth=other,
                            ).start()

                sized(k, act)

    def place(target, step, k, q, at):
        inside = inner[step, kind(k), q]
        window = windows.at[step, kind(k), q]
        rows = slice(at, at + reach)
        for part in range(2):
            head = window[:, part * FRAME : part * FRAME + margin]
            kept = head * inside
            left = part * columns
            target[rows, left : left + margin] = kept
            target[rows, left + margin : left + FRAME] = window[
                :, part * FRAME + margin : (part + 1) * FRAME
            ]
            target[rows, left + FRAME : left + columns] = head - kept

    def add(chosen, target):
        value = dot(chosen[...], target[...]) * scaling
        for z in range(layers):
            for part in range(2):
                out[z, part] += value[
                    z * share : (z + 1) * share, part * columns : (part + 1) * columns
                ]

    @pl.when(reached(1))
    def _():
        relay(0, 1)
        for q in range(slots):

            @pl.when(d != q // half)
            def _():
                recv(0, 1, q)

        for item in locals_:
            place(placed_local, *item)
        add(picks_local, placed_local)

    for k, step in [(k, step) for k in range(REACHES) for step in range(angle_devs)]:
        if (step, k) != (0, 1):

            @pl.when(reached(k))
            def _():
                relay(step, k)

    for item in sorted(mine, key=lambda item: item[1] is None):
        guarded(item[1], lambda: place(placed_mine, *item))

    add(picks_mine, placed_mine)
    for i in range(1, depths):
        held = sorted(theirs[i - 1], key=lambda item: item[1] is None)
        for item in held:

            def take():
                recv(*item[:3])
                if item[1] is not None:
                    place(placed_theirs.at[i - 1], *item)

            guarded(item[1], take)
        for item in held:
            if item[1] is None:
                place(placed_theirs.at[i - 1], *item)


    for other in range(depths):

        @pl.when(d != other)
        def _():
            amp_copy(other).wait_send()

    for step in range(1, angle_devs):
        meta_waits(step, meta_send)
    for k in range(REACHES):

        @pl.when(reached(k))
        def _():
            for q in range(slots):
                if own_strip(k, q):

                    @pl.when(d != q // half)
                    def _():
                        own_copy(q).wait_send()
            rest = [q for q in range(slots) if not own_strip(k, q)]
            if ahead(k, 0):
                first = sent[k].at[0]
                pltpu.make_async_copy(first, first, early_send.at[kind(k)]).wait()
                rest = rest[1:]
            if rest:
                whole = parts[k].at[slots - len(rest) :]
                pltpu.make_async_copy(whole, whole, film_send.at[crossing(k)]).wait()
                for step in range(1, depths):
                    pltpu.make_async_copy(whole, whole, mix_send.at[crossing(k), step - 1]).wait()

    def finish(ref, sem):
        pltpu.make_async_copy(ref, ref, sem).wait()

    def drain(lane, quota, home, local):
        finish(cuts.at[lane, 0:2, 0, 0:share], cut_send.at[1, lane])
        if quarter == 1:
            if angle_devs > 1:
                finish(cuts.at[lane, :, 1:], cut_send.at[0, lane])
        else:
            if angle_devs > 1:
                finish(cuts.at[lane, 0:2, 1:], cut_send.at[0, lane])

            @pl.when(local)
            def _():
                if angle_devs > 1:
                    finish(cuts.at[lane, 1, 1:], cut_send.at[2, lane])

            @pl.when(jnp.logical_not(local))
            def _():
                finish(cuts.at[lane, 1], cut_send.at[2, lane])

    owned(drain)

    for k in range(REACHES):

        @pl.when(reached(k))
        def _():
            for other in range(depths):

                @pl.when(d != other)
                def _():
                    def act(rows):
                        whole = windows.at[:, kind(k), 0:half, rows]
                        pltpu.make_async_copy(
                            whole, whole, pass_send.at[kind(k), seat(other)]
                        ).wait()

                    sized(k, act)


def finish_kernel(flushes, scaling, sums, picks, placed, out, total, sem):
    layers, parts, share, columns = sums.shape
    step = layers // flushes
    copies = []
    for i in range(flushes):
        rows = slice(i * step * share, (i + 1) * step * share)
        value = dot(picks[0, rows], placed[0])
        for other in range(1, picks.shape[0]):
            value = value + dot(picks[other, rows], placed[other])
        value = value * scaling
        for z in range(step):
            for part in range(parts):
                piece = value[z * share : (z + 1) * share, part * columns : (part + 1) * columns]
                total[i * step + z, part] = sums[i * step + z, part] + piece
        at = slice(i * step, (i + 1) * step)
        copies.append(pltpu.make_async_copy(total.at[at], out.at[at], sem.at[i]))
        copies[-1].start()
    for copy in copies:
        copy.wait()


def body(sizes_of, crystal, probe, amplitude, shear, scan_x, scan_y, slot_angle, owner_slot, counts):
    strips, angle_devs, depths = sizes_of
    layers, _, _, columns = crystal.shape
    slots = owner_slot.shape[2]
    half = slots // depths
    share = WX // angle_devs
    reach = share + SHEAR
    kinds = bands(strips)
    seats = 1 if depths == 2 else depths
    crossings = 1 if strips == 4 else kinds
    local_rows = -(-(slots * reach) // 128) * 128
    batch_rows = -(-(half * len(batch_of(strips, angle_devs)) * reach) // 128) * 128
    dft = dft_tables()
    bf16 = jnp.bfloat16
    scan_x, scan_y, slot_angle, owner_slot = [
        jnp.swapaxes(value, 1, 2) for value in (scan_x, scan_y, slot_angle, owner_slot)
    ]
    sizes = (strips, angle_devs, depths, layers, slots, columns)
    hbm = pl.BlockSpec(memory_space=pltpu.HBM)
    vmem = pl.BlockSpec(memory_space=pltpu.VMEM)
    dma = pltpu.SemaphoreType.DMA
    small = (shear, scan_x, scan_y, slot_angle, owner_slot, counts)
    gathered = ((angle_devs,) + shear.shape, (angle_devs, 3) + scan_x.shape)
    scratch = [pltpu.SMEM(x, jnp.int32) for x in (shear.shape, (4,) + scan_x.shape, counts.shape)]
    scratch += [pltpu.SMEM(x, jnp.int32) for x in gathered]
    scratch += [
        pltpu.VMEM((layers, WX, 2 * columns), bf16),
        pltpu.VMEM(probe.shape, bf16),
        pltpu.VMEM(dft.shape, bf16),
    ]
    scratch += [pltpu.VMEM((slots, rows, 2 * FRAME), bf16) for rows in ROWS]
    extra = (depths - 1) * EARLY
    scratch += [
        pltpu.VMEM((half, rows + (0 if k == 1 else extra), 2 * FRAME), bf16)
        for k, rows in enumerate(ROWS)
    ]
    scratch += [pltpu.VMEM((slots, depths - 1, rows // depths, 2 * FRAME), bf16) for rows in ROWS]
    scratch += [pltpu.VMEM((slots, rows // depths, 2 * FRAME), bf16) for rows in ROWS]
    scratch += [pltpu.VMEM((depths, half, FRAME, 2 * FRAME), bf16)]
    scratch += [
        pltpu.VMEM((depths, half, FRAME // depths, FRAME), bf16),
        pltpu.VMEM((half, REACHES, angle_devs, reach, 2 * FRAME), bf16),
        pltpu.VMEM((angle_devs, kinds, slots, reach, 2 * FRAME), bf16),
        pltpu.VMEM((half,) + dft.shape, bf16),
        pltpu.VMEM((half,) + probe.shape, bf16),
        pltpu.VMEM((angle_devs, kinds, slots, reach, columns - FRAME), bf16),
        pltpu.VMEM((layers * share, local_rows), bf16),
        pltpu.VMEM((layers * share, batch_rows), bf16),
        pltpu.VMEM((local_rows, 2 * columns), bf16),
        pltpu.VMEM((batch_rows, 2 * columns), bf16),
        pltpu.VMEM((2 * FRAME, FRAME), jnp.float32),
        pltpu.VMEM((FRAME, 2 * FRAME), bf16),
        dma((3,)),
        dma((kinds,)),
        dma((crossings,)),
        dma((REACHES, half)),
        dma((crossings, depths - 1)),
        dma((crossings, slots, depths - 1)),
        dma((half, seats)),
        dma((half, seats)),
        dma((seats,)),
        dma((1,)),
        dma((3,)),
        dma((angle_devs - 1, 2)),
        dma((angle_devs - 1, 2)),
        dma((angle_devs - 1, 2)),
        dma((2 if strips == 4 else 3, half)),
        dma((kinds, seats)),
        dma((angle_devs, kinds, slots)),
    ]
    scaling = 1.0 / (shear.shape[0] * angle_devs)
    whole = (layers, 2, share, columns)
    flushes = 2 - layers % 2
    sums, picks, placed, *_ = pl.pallas_call(
        functools.partial(kernel, sizes, scaling),
        out_shape=(
            jax.ShapeDtypeStruct(whole, jnp.float32),
            jax.ShapeDtypeStruct((depths - 1, layers * share, batch_rows), bf16),
            jax.ShapeDtypeStruct((depths - 1, batch_rows, 2 * columns), bf16),
        )
        + tuple(jax.ShapeDtypeStruct(x, jnp.int32) for x in gathered),
        in_specs=[hbm] * 10,
        out_specs=(vmem,) * 3 + (hbm,) * 2,
        scratch_shapes=scratch,
        compiler_params=pltpu.CompilerParams(
            collective_id=0, has_side_effects=True, vmem_limit_bytes=VMEM_LIMIT
        ),
    )(
        *(
            pltpu.with_memory_space_constraint(x, pltpu.HBM)
            for x in (crystal, probe, amplitude, dft, *small)
        )
    )
    return pl.pallas_call(
        functools.partial(finish_kernel, flushes, scaling),
        out_shape=jax.ShapeDtypeStruct(whole, jnp.float32),
        in_specs=[vmem] * 3,
        out_specs=hbm,
        scratch_shapes=[pltpu.VMEM(whole, jnp.float32), dma((flushes,))],
        compiler_params=pltpu.CompilerParams(vmem_limit_bytes=VMEM_LIMIT),
    )(sums, picks, placed)


def solution(mesh):
    placed = (
        P(("groups", "depth"), None, "strip", None),
        P(),
        P("angle", ("groups", "strip", "depth"), None),
        P(("groups", "angle"), "depth"),
        P(("groups", "angle"), None, None),
        P(("groups", "angle"), None, None),
        P(("groups", "angle"), None, None),
        P(("groups", "angle"), None, None),
        P(("groups", "angle"), None),
    )
    sizes_of = (mesh.shape["strip"], mesh.shape["angle"], mesh.shape["depth"])
    return jax.shard_map(
        functools.partial(body, sizes_of),
        mesh=mesh,
        in_specs=placed,
        out_specs=P(("groups", "depth"), None, ("strip", "angle"), None),
        check_vma=False,
    )
```
